32 devices in a mesh: rep: 4 (over y, x), fsdp: 8 (over z, core).
Axes of the slice: x: 2, y: 2, z: 4, core: 2. Of those that a mesh axis runs over, the one named last changes fastest.
Arguments:
- tokens: bfloat16 [32768, 768], P(('rep', 'fsdp')), may hold values from -6 to 6
- latent: bfloat16 [32768, 768], P(('rep', 'fsdp')), may hold values from -6 to 6
- segment_ids: int32 [32, 1024], P(('rep', 'fsdp')), may hold values from 0 to 7, never falling along the last dimension, each value on 1 to 512 neighbouring positions
- latent_flags: int32 [32, 1024], P(('rep', 'fsdp')), may hold values 0 or 1
- norm1_gain: bfloat16 [768], P('fsdp'), may hold values from 0.25 to 1.75
- norm1_shift: bfloat16 [768], P('fsdp'), may hold values from -4 to 4
- w_qkv: bfloat16 [768, 2304], P('fsdp'), may hold values from -0.21875 to 0.21875
- b_qv: bfloat16 [1536], P('fsdp'), may hold values from -4 to 4
- w_out: bfloat16 [768, 768], P(None, 'fsdp'), may hold values from -1.25 to 1.25
- b_out: bfloat16 [768], P('fsdp'), may hold values from -4 to 4
- norm2_gain: bfloat16 [768], P('fsdp'), may hold values from 0.25 to 1.75
- norm2_shift: bfloat16 [768], P('fsdp'), may hold values from -4 to 4
- w_fc: bfloat16 [768, 3072], P('fsdp'), may hold values from -0.21875 to 0.21875
- b_fc: bfloat16 [3072], P('fsdp'), may hold values from -4 to 4
- w_proj: bfloat16 [3072, 768], P(None, 'fsdp'), may hold values from -0.109375 to 0.109375
- b_proj: bfloat16 [768], P('fsdp'), may hold values from -4 to 4
- cotangent: bfloat16 [32768, 768], P(('rep', 'fsdp')), may hold values from -6 to 6
Outputs:
- output: bfloat16 [32768, 768], P(('rep', 'fsdp'))
- grad_inputs: float32 [32768, 768], P(('rep', 'fsdp'))
- grad_norm1_gain: float32 [768], P('fsdp')
- grad_norm1_shift: float32 [768], P('fsdp')
- grad_w_qkv: float32 [768, 2304], P('fsdp')
- grad_b_qv: float32 [1536], P('fsdp')
- grad_w_out: float32 [768, 768], P(None, 'fsdp')
- grad_b_out: float32 [768], P('fsdp')
- grad_norm2_gain: float32 [768], P('fsdp')
- grad_norm2_shift: float32 [768], P('fsdp')
- grad_w_fc: float32 [768, 3072], P('fsdp')
- grad_b_fc: float32 [3072], P('fsdp')
- grad_w_proj: float32 [3072, 768], P(None, 'fsdp')
- grad_b_proj: float32 [768], P('fsdp')
The draws below stay inside these ranges and needn't reach their ends.
Inputs may be any that keep to these rules, and one draw needn't show every extreme that they name: `segment_ids`: within each sequence of 1024 positions the ids never fall; each document spans 1 to 512 positions, and some document spans exactly 512.
All inputs are finite; a program needn't handle non-finite values. No bound on the sum of `latent_flags` on one device may be relied on, other than what follows from the above.
Results may differ from the reference program's by a relative error of at most 0.014.
Values may be sent and summed in bfloat16 or wider, within the bound.
A program may use at most 256 MiB of HBM per device.

```python
import math
import jax
import jax.numpy as jnp
import numpy as np
from jax import lax

D = 768
HEADS = 12
HD = 64
FF = 3072
LEN = 1024
DOCS = 8
SEQS = 32
TOKENS = 32768


def plant(values, key, least, largest):
    shape = values.shape
    index_at = [jax.random.randint(jax.random.fold_in(key, axis), (), 0, shape[axis]) for axis in range(len(shape))]
    values = values.at[tuple(index_at)].set(least)
    longest = shape.index(max(shape))
    index_at[longest] = (index_at[longest] + 1) % shape[longest]
    return values.at[tuple(index_at)].set(largest)


def spiked(entries, stream_key, source, target, shards_of, factor):
    owner, partner = [(jnp.arange(entries.shape[axis_at]) // (entries.shape[axis_at] // shards_of)).reshape([-1 if axis == axis_at else 1 for axis in range(entries.ndim)]) for axis_at in (source, target)]
    chosen = jax.random.permutation(stream_key, shards_of)[partner]
    strong = (owner == chosen) | (owner == (partner + shards_of // 2) % shards_of)
    return jnp.where(strong, factor * entries, entries)


def shard_levels(key, dims, cuts, least, top_value):
    def one(dim, shards_of):
        steps = jax.random.uniform(jax.random.fold_in(jax.random.fold_in(key, 6), dim), (shards_of,), jnp.float32, least / len(cuts), top_value / len(cuts))
        return jnp.repeat(jnp.exp(steps), dims[dim] // shards_of).reshape((-1,) + (1,) * (len(dims) - dim - 1))

    gain = one(*cuts[0])
    for cut in cuts[1:]:
        gain = gain * one(*cut)
    return gain


def profile(amount, total, reach, lean):
    weights = [(1 << 20) // math.isqrt(grade ** lean) + 1 for grade in range(2, amount + 1)]
    rest, holding = total - reach - (amount - 1), [1] * (amount - 1)
    while rest > 0:
        free = [i for i in range(amount - 1) if holding[i] < reach]
        pool, budget = sum([weights[i] for i in free]), rest
        for i in free:
            more = min(reach - holding[i], max(1, budget * weights[i] // pool), rest)
            holding[i] = holding[i] + more
            rest = rest - more
    return np.array([reach] + holding)


def ragged_sizes(key, count, total, reach, lean):
    if count == 2:
        one = jax.random.randint(key, (), max(1, total - reach), min(reach, total - 1) + 1)
        return jnp.stack([one, total - one])
    lengths = jnp.asarray(profile(count, total, reach, lean), jnp.int32)
    twos = (count - 1) // 2
    source_of, receiver = lengths[1:1 + 2 * twos:2], lengths[2:2 + 2 * twos:2]
    room = jnp.minimum(source_of - 1, reach - receiver)
    moved = jax.random.randint(jax.random.fold_in(key, 1), (twos,), 0, 1 << 20) % (room + 1)
    lengths = lengths.at[1:1 + 2 * twos:2].set(source_of - moved).at[2:2 + 2 * twos:2].set(receiver + moved)
    return lengths[jax.random.permutation(jax.random.fold_in(key, 2), count)]


def scatter_about(key, extent, scale, bound, shards=(), kind=jnp.bfloat16):
    level = shard_levels(key, extent, shards, -0.22, 0.18) if shards else 1.0
    drawn = jax.random.normal(key, extent, jnp.float32) * scale * level
    return jnp.minimum(jnp.maximum(drawn, -bound), bound).astype(kind)


def gaussian_with(own_key, extent, deviation, reach, cuts, heavy, kind=jnp.bfloat16):
    array = deviation * jax.random.normal(own_key, extent, jnp.float32)
    if cuts:
        array = array * shard_levels(own_key, extent, cuts, -0.22, 0.18)
    return jnp.clip(spiked(array, jax.random.fold_in(own_key, 3), *heavy), -reach, reach).astype(kind)


def setup_inputs(seed: int = 0) -> dict:
    keys = jax.random.split(jax.random.key(seed), 18)
    tokens = scatter_about(keys[0], (TOKENS, D), 1.0, 6.0, ((0, 32),))
    latent = scatter_about(keys[1], (TOKENS, D), 1.0, 6.0, ((0, 32),))
    segment_ids = jax.vmap(lambda own: jnp.searchsorted(jnp.cumsum(ragged_sizes(own, DOCS, LEN, LEN // 2, 2)), jnp.arange(LEN), side="right"))(jax.random.split(keys[2], SEQS)).reshape((SEQS, LEN)).astype(jnp.int32)
    latent_flags = plant((jax.random.randint(keys[3], (SEQS, LEN), 0, 4) < 1).astype(jnp.int32), jax.random.fold_in(keys[3], 1), 0, 1)
    norm1_gain = jnp.clip(1.0 + 0.15 * jax.random.normal(keys[4], (D,), jnp.float32), 0.25, 1.75).astype(jnp.bfloat16)
    norm1_shift = scatter_about(keys[5], (D,), 0.3, 4.0, ((0, 8),))
    w_qkv = scatter_about(keys[6], (D, 3 * D), D ** -0.5, 0.21875, ((0, 8),))
    b_qv = scatter_about(keys[7], (2 * D,), 0.3, 4.0, ((0, 8),))
    w_out = scatter_about(keys[8], (D, D), (D // 32) ** -0.5, 1.25, ((1, 8),))
    b_out = scatter_about(keys[9], (D,), 0.3, 4.0, ((0, 8),))
    norm2_gain = jnp.clip(1.0 + 0.15 * jax.random.normal(keys[10], (D,), jnp.float32), 0.25, 1.75).astype(jnp.bfloat16)
    norm2_shift = scatter_about(keys[11], (D,), 0.3, 4.0, ((0, 8),))
    w_fc = scatter_about(keys[12], (D, FF), D ** -0.5, 0.21875, ((0, 8),))
    b_fc = scatter_about(keys[13], (FF,), 0.3, 4.0, ((0, 8),))
    w_proj = scatter_about(keys[14], (FF, D), FF ** -0.5, 0.109375, ((1, 8),))
    b_proj = scatter_about(keys[15], (D,), 0.3, 4.0, ((0, 8),))
    cotangent = gaussian_with(keys[16], (TOKENS, D), 1.0, 6.0, ((0, 32),), (0, 1, 32, 2.75))
    return dict(tokens=tokens, latent=latent, segment_ids=segment_ids, latent_flags=latent_flags, norm1_gain=norm1_gain, norm1_shift=norm1_shift, w_qkv=w_qkv, b_qv=b_qv, w_out=w_out, b_out=b_out, norm2_gain=norm2_gain, norm2_shift=norm2_shift, w_fc=w_fc, b_fc=b_fc, w_proj=w_proj, b_proj=b_proj, cotangent=cotangent)


@jax.custom_vjp
def low(v):
    return lax.optimization_barrier(v.astype(jnp.bfloat16)).astype(jnp.float32)

@jax.custom_vjp
def low_back(v):
    return v

def low_keep(v):
    return (low(v), None)

def low_pass(kept, grad):
    return (grad,)

def back_keep(v):
    return (v, None)

def back_low(kept, grad):
    return (low(grad),)
low.defvjp(low_keep, low_pass)
low_back.defvjp(back_keep, back_low)
eps_norm = 1e-05
highest = lax.Precision.HIGHEST

def layer_norm(inputs, scale_row, shift_row):
    center = inputs - lax.optimization_barrier(jnp.mean(inputs, axis=-1, keepdims=True))
    spread = lax.optimization_barrier(jnp.mean(center * center, axis=-1, keepdims=True))
    return center * lax.rsqrt(spread + eps_norm) * scale_row + shift_row

def product(left, right):
    return jnp.dot(left, right, precision=highest, preferred_element_type=jnp.float32)

def allowed_pairs(segment_row):
    length = segment_row.shape[0]
    place = lax.broadcasted_iota(jnp.int32, (length, length), 0)
    other = lax.broadcasted_iota(jnp.int32, (length, length), 1)
    return jnp.logical_and(other <= place, segment_row[:, None] == segment_row[None, :])

def attend(pieces):
    queries, key_rows, values, segment_row = pieces
    allowed = allowed_pairs(segment_row)
    heads_q = queries.reshape(LEN, HEADS, HD).transpose(1, 0, 2)
    heads_k = key_rows.reshape(LEN, HEADS, HD).transpose(1, 0, 2)
    heads_v = values.reshape(LEN, HEADS, HD).transpose(1, 0, 2)
    raw = jnp.einsum('hqd,hkd->hqk', heads_q, heads_k, precision=highest)
    scores = low_back(raw * HD ** (-0.5))
    masked = jnp.where(allowed[None], scores, -1e+30)
    maximum = lax.optimization_barrier(jnp.max(masked, axis=2, keepdims=True))
    exponent = jnp.exp(masked - maximum)
    probable = low(exponent / lax.optimization_barrier(jnp.sum(exponent, axis=2, keepdims=True)))
    mixed = jnp.einsum('hqk,hkd->hqd', probable, heads_v, precision=highest)
    return mixed.transpose(1, 0, 2).reshape(LEN, HEADS * HD)

def forward(inputs, segments, norm1_gain, norm1_shift, w_qkv, b_qv, w_out, b_out, norm2_gain, norm2_shift, w_fc, b_fc, w_proj, b_proj):
    width = HEADS * HD
    normed = low(layer_norm(inputs, norm1_gain, norm1_shift))
    bias_row = jnp.concatenate([b_qv[:width], jnp.zeros((width,), b_qv.dtype), b_qv[width:]])
    joined = low(low_back(product(normed, w_qkv) + bias_row))
    count = segments.shape[0]

    def split(first):
        return joined[:, first * width:(first + 1) * width].reshape(count, LEN, width)
    mixed = lax.map(jax.checkpoint(attend), (split(0), split(1), split(2), segments))
    mixed = low(low_back(mixed.reshape(count * LEN, width)))
    middle = inputs + low_back(product(mixed, w_out) + b_out)
    second = low(layer_norm(middle, norm2_gain, norm2_shift))
    hidden = low_back(product(second, w_fc) + b_fc)
    active = low(jax.nn.gelu(hidden, approximate=True))
    return middle + low_back(product(active, w_proj) + b_proj)

def reference(tokens, latent, segment_ids, latent_flags, norm1_gain, norm1_shift, w_qkv, b_qv, w_out, b_out, norm2_gain, norm2_shift, w_fc, b_fc, w_proj, b_proj, cotangent):
    width = HEADS * HD
    chosen = latent_flags.reshape(-1, 1) == 1
    inputs = jnp.where(chosen, latent.astype(jnp.float32), tokens.astype(jnp.float32))
    params = jax.tree.map(lambda member: member.astype(jnp.float32), (norm1_gain, norm1_shift, w_qkv, b_qv, w_out, b_out, norm2_gain, norm2_shift, w_fc, b_fc, w_proj, b_proj))
    per_round = 4 if SEQS % 4 == 0 else 1
    rounds = SEQS // per_round
    block_inputs = inputs.reshape(rounds, per_round * LEN, width)
    block_segments = segment_ids.reshape(rounds, per_round, LEN)
    block_cots = cotangent.astype(jnp.float32).reshape(rounds, per_round * LEN, width)

    def advance(totals, record):
        row_inputs, row_segments, row_cots = record

        def local_forward(layer_in, *weights):
            return forward(layer_in, row_segments, *weights)
        result, pullback = jax.vjp(local_forward, row_inputs, *params)
        gradients = pullback(row_cots)
        updated = jax.tree.map(lambda former, latter: former + latter, totals, tuple(gradients[1:]))
        return (updated, (result.astype(jnp.bfloat16), gradients[0]))
    initial = jax.tree.map(jnp.zeros_like, params)
    totals, (results, grad_rows) = lax.scan(advance, initial, (block_inputs, block_segments, block_cots))
    return (results.reshape(TOKENS, width), grad_rows.reshape(TOKENS, width), totals[0], totals[1], totals[2], totals[3], totals[4], totals[5], totals[6], totals[7], totals[8], totals[9], totals[10], totals[11])
```

```python
from functools import partial

import jax
import jax.numpy as jnp
from jax import lax
from jax.experimental import pallas as pl
from jax.experimental.pallas import tpu as pltpu
from jax.sharding import PartitionSpec as P

D = 768
FF = 3072
NSMALL = 9216
NFFN = 6912
EPS = 1e-05
NEG = -1e30
G1, S1, BQ, BV, BO, G2, S2, BF, BP = 0, 768, 1536, 2304, 3072, 3840, 4608, 5376, 8448
F32 = jnp.float32
BF16 = jnp.bfloat16
VLIM = 60 << 20


def nn(a, b):
    return jnp.dot(a, b, preferred_element_type=F32)


def nt(a, b):
    return lax.dot_general(a, b, (((1,), (1,)), ((), ())), preferred_element_type=F32)


def norm_stats(x):
    mean = jnp.mean(x, axis=-1, keepdims=True)
    center = x - mean
    var = jnp.mean(center * center, axis=-1, keepdims=True)
    rs = lax.rsqrt(var + EPS)
    return center * rs, rs


def pick_rows(flags_row, tok, lat):
    t = flags_row.shape[1]
    col = jnp.broadcast_to(flags_row.astype(F32), (128, t)).T
    wide = jnp.concatenate([col] * (D // 128), axis=1)
    return jnp.where(wide > 0.5, lat.astype(F32), tok.astype(F32))


def ln_qkv_kernel(tok, lat, flags, small8, wq, qkv, a_t, small):
    sm = jnp.sum(small8[...].astype(F32), axis=0, keepdims=True)

    @pl.when(pl.program_id(0) == 0)
    def _():
        small[...] = sm

    x = pick_rows(flags[...], tok[...], lat[...])
    xh, _ = norm_stats(x)
    a = (xh * sm[:, G1:G1 + D] + sm[:, S1:S1 + D]).astype(BF16)
    a_t[...] = a.T
    for i in range(3):
        y = nn(a, wq[:, i * D:(i + 1) * D])
        if i == 0:
            y = y + sm[:, BQ:BQ + D]
        if i == 2:
            y = y + sm[:, BV:BV + D]
        qkv[i] = y.astype(BF16)


def ln_qkv(tok, lat, flags, small8, wq):
    n = tok.shape[0]
    t = 256
    return pl.pallas_call(
        ln_qkv_kernel,
        grid=(n // t,),
        in_specs=[
            pl.BlockSpec((t, D), lambda i: (i, 0)),
            pl.BlockSpec((t, D), lambda i: (i, 0)),
            pl.BlockSpec((1, t), lambda i: (0, i)),
            pl.BlockSpec(small8.shape, lambda i: (0, 0)),
            pl.BlockSpec((D, 3 * D), lambda i: (0, 0)),
        ],
        out_specs=[
            pl.BlockSpec((3, t, D), lambda i: (0, i, 0)),
            pl.BlockSpec((D, t), lambda i: (0, i)),
            pl.BlockSpec((1, NSMALL), lambda i: (0, 0)),
        ],
        out_shape=[
            jax.ShapeDtypeStruct((3, n, D), BF16),
            jax.ShapeDtypeStruct((D, n), BF16),
            jax.ShapeDtypeStruct((1, NSMALL), F32),
        ],
        compiler_params=pltpu.CompilerParams(vmem_limit_bytes=VLIM),
        name="ln_qkv",
    )(tok, lat, flags, small8, wq)


TQ = 256


def span(t):
    lo = max(0, t - 2)
    return lo * TQ, (t + 1 - lo) * TQ


def doc_starts(seg):
    st = jnp.zeros(seg.shape, jnp.int32)
    for s in range(1, 8):
        cnt = jnp.sum((seg < s).astype(jnp.int32), axis=1, keepdims=True)
        st = jnp.where(seg == s, cnt, st)
    return st


def build_bias(seg_ref, bias):
    st = doc_starts(seg_ref[...])
    for t in range(4):
        lo, size = span(t)
        j = lax.broadcasted_iota(jnp.int32, (size, TQ), 0) + lo
        i = lax.broadcasted_iota(jnp.int32, (size, TQ), 1) + t * TQ
        ok = jnp.logical_and(j >= st[:, t * TQ:(t + 1) * TQ], j <= i)
        bias[t, 0:size, :] = jnp.where(ok, 0.0, NEG)


def attn_fwd_kernel(seg_ref, qkv, o, lse, bias):
    @pl.when(pl.program_id(0) == 0)
    def _():
        build_bias(seg_ref, bias)

    qt = (qkv[0] * 0.125).T
    vt = qkv[2].T
    k = qkv[1]
    lane = lax.broadcasted_iota(jnp.int32, k.shape, 1)
    zero = jnp.zeros_like(k)
    ks = [jnp.where(lane < 64, k, zero), jnp.where(lane < 64, zero, k)]
    for t in range(4):
        lo, size = span(t)
        outs = []
        for h in range(2):
            s = nn(ks[h][lo:lo + size], qt[:, t * TQ:(t + 1) * TQ]) + bias[t, 0:size, :]
            m = jnp.max(s, axis=0, keepdims=True)
            p = jnp.exp(s - m)
            l = jnp.sum(p, axis=0, keepdims=True)
            ot = nn(vt[h * 64:(h + 1) * 64, lo:lo + size], p.astype(BF16))
            outs.append(ot * (1.0 / l))
            lse[0, h:h + 1, t * TQ:(t + 1) * TQ] = m + jnp.log(l)
        o[t * TQ:(t + 1) * TQ, :] = jnp.concatenate(outs, axis=0).T.astype(BF16)


def attn_fwd(seg, qkv):
    n = qkv.shape[1]
    return pl.pallas_call(
        attn_fwd_kernel,
        grid=(6,),
        in_specs=[
            pl.BlockSpec((1, n), lambda p: (0, 0)),
            pl.BlockSpec((3, n, 128), lambda p: (0, 0, p)),
        ],
        out_specs=[
            pl.BlockSpec((n, 128), lambda p: (0, p)),
            pl.BlockSpec((1, 2, n), lambda p: (p, 0, 0)),
        ],
        out_shape=[
            jax.ShapeDtypeStruct((n, D), BF16),
            jax.ShapeDtypeStruct((6, 2, n), F32),
        ],
        scratch_shapes=[pltpu.VMEM((4, 768, TQ), F32)],
        compiler_params=pltpu.CompilerParams(vmem_limit_bytes=VLIM),
        name="attn_fwd",
    )(seg, qkv)


C0 = 0.7978845608028654
C1 = 0.044715
TR = 512
TC = 512


def ffn_kernel(tok, lat, flags, small, o_h, cot_h, wo_h, wf_h, wp_h,
               out_h, dr_h, do_h, gffn_h, gsmall,
               o, cot, wo, wf, wp, gs, dfs, ct, ht, dyt, xs, rs_s, outs, dos, gwo, gwf, gwp, isem, osem):
    n = o.shape[0]
    ins = [pltpu.make_async_copy(a, b, isem.at[i]) for i, (a, b) in enumerate(
        [(o_h, o), (wo_h, wo), (cot_h, cot), (wf_h, wf), (wp_h, wp)])]
    for c in ins:
        c.start()
    gsmall[...] = jnp.zeros_like(gsmall)
    ins[0].wait()
    ins[1].wait()
    ins[2].wait()
    ins[3].wait()
    ins[4].wait()

    def row_tile(i, carry):
        r0 = pl.multiple_of(i * TR, TR)
        rows = pl.ds(r0, TR)
        x = pick_rows(flags[:, rows], tok[rows, :], lat[rows, :])
        r = x + nt(o[rows, :], wo[...]) + small[:, BO:BO + D]
        rh, rs = norm_stats(r)
        h = (rh * small[:, G2:G2 + D] + small[:, S2:S2 + D]).astype(BF16)
        ht[:, rows] = h.T
        c_t = cot[rows, :]
        ct[:, rows] = c_t.T
        gsmall[:, BP:BP + D] += jnp.sum(c_t.astype(F32), axis=0, keepdims=True)

        xs[...] = jnp.zeros_like(xs)
        rs_s[...] = jnp.zeros_like(rs_s)

        def col_tile(j, cc):
            c0 = pl.multiple_of(j * TC, TC)
            cols = pl.ds(c0, TC)
            f = nn(h, wf[:, cols]) + small[:, pl.ds(pl.multiple_of(BF + c0, 128), TC)]
            u = nn(c_t, wp[:, cols])
            f2 = f * f
            th = jnp.tanh(f * (C0 + (C0 * C1) * f2))
            hp = 0.5 + 0.5 * th
            g = f * hp
            gp = hp + (g * (2.0 - 2.0 * hp)) * (C0 + (3.0 * C0 * C1) * f2)
            gb = g.astype(BF16)
            df = (u * gp).astype(BF16)
            gs[rows, cols] = gb
            dfs[rows, cols] = df
            sl = pl.ds(pl.multiple_of(BF + c0, 128), TC)
            gsmall[:, sl] += jnp.sum(df.astype(F32), axis=0, keepdims=True)
            xs[...] += nt(gb, wp[:, cols])
            rs_s[...] += nt(df, wf[:, cols])
            return cc

        lax.fori_loop(0, FF // TC, col_tile, 0)
        outs[rows, :] = (r + xs[...] + small[:, BP:BP + D]).astype(BF16)
        dh = rs_s[...]
        gsmall[:, G2:G2 + D] += jnp.sum(dh * rh, axis=0, keepdims=True)
        gsmall[:, S2:S2 + D] += jnp.sum(dh, axis=0, keepdims=True)
        e = dh * small[:, G2:G2 + D]
        dr = c_t.astype(F32) + rs * (e - jnp.mean(e, axis=-1, keepdims=True) - rh * jnp.mean(e * rh, axis=-1, keepdims=True))
        dy = dr.astype(BF16)
        gsmall[:, BO:BO + D] += jnp.sum(dy.astype(F32), axis=0, keepdims=True)
        dyt[:, rows] = dy.T
        xs[...] = dr
        cp = pltpu.make_async_copy(xs, dr_h.at[rows, :], isem.at[0])
        cp.start()
        dos[rows, :] = nn(dy, wo[...]).astype(BF16)
        cp.wait()
        return carry

    lax.fori_loop(0, n // TR, row_tile, 0)
    c1 = pltpu.make_async_copy(outs, out_h, osem.at[0])
    c1.start()
    c2 = pltpu.make_async_copy(dos, do_h, osem.at[1])
    c2.start()

    def grad_tile(j, cc):
        cols = pl.ds(pl.multiple_of(j * TC, TC), TC)
        gwp[:, cols] = nn(ct[...], gs[:, cols]).astype(BF16)
        gwf[:, cols] = nn(ht[...], dfs[:, cols]).astype(BF16)
        return cc

    lax.fori_loop(0, FF // TC, grad_tile, 0)
    c3 = pltpu.make_async_copy(gwp, gffn_h.at[:, 0:FF], osem.at[2])
    c3.start()
    c4 = pltpu.make_async_copy(gwf, gffn_h.at[:, FF:2 * FF], osem.at[3])
    c4.start()

    def gwo_tile(j, cc):
        cols = pl.ds(pl.multiple_of(j * 256, 256), 256)
        gwo[:, cols] = nn(dyt[...], o[:, cols]).astype(BF16)
        return cc

    lax.fori_loop(0, D // 256, gwo_tile, 0)
    c5 = pltpu.make_async_copy(gwo, gffn_h.at[:, 2 * FF:], osem.at[4])
    c5.start()
    for c in (c1, c2, c3, c4, c5):
        c.wait()


def ffn(tok, lat, flags, small, o, cot, wo, wf, wp):
    n = tok.shape[0]
    anyspec = pl.BlockSpec(memory_space=pl.ANY)
    vspec = pl.BlockSpec(memory_space=pltpu.VMEM)
    return pl.pallas_call(
        ffn_kernel,
        in_specs=[vspec] * 4 + [anyspec] * 5,
        out_specs=[anyspec] * 4 + [vspec],
        out_shape=[
            jax.ShapeDtypeStruct((n, D), BF16),
            jax.ShapeDtypeStruct((n, D), F32),
            jax.ShapeDtypeStruct((n, D), BF16),
            jax.ShapeDtypeStruct((D, NFFN), BF16),
            jax.ShapeDtypeStruct((1, NSMALL), F32),
        ],
        scratch_shapes=[
            pltpu.VMEM((n, D), BF16),
            pltpu.VMEM((n, D), BF16),
            pltpu.VMEM((D, D), BF16),
            pltpu.VMEM((D, FF), BF16),
            pltpu.VMEM((D, FF), BF16),
            pltpu.VMEM((n, FF), BF16),
            pltpu.VMEM((n, FF), BF16),
            pltpu.VMEM((D, n), BF16),
            pltpu.VMEM((D, n), BF16),
            pltpu.VMEM((D, n), BF16),
            pltpu.VMEM((TR, D), F32),
            pltpu.VMEM((TR, D), F32),
            pltpu.VMEM((n, D), BF16),
            pltpu.VMEM((n, D), BF16),
            pltpu.VMEM((D, D), BF16),
            pltpu.VMEM((D, FF), BF16),
            pltpu.VMEM((D, FF), BF16),
            pltpu.SemaphoreType.DMA((5,)),
            pltpu.SemaphoreType.DMA((5,)),
        ],
        compiler_params=pltpu.CompilerParams(vmem_limit_bytes=VLIM),
        name="ffn",
    )(tok, lat, flags, small, o, cot, wo, wf, wp)


def attn_bwd_kernel(seg_ref, qkv, do, lse, dqkv, bias, dk_acc, dv_acc):
    @pl.when(pl.program_id(0) == 0)
    def _():
        build_bias(seg_ref, bias)

    q8 = qkv[0] * 0.125
    qt = q8.T
    k = qkv[1]
    kt = k.T
    v = qkv[2]
    d = do[...]
    dt = d.T
    lane = lax.broadcasted_iota(jnp.int32, k.shape, 1)
    zero = jnp.zeros_like(k)
    ks = [jnp.where(lane < 64, k, zero), jnp.where(lane < 64, zero, k)]
    vs = [jnp.where(lane < 64, v, zero), jnp.where(lane < 64, zero, v)]
    dk_acc[...] = jnp.zeros_like(dk_acc)
    dv_acc[...] = jnp.zeros_like(dv_acc)
    for t in range(4):
        lo, size = span(t)
        tq = slice(t * TQ, (t + 1) * TQ)
        dqs, dks, dvs = [], [], []
        for h in range(2):
            s = nn(ks[h][lo:lo + size], qt[:, tq]) + bias[t, 0:size, :]
            p = jnp.exp(s - lse[0, h:h + 1, tq])
            dp = nn(vs[h][lo:lo + size], dt[:, tq])
            dd = jnp.sum(dp * p, axis=0, keepdims=True)
            ds = (p * (dp - dd)).astype(BF16)
            dvs.append(nn(p.astype(BF16), d[tq, :]))
            dks.append(nn(ds, q8[tq, :]))
            dqs.append(nn(kt[h * 64:(h + 1) * 64, lo:lo + size], ds))
        lane2 = lax.broadcasted_iota(jnp.int32, (size, 128), 1)
        dk_acc[lo:lo + size, :] += jnp.where(lane2 < 64, dks[0], dks[1])
        dv_acc[lo:lo + size, :] += jnp.where(lane2 < 64, dvs[0], dvs[1])
        dqkv[0, tq, :] = (jnp.concatenate(dqs, axis=0).T * 0.125).astype(BF16)
    dqkv[1] = dk_acc[...].astype(BF16)
    dqkv[2] = dv_acc[...].astype(BF16)


def attn_bwd(seg, qkv, do, lse):
    n = qkv.shape[1]
    return pl.pallas_call(
        attn_bwd_kernel,
        grid=(6,),
        in_specs=[
            pl.BlockSpec((1, n), lambda p: (0, 0)),
            pl.BlockSpec((3, n, 128), lambda p: (0, 0, p)),
            pl.BlockSpec((n, 128), lambda p: (0, p)),
            pl.BlockSpec((1, 2, n), lambda p: (p, 0, 0)),
        ],
        out_specs=pl.BlockSpec((3, n, 128), lambda p: (0, 0, p)),
        out_shape=jax.ShapeDtypeStruct((3, n, D), BF16),
        scratch_shapes=[
            pltpu.VMEM((4, 768, TQ), F32),
            pltpu.VMEM((n, 128), F32),
            pltpu.VMEM((n, 128), F32),
        ],
        compiler_params=pltpu.CompilerParams(vmem_limit_bytes=VLIM),
        name="attn_bwd",
    )(seg, qkv, do, lse)


def last_body(tok, lat, flags, small, gsm_in, dr, dqkv, a_t, wq, gin, gwq, gsmall):
    i = pl.program_id(0)
    t = 256

    @pl.when(i == 0)
    def _():
        gsmall[...] = gsm_in[...]

    rows = pl.ds(pl.multiple_of(i * t, t), t)
    x = pick_rows(flags[:, rows], tok[rows, :], lat[rows, :])
    xh, rs = norm_stats(x)
    d0, d1, d2 = dqkv[0, rows, :], dqkv[1, rows, :], dqkv[2, rows, :]
    da = nt(d0, wq[:, 0:D]) + nt(d1, wq[:, D:2 * D]) + nt(d2, wq[:, 2 * D:3 * D])
    gsmall[:, G1:G1 + D] += jnp.sum(da * xh, axis=0, keepdims=True)
    gsmall[:, S1:S1 + D] += jnp.sum(da, axis=0, keepdims=True)
    gsmall[:, BQ:BQ + D] += jnp.sum(d0.astype(F32), axis=0, keepdims=True)
    gsmall[:, BV:BV + D] += jnp.sum(d2.astype(F32), axis=0, keepdims=True)
    e = da * small[:, G1:G1 + D]
    gin[...] = dr[...] + rs * (e - jnp.mean(e, axis=-1, keepdims=True) - xh * jnp.mean(e * xh, axis=-1, keepdims=True))
    ar = pl.ds(pl.multiple_of(i * 192, 192), 192)
    for c in range(3):
        gwq[:, c * D:(c + 1) * D] = nn(a_t[ar, :], dqkv[c]).astype(BF16)


def last(tok, lat, flags, small, gsm, dr, dqkv, a_t, wq):
    n = tok.shape[0]
    t = 256
    whole = lambda *s: pl.BlockSpec(s, lambda i: (0,) * len(s))
    return pl.pallas_call(
        last_body,
        grid=(n // t,),
        in_specs=[
            whole(n, D), whole(n, D), whole(1, n), whole(1, NSMALL), whole(1, NSMALL),
            pl.BlockSpec((t, D), lambda i: (i, 0)),
            whole(3, n, D), whole(D, n), whole(D, 3 * D),
        ],
        out_specs=[
            pl.BlockSpec((t, D), lambda i: (i, 0)),
            pl.BlockSpec((192, 3 * D), lambda i: (i, 0)),
            whole(1, NSMALL),
        ],
        out_shape=[
            jax.ShapeDtypeStruct((n, D), F32),
            jax.ShapeDtypeStruct((D, 3 * D), BF16),
            jax.ShapeDtypeStruct((1, NSMALL), F32),
        ],
        compiler_params=pltpu.CompilerParams(vmem_limit_bytes=VLIM),
        name="last",
    )(tok, lat, flags, small, gsm, dr, dqkv, a_t, wq)


MESH = pl.DeviceIdType.MESH
RQ = 24


def gather_kernel(sq, so, sf, sp, ss, gq, go, gf, gp, gs,
                  z_s, z_r, x_s, x_r, y_s, y_r, dx_s, dx_r, dy_s, dy_r, c_s, c_r, own_s, own_r, sm_s, sm_r, loc):
    r = lax.axis_index("rep")
    f = lax.axis_index("fsdp")
    src, dst = (sq, so, sf, sp), (gq, go, gf, gp)
    bar = pltpu.get_barrier_semaphore()
    for d in range(1, 8):
        pl.semaphore_signal(bar, inc=1, device_id=(r, f ^ d), device_id_type=MESH)
    for d in (1, 2):
        pl.semaphore_signal(bar, inc=1, device_id=(r ^ d, f), device_id_type=MESH)
    pl.semaphore_wait(bar, 9)

    def remote(a, b, ssem, rsem, rr, ff):
        return pltpu.make_async_remote_copy(src_ref=a, dst_ref=b, send_sem=ssem, recv_sem=rsem,
                                            device_id=(rr, ff), device_id_type=MESH)

    started = []

    def go_on(c):
        c.start()
        started.append(c)

    locals_ = [pltpu.make_async_copy(ss, gs.at[f], loc.at[4])]
    for w in range(4):
        locals_.append(pltpu.make_async_copy(src[w], dst[w].at[f], loc.at[w]))
    for c in locals_:
        c.start()
    for d in range(1, 8):
        go_on(remote(ss, gs.at[f], sm_s.at[d - 1], sm_r.at[d - 1], r, f ^ d))
    for w in range(4):
        for d in (1, 2, 3):
            go_on(remote(src[w].at[r], dst[w].at[f, r], z_s.at[w, d - 1], z_r.at[w, d - 1], r, f ^ (2 * d)))
        go_on(remote(src[w], dst[w].at[f], own_s.at[w], own_r.at[w], r, f ^ 1))

    def piece(w, d, q):
        return dst[w].at[f ^ (2 * d), q]

    def half(w, d, q, k):
        n = dst[w].shape[-1] // 2
        return dst[w].at[f ^ (2 * d), q, :, k * n:(k + 1) * n]

    def core(w, d, kind, q):
        go_on(remote(piece(w, d, q), piece(w, d, q), c_s.at[w, d - 1, kind], c_r.at[w, d - 1, kind], r, f ^ 1))

    def first(w):
        for d in (1, 2, 3):
            p = piece(w, d, r)
            remote(p, p, z_s.at[w, d - 1], z_r.at[w, d - 1], r, f).wait_recv()
            go_on(remote(p, p, x_s.at[w, d - 1], x_r.at[w, d - 1], r ^ 1, f))
            go_on(remote(p, p, y_s.at[w, d - 1], y_r.at[w, d - 1], r ^ 2, f))
            core(w, d, 0, r)

    def second(w):
        for d in (1, 2, 3):
            p = piece(w, d, r ^ 1)
            remote(p, p, x_s.at[w, d - 1], x_r.at[w, d - 1], r, f).wait_recv()
            h = half(w, d, r ^ 1, 0)
            go_on(remote(h, h, dy_s.at[w, d - 1], dy_r.at[w, d - 1], r ^ 2, f))
            core(w, d, 1, r ^ 1)
            p = piece(w, d, r ^ 2)
            remote(p, p, y_s.at[w, d - 1], y_r.at[w, d - 1], r, f).wait_recv()
            h = half(w, d, r ^ 2, 1)
            go_on(remote(h, h, dx_s.at[w, d - 1], dx_r.at[w, d - 1], r ^ 1, f))
            core(w, d, 2, r ^ 2)

    def third(w):
        for d in (1, 2, 3):
            h = half(w, d, r ^ 3, 0)
            remote(h, h, dy_s.at[w, d - 1], dy_r.at[w, d - 1], r, f).wait_recv()
            h = half(w, d, r ^ 3, 1)
            remote(h, h, dx_s.at[w, d - 1], dx_r.at[w, d - 1], r, f).wait_recv()
            core(w, d, 3, r ^ 3)

    for step in range(6):
        if step < 4:
            first(step)
        if 0 <= step - 1 < 4:
            second(step - 1)
        if 0 <= step - 2 < 4:
            third(step - 2)

    for w in range(4):
        remote(src[w], dst[w].at[f ^ 1], own_s.at[w], own_r.at[w], r, f).wait_recv()
        for d in (1, 2, 3):
            for kind, q in enumerate((r, r ^ 1, r ^ 2, r ^ 3)):
                p = dst[w].at[(f ^ 1) ^ (2 * d), q]
                remote(p, p, c_s.at[w, d - 1, kind], c_r.at[w, d - 1, kind], r, f).wait_recv()
    for d in range(1, 8):
        remote(ss, gs.at[f ^ d], sm_s.at[d - 1], sm_r.at[d - 1], r, f).wait_recv()
    for c in locals_:
        c.wait()
    for c in started:
        c.wait_send()


def gather_all(ws, row):
    dma = pltpu.SemaphoreType.DMA
    anyspec = pl.BlockSpec(memory_space=pl.ANY)
    shards_ = [w.reshape(4, RQ, w.shape[1]) for w in ws]
    outs = pl.pallas_call(
        gather_kernel,
        in_specs=[anyspec] * 5,
        out_specs=[anyspec] * 5,
        out_shape=[jax.ShapeDtypeStruct((8,) + s.shape, BF16) for s in shards_]
        + [jax.ShapeDtypeStruct((8,) + row.shape, row.dtype)],
        scratch_shapes=[dma((4, 3))] * 10 + [dma((4, 3, 4))] * 2 + [dma((4,))] * 2 + [dma((7,))] * 2 + [dma((5,))],
        compiler_params=pltpu.CompilerParams(collective_id=1, has_side_effects=True),
        name="gather_all",
    )(*shards_, row)
    return [o.reshape(D, o.shape[-1]) for o in outs[:4]] + [outs[4].reshape(8, NSMALL)]


NCH = 12
CW = 768


def reduce_kernel(gf, gq, sg, fin, small, l1, r1, r2, r3, r4, sbuf, srcv,
                  ls, a_s, a_r, b_s, b_r, d_s, d_r, e_s, e_r, h_s, h_r, m_s, m_r):
    r = lax.axis_index("rep")
    f = lax.axis_index("fsdp")
    c, z, x, y = f & 1, f >> 1, r & 1, r >> 1
    bar = pltpu.get_barrier_semaphore()
    for d in (1, 2, 4, 6):
        pl.semaphore_signal(bar, inc=1, device_id=(r, f ^ d), device_id_type=MESH)
    for d in (1, 2, 3):
        pl.semaphore_signal(bar, inc=1, device_id=(r ^ d, f), device_id_type=MESH)
    pl.semaphore_wait(bar, 7)

    def remote(a, b, ssem, rsem, rr, ff):
        return pltpu.make_async_remote_copy(src_ref=a, dst_ref=b, send_sem=ssem, recv_sem=rsem,
                                            device_id=(rr, ff), device_id_type=MESH)

    def first_pair(k, g, kk):
        cols = pl.ds(pl.multiple_of(kk * CW, CW), CW)
        return (remote(g.at[:, 1 - c, :, :, :, cols], r1.at[k], a_s.at[k], a_r.at[k], r, f ^ 1),
                pltpu.make_async_copy(g.at[:, c, :, :, :, cols], l1.at[k], ls.at[k]))

    def start1(k):
        @pl.when(k < 9)
        def _():
            for cp in first_pair(k, gf, k):
                cp.start()

        @pl.when(k >= 9)
        def _():
            for cp in first_pair(k, gq, k - 9):
                cp.start()

    def hop2(k, even):
        if even:
            return remote(l1.at[k, :, :, 1 - x], r2.at[k], b_s.at[k], b_r.at[k], r ^ 1, f)
        return remote(l1.at[k, :, 1 - y], r2.at[k], b_s.at[k], b_r.at[k], r ^ 2, f)

    def hop3(k, even):
        if even:
            return remote(r2.at[k, :, 1 - y], r3.at[k], d_s.at[k], d_r.at[k], r ^ 2, f)
        return remote(r2.at[k, :, 1 - x], r3.at[k], d_s.at[k], d_r.at[k], r ^ 1, f)

    def hop4(k, d):
        return remote(r3.at[k, z ^ d], r4.at[k, d - 1], e_s.at[k, d - 1], e_r.at[k, d - 1], r, f ^ (2 * d))

    def hop5(k, d):
        return remote(fin.at[k, r], fin.at[k, r], h_s.at[k, d - 1], h_r.at[k, d - 1], r ^ d, f)

    def hop5_in(k, d):
        return remote(fin.at[k, r ^ d], fin.at[k, r ^ d], h_s.at[k, d - 1], h_r.at[k, d - 1], r ^ d, f)

    def parity(k, fn):
        @pl.when(k % 2 == 0)
        def _():
            fn(True)

        @pl.when(k % 2 == 1)
        def _():
            fn(False)

    def start2(k):
        cp = first_pair(k, gf, 0)
        cp[0].wait()
        cp[1].wait()

        def add(i, cc):
            l1[k, i] = (l1[k, i].astype(F32) + r1[k, i].astype(F32)).astype(BF16)
            return cc

        lax.fori_loop(0, 4, add, 0)
        parity(k, lambda even: hop2(k, even).start())

    def start3(k):
        def run(even):
            hop2(k, even).wait()

            def add(i, cc):
                own = l1[k, i, :, x] if even else l1[k, i, y]
                r2[k, i] = (own.astype(F32) + r2[k, i].astype(F32)).astype(BF16)
                return cc

            lax.fori_loop(0, 4, add, 0)
            hop3(k, even).start()

        parity(k, run)

    def start4(k):
        def run(even):
            hop3(k, even).wait()

            def add(i, cc):
                own = r2[k, i, y] if even else r2[k, i, x]
                r3[k, i] = (own.astype(F32) + r3[k, i].astype(F32)).astype(BF16)
                return cc

            lax.fori_loop(0, 4, add, 0)

        parity(k, run)
        for d in (1, 2, 3):
            hop4(k, d).start()

    def start5(k):
        total = r3[k, z].astype(F32)
        for d in (1, 2, 3):
            hop4(k, d).wait()
            total = total + r4[k, d - 1].astype(F32)
        fin[k, r] = total.astype(BF16)
        for d in (1, 2, 3):
            hop5(k, d).start()

    def finish(k):
        for d in (1, 2, 3):
            hop5(k, d).wait_send()
            hop5_in(k, d).wait_recv()

    partners = ((r, f ^ 1), (r ^ 1, f), (r ^ 2, f), (r, f ^ 2), (r, f ^ 4))

    def small_hop(i):
        return remote(sbuf.at[i], srcv.at[i], m_s.at[i], m_r.at[i], *partners[i])

    sbuf[0] = sg[...]
    small_hop(0).start()

    def step(i, cc):
        for fn, lag in ((start1, 0), (start2, 1), (start3, 2), (start4, 3), (start5, 4), (finish, 5)):
            k = i - lag

            @pl.when(jnp.logical_and(k >= 0, k < NCH))
            def _(fn=fn, k=k):
                fn(k)

        return cc

    for i in range(5):
        step(jnp.int32(i), 0)
        small_hop(i).wait()
        v = sbuf[i] + srcv[i]
        if i < 4:
            sbuf[i + 1] = v
            small_hop(i + 1).start()
        else:
            small[...] = v
    lax.fori_loop(5, NCH + 5, step, 0)


def reduce_all(gffn, gq, small):
    dma = pltpu.SemaphoreType.DMA
    anyspec = pl.BlockSpec(memory_space=pl.ANY)
    vspec = pl.BlockSpec(memory_space=pltpu.VMEM)
    fin, sm = pl.pallas_call(
        reduce_kernel,
        in_specs=[anyspec, anyspec, vspec],
        out_specs=[vspec, vspec],
        out_shape=[jax.ShapeDtypeStruct((NCH, 4, RQ, CW), BF16), jax.ShapeDtypeStruct((1, NSMALL), F32)],
        scratch_shapes=[
            pltpu.VMEM((NCH, 4, 2, 2, RQ, CW), BF16),
            pltpu.VMEM((NCH, 4, 2, 2, RQ, CW), BF16),
            pltpu.VMEM((NCH, 4, 2, RQ, CW), BF16),
            pltpu.VMEM((NCH, 4, RQ, CW), BF16),
            pltpu.VMEM((NCH, 3, RQ, CW), BF16),
            pltpu.VMEM((5, 1, NSMALL), F32),
            pltpu.VMEM((5, 1, NSMALL), F32),
            dma((NCH,)), dma((NCH,)), dma((NCH,)), dma((NCH,)), dma((NCH,)), dma((NCH,)), dma((NCH,)),
            dma((NCH, 3)), dma((NCH, 3)), dma((NCH, 3)), dma((NCH, 3)), dma((5,)), dma((5,)),
        ],
        compiler_params=pltpu.CompilerParams(collective_id=2, has_side_effects=True, vmem_limit_bytes=VLIM),
        name="reduce_all",
    )(gffn.reshape(4, 2, 2, 2, RQ, NFFN), gq.reshape(4, 2, 2, 2, RQ, 3 * D), small)
    rows = fin.reshape(NCH, 96, CW)
    wide = lambda a: a.transpose(1, 0, 2).reshape(96, -1)
    return wide(rows[9:]), wide(rows[8:9]), wide(rows[4:8]), wide(rows[:4]), sm


def own_slots(v, nf, f):
    m = v.shape[0]
    wide = jnp.broadcast_to(v[None, :], (nf, m))
    mine = lax.broadcasted_iota(jnp.int32, (nf, m), 0) == f
    return jnp.where(mine, wide, jnp.zeros_like(wide)).reshape(-1)


def shards(fast, tokens, latent, segment_ids, latent_flags, norm1_gain, norm1_shift, w_qkv, b_qv, w_out, b_out,
           norm2_gain, norm2_shift, w_fc, b_fc, w_proj, b_proj, cotangent):
    nf = lax.axis_size("fsdp")
    f = lax.axis_index("fsdp")
    vectors = (norm1_gain, norm1_shift, b_qv, b_out, norm2_gain, norm2_shift, b_fc, b_proj)
    row = jnp.concatenate([own_slots(v, nf, f) for v in vectors]).reshape(1, NSMALL)
    ws = (w_qkv, w_out.T, w_fc, w_proj.T)
    if fast:
        wq, wo, wf, wp, small8 = gather_all(ws, row)
    else:
        wq, wo, wf, wp = [lax.all_gather(w, "fsdp", axis=0, tiled=True) for w in ws]
        small8 = lax.all_gather(row, "fsdp", axis=0, tiled=True)
    qkv, a_t, small = ln_qkv(tokens, latent, latent_flags, small8, wq)
    o, lse = attn_fwd(segment_ids, qkv)
    out, dr, do, gffn, gsm = ffn(tokens, latent, latent_flags, small, o, cotangent, wo, wf, wp)
    dqkv = attn_bwd(segment_ids, qkv, do, lse)
    gin, gq, gsm = last(tokens, latent, latent_flags, small, gsm, dr, dqkv, a_t, wq)
    if fast:
        tq, to, tf, tp, gsm = reduce_all(gffn, gq, gsm)
    else:
        def scatter(g):
            part = lax.psum_scatter(g, "fsdp", scatter_dimension=0, tiled=True)
            return lax.psum(part, "rep")

        tq, tp, tf, to = [scatter(g) for g in (gq, gffn[:, :FF], gffn[:, FF:2 * FF], gffn[:, 2 * FF:])]
        gsm = lax.psum(gsm, ("rep", "fsdp"))

    def mine(at, v):
        m = v.shape[0]
        return lax.dynamic_slice(gsm[0], (at + f * m,), (m,))

    v = [mine(at, v) for at, v in zip((G1, S1, BQ, BO, G2, S2, BF, BP), vectors)]
    return (out, gin, v[0], v[1], tq.astype(F32), v[2], to.astype(F32).T, v[3], v[4], v[5],
            tf.astype(F32), v[6], tp.astype(F32).T, v[7])


def solution(mesh):
    fast = mesh.shape["rep"] == 4 and mesh.shape["fsdp"] == 8
    both = P(("rep", "fsdp"), None)
    one, row, col = P("fsdp"), P("fsdp", None), P(None, "fsdp")
    return jax.shard_map(
        partial(shards, fast),
        mesh=mesh,
        in_specs=(both, both, both, both, one, one, row, one, col, one, one, one, row, one, col, one, both),
        out_specs=(both, both, one, one, row, one, col, one, one, one, row, one, col, one),
        check_vma=False,
    )
```

```python
from functools import partial

import jax
import jax.numpy as jnp
from jax import lax
from jax.experimental import pallas as pl
from jax.experimental.pallas import tpu as pltpu
from jax.sharding import PartitionSpec as P

D = 768
FF = 3072
NSMALL = 9216
NFFN = 6912
EPS = 1e-05
NEG = -1e30
G1, S1, BQ, BV, BO, G2, S2, BF, BP = 0, 768, 1536, 2304, 3072, 3840, 4608, 5376, 8448
F32 = jnp.float32
BF16 = jnp.bfloat16
VLIM = 60 << 20


def nn(a, b):
    return jnp.dot(a, b, preferred_element_type=F32)


def nt(a, b):
    return lax.dot_general(a, b, (((1,), (1,)), ((), ())), preferred_element_type=F32)


def norm_stats(x):
    mean = jnp.mean(x, axis=-1, keepdims=True)
    center = x - mean
    var = jnp.mean(center * center, axis=-1, keepdims=True)
    rs = lax.rsqrt(var + EPS)
    return center * rs, rs


def pick_rows(flags_row, tok, lat):
    t = flags_row.shape[1]
    col = jnp.broadcast_to(flags_row.astype(F32), (128, t)).T
    wide = jnp.concatenate([col] * (D // 128), axis=1)
    return jnp.where(wide > 0.5, lat.astype(F32), tok.astype(F32))


def ln_qkv_kernel(tok, lat, flags, small8, wq, qkv, a_t, small):
    sm = jnp.sum(small8[...].astype(F32), axis=0, keepdims=True)

    @pl.when(pl.program_id(0) == 0)
    def _():
        small[...] = sm

    x = pick_rows(flags[...], tok[...], lat[...])
    xh, _ = norm_stats(x)
    a = (xh * sm[:, G1:G1 + D] + sm[:, S1:S1 + D]).astype(BF16)
    a_t[...] = a.T
    for i in range(3):
        y = nn(a, wq[:, i * D:(i + 1) * D])
        if i == 0:
            y = y + sm[:, BQ:BQ + D]
        if i == 2:
            y = y + sm[:, BV:BV + D]
        qkv[i] = y.astype(BF16)


def ln_qkv(tok, lat, flags, small8, wq):
    n = tok.shape[0]
    t = 256
    return pl.pallas_call(
        ln_qkv_kernel,
        grid=(n // t,),
        in_specs=[
            pl.BlockSpec((t, D), lambda i: (i, 0)),
            pl.BlockSpec((t, D), lambda i: (i, 0)),
            pl.BlockSpec((1, t), lambda i: (0, i)),
            pl.BlockSpec(small8.shape, lambda i: (0, 0)),
            pl.BlockSpec((D, 3 * D), lambda i: (0, 0)),
        ],
        out_specs=[
            pl.BlockSpec((3, t, D), lambda i: (0, i, 0)),
            pl.BlockSpec((D, t), lambda i: (0, i)),
            pl.BlockSpec((1, NSMALL), lambda i: (0, 0)),
        ],
        out_shape=[
            jax.ShapeDtypeStruct((3, n, D), BF16),
            jax.ShapeDtypeStruct((D, n), BF16),
            jax.ShapeDtypeStruct((1, NSMALL), F32),
        ],
        compiler_params=pltpu.CompilerParams(vmem_limit_bytes=VLIM),
        name="ln_qkv",
    )(tok, lat, flags, small8, wq)


TQ = 256


def span(t):
    lo = max(0, t - 2)
    return lo * TQ, (t + 1 - lo) * TQ


def doc_starts(seg):
    st = jnp.zeros(seg.shape, jnp.int32)
    for s in range(1, 8):
        cnt = jnp.sum((seg < s).astype(jnp.int32), axis=1, keepdims=True)
        st = jnp.where(seg == s, cnt, st)
    return st


def build_bias(seg_ref, bias):
    st = doc_starts(seg_ref[...])
    for t in range(4):
        lo, size = span(t)
        j = lax.broadcasted_iota(jnp.int32, (size, TQ), 0) + lo
        i = lax.broadcasted_iota(jnp.int32, (size, TQ), 1) + t * TQ
        ok = jnp.logical_and(j >= st[:, t * TQ:(t + 1) * TQ], j <= i)
        bias[t, 0:size, :] = jnp.where(ok, 0.0, NEG)


def attn_fwd_kernel(seg_ref, qkv, o, lse, bias):
    @pl.when(pl.program_id(0) == 0)
    def _():
        build_bias(seg_ref, bias)

    qt = (qkv[0] * 0.125).T
    vt = qkv[2].T
    k = qkv[1]
    lane = lax.broadcasted_iota(jnp.int32, k.shape, 1)
    zero = jnp.zeros_like(k)
    ks = [jnp.where(lane < 64, k, zero), jnp.where(lane < 64, zero, k)]
    for t in range(4):
        lo, size = span(t)
        outs = []
        for h in range(2):
            s = nn(ks[h][lo:lo + size], qt[:, t * TQ:(t + 1) * TQ]) + bias[t, 0:size, :]
            m = jnp.max(s, axis=0, keepdims=True)
            p = jnp.exp(s - m)
            l = jnp.sum(p, axis=0, keepdims=True)
            ot = nn(vt[h * 64:(h + 1) * 64, lo:lo + size], p.astype(BF16))
            outs.append(ot * (1.0 / l))
            lse[0, h:h + 1, t * TQ:(t + 1) * TQ] = m + jnp.log(l)
        o[t * TQ:(t + 1) * TQ, :] = jnp.concatenate(outs, axis=0).T.astype(BF16)


def attn_fwd(seg, qkv):
    n = qkv.shape[1]
    return pl.pallas_call(
        attn_fwd_kernel,
        grid=(6,),
        in_specs=[
            pl.BlockSpec((1, n), lambda p: (0, 0)),
            pl.BlockSpec((3, n, 128), lambda p: (0, 0, p)),
        ],
        out_specs=[
            pl.BlockSpec((n, 128), lambda p: (0, p)),
            pl.BlockSpec((1, 2, n), lambda p: (p, 0, 0)),
        ],
        out_shape=[
            jax.ShapeDtypeStruct((n, D), BF16),
            jax.ShapeDtypeStruct((6, 2, n), F32),
        ],
        scratch_shapes=[pltpu.VMEM((4, 768, TQ), F32)],
        compiler_params=pltpu.CompilerParams(vmem_limit_bytes=VLIM),
        name="attn_fwd",
    )(seg, qkv)


C0 = 0.7978845608028654
C1 = 0.044715
TR = 512
TC = 512


def ffn_kernel(tok, lat, flags, small, o_h, cot_h, wo_h, wf_h, wp_h,
               out_h, dr_h, do_h, gffn_h, gsmall,
               o, cot, wo, wf, wp, gs, dfs, ct, ht, dyt, xs, rs_s, outs, dos, gwo, gwf, gwp, isem, osem):
    n = o.shape[0]
    ins = [pltpu.make_async_copy(a, b, isem.at[i]) for i, (a, b) in enumerate(
        [(o_h, o), (wo_h, wo), (cot_h, cot), (wf_h, wf), (wp_h, wp)])]
    for c in ins:
        c.start()
    gsmall[...] = jnp.zeros_like(gsmall)
    ins[0].wait()
    ins[1].wait()
    ins[2].wait()
    ins[3].wait()
    ins[4].wait()

    def row_tile(i, carry):
        r0 = pl.multiple_of(i * TR, TR)
        rows = pl.ds(r0, TR)
        x = pick_rows(flags[:, rows], tok[rows, :], lat[rows, :])
        r = x + nt(o[rows, :], wo[...]) + small[:, BO:BO + D]
        rh, rs = norm_stats(r)
        h = (rh * small[:, G2:G2 + D] + small[:, S2:S2 + D]).astype(BF16)
        ht[:, rows] = h.T
        c_t = cot[rows, :]
        ct[:, rows] = c_t.T
        gsmall[:, BP:BP + D] += jnp.sum(c_t.astype(F32), axis=0, keepdims=True)

        xs[...] = jnp.zeros_like(xs)
        rs_s[...] = jnp.zeros_like(rs_s)

        def col_tile(j, cc):
            c0 = pl.multiple_of(j * TC, TC)
            cols = pl.ds(c0, TC)
            f = nn(h, wf[:, cols]) + small[:, pl.ds(pl.multiple_of(BF + c0, 128), TC)]
            u = nn(c_t, wp[:, cols])
            f2 = f * f
            th = jnp.tanh(f * (C0 + (C0 * C1) * f2))
            hp = 0.5 + 0.5 * th
            g = f * hp
            gp = hp + (g * (2.0 - 2.0 * hp)) * (C0 + (3.0 * C0 * C1) * f2)
            gb = g.astype(BF16)
            df = (u * gp).astype(BF16)
            gs[rows, cols] = gb
            dfs[rows, cols] = df
            sl = pl.ds(pl.multiple_of(BF + c0, 128), TC)
            gsmall[:, sl] += jnp.sum(df.astype(F32), axis=0, keepdims=True)
            xs[...] += nt(gb, wp[:, cols])
            rs_s[...] += nt(df, wf[:, cols])
            return cc

        lax.fori_loop(0, FF // TC, col_tile, 0)
        outs[rows, :] = (r + xs[...] + small[:, BP:BP + D]).astype(BF16)
        dh = rs_s[...]
        gsmall[:, G2:G2 + D] += jnp.sum(dh * rh, axis=0, keepdims=True)
        gsmall[:, S2:S2 + D] += jnp.sum(dh, axis=0, keepdims=True)
        e = dh * small[:, G2:G2 + D]
        dr = c_t.astype(F32) + rs * (e - jnp.mean(e, axis=-1, keepdims=True) - rh * jnp.mean(e * rh, axis=-1, keepdims=True))
        dy = dr.astype(BF16)
        gsmall[:, BO:BO + D] += jnp.sum(dy.astype(F32), axis=0, keepdims=True)
        dyt[:, rows] = dy.T
        xs[...] = dr
        cp = pltpu.make_async_copy(xs, dr_h.at[rows, :], isem.at[0])
        cp.start()
        dos[rows, :] = nn(dy, wo[...]).astype(BF16)
        cp.wait()
        return carry

    lax.fori_loop(0, n // TR, row_tile, 0)
    c1 = pltpu.make_async_copy(outs, out_h, osem.at[0])
    c1.start()
    c2 = pltpu.make_async_copy(dos, do_h, osem.at[1])
    c2.start()

    def grad_tile(j, cc):
        cols = pl.ds(pl.multiple_of(j * TC, TC), TC)
        gwp[:, cols] = nn(ct[...], gs[:, cols]).astype(BF16)
        gwf[:, cols] = nn(ht[...], dfs[:, cols]).astype(BF16)
        return cc

    lax.fori_loop(0, FF // TC, grad_tile, 0)
    c3 = pltpu.make_async_copy(gwp, gffn_h.at[:, 0:FF], osem.at[2])
    c3.start()
    c4 = pltpu.make_async_copy(gwf, gffn_h.at[:, FF:2 * FF], osem.at[3])
    c4.start()

    def gwo_tile(j, cc):
        cols = pl.ds(pl.multiple_of(j * 256, 256), 256)
        gwo[:, cols] = nn(dyt[...], o[:, cols]).astype(BF16)
        return cc

    lax.fori_loop(0, D // 256, gwo_tile, 0)
    c5 = pltpu.make_async_copy(gwo, gffn_h.at[:, 2 * FF:], osem.at[4])
    c5.start()
    for c in (c1, c2, c3, c4, c5):
        c.wait()


def ffn(tok, lat, flags, small, o, cot, wo, wf, wp):
    n = tok.shape[0]
    anyspec = pl.BlockSpec(memory_space=pl.ANY)
    vspec = pl.BlockSpec(memory_space=pltpu.VMEM)
    return pl.pallas_call(
        ffn_kernel,
        in_specs=[vspec] * 4 + [anyspec] * 5,
        out_specs=[anyspec] * 4 + [vspec],
        out_shape=[
            jax.ShapeDtypeStruct((n, D), BF16),
            jax.ShapeDtypeStruct((n, D), F32),
            jax.ShapeDtypeStruct((n, D), BF16),
            jax.ShapeDtypeStruct((D, NFFN), BF16),
            jax.ShapeDtypeStruct((1, NSMALL), F32),
        ],
        scratch_shapes=[
            pltpu.VMEM((n, D), BF16),
            pltpu.VMEM((n, D), BF16),
            pltpu.VMEM((D, D), BF16),
            pltpu.VMEM((D, FF), BF16),
            pltpu.VMEM((D, FF), BF16),
            pltpu.VMEM((n, FF), BF16),
            pltpu.VMEM((n, FF), BF16),
            pltpu.VMEM((D, n), BF16),
            pltpu.VMEM((D, n), BF16),
            pltpu.VMEM((D, n), BF16),
            pltpu.VMEM((TR, D), F32),
            pltpu.VMEM((TR, D), F32),
            pltpu.VMEM((n, D), BF16),
            pltpu.VMEM((n, D), BF16),
            pltpu.VMEM((D, D), BF16),
            pltpu.VMEM((D, FF), BF16),
            pltpu.VMEM((D, FF), BF16),
            pltpu.SemaphoreType.DMA((5,)),
            pltpu.SemaphoreType.DMA((5,)),
        ],
        compiler_params=pltpu.CompilerParams(vmem_limit_bytes=VLIM),
        name="ffn",
    )(tok, lat, flags, small, o, cot, wo, wf, wp)


def attn_bwd_kernel(seg_ref, qkv, do, lse, dqkv, bias, dk_acc, dv_acc):
    @pl.when(pl.program_id(0) == 0)
    def _():
        build_bias(seg_ref, bias)

    q8 = qkv[0] * 0.125
    qt = q8.T
    k = qkv[1]
    kt = k.T
    v = qkv[2]
    d = do[...]
    dt = d.T
    lane = lax.broadcasted_iota(jnp.int32, k.shape, 1)
    zero = jnp.zeros_like(k)
    ks = [jnp.where(lane < 64, k, zero), jnp.where(lane < 64, zero, k)]
    vs = [jnp.where(lane < 64, v, zero), jnp.where(lane < 64, zero, v)]
    dk_acc[...] = jnp.zeros_like(dk_acc)
    dv_acc[...] = jnp.zeros_like(dv_acc)
    for t in range(4):
        lo, size = span(t)
        tq = slice(t * TQ, (t + 1) * TQ)
        dqs, dks, dvs = [], [], []
        for h in range(2):
            s = nn(ks[h][lo:lo + size], qt[:, tq]) + bias[t, 0:size, :]
            p = jnp.exp(s - lse[0, h:h + 1, tq])
            dp = nn(vs[h][lo:lo + size], dt[:, tq])
            dd = jnp.sum(dp * p, axis=0, keepdims=True)
            ds = (p * (dp - dd)).astype(BF16)
            dvs.append(nn(p.astype(BF16), d[tq, :]))
            dks.append(nn(ds, q8[tq, :]))
            dqs.append(nn(kt[h * 64:(h + 1) * 64, lo:lo + size], ds))
        lane2 = lax.broadcasted_iota(jnp.int32, (size, 128), 1)
        dk_acc[lo:lo + size, :] += jnp.where(lane2 < 64, dks[0], dks[1])
        dv_acc[lo:lo + size, :] += jnp.where(lane2 < 64, dvs[0], dvs[1])
        dqkv[0, tq, :] = (jnp.concatenate(dqs, axis=0).T * 0.125).astype(BF16)
    dqkv[1] = dk_acc[...].astype(BF16)
    dqkv[2] = dv_acc[...].astype(BF16)


def attn_bwd(seg, qkv, do, lse):
    n = qkv.shape[1]
    return pl.pallas_call(
        attn_bwd_kernel,
        grid=(6,),
        in_specs=[
            pl.BlockSpec((1, n), lambda p: (0, 0)),
            pl.BlockSpec((3, n, 128), lambda p: (0, 0, p)),
            pl.BlockSpec((n, 128), lambda p: (0, p)),
            pl.BlockSpec((1, 2, n), lambda p: (p, 0, 0)),
        ],
        out_specs=pl.BlockSpec((3, n, 128), lambda p: (0, 0, p)),
        out_shape=jax.ShapeDtypeStruct((3, n, D), BF16),
        scratch_shapes=[
            pltpu.VMEM((4, 768, TQ), F32),
            pltpu.VMEM((n, 128), F32),
            pltpu.VMEM((n, 128), F32),
        ],
        compiler_params=pltpu.CompilerParams(vmem_limit_bytes=VLIM),
        name="attn_bwd",
    )(seg, qkv, do, lse)


def last_body(tok, lat, flags, small, gsm_in, dr, dqkv, a_t, wq, gin, gwq, gsmall):
    i = pl.program_id(0)
    t = 256

    @pl.when(i == 0)
    def _():
        gsmall[...] = gsm_in[...]

    rows = pl.ds(pl.multiple_of(i * t, t), t)
    x = pick_rows(flags[:, rows], tok[rows, :], lat[rows, :])
    xh, rs = norm_stats(x)
    d0, d1, d2 = dqkv[0, rows, :], dqkv[1, rows, :], dqkv[2, rows, :]
    da = nt(d0, wq[:, 0:D]) + nt(d1, wq[:, D:2 * D]) + nt(d2, wq[:, 2 * D:3 * D])
    gsmall[:, G1:G1 + D] += jnp.sum(da * xh, axis=0, keepdims=True)
    gsmall[:, S1:S1 + D] += jnp.sum(da, axis=0, keepdims=True)
    gsmall[:, BQ:BQ + D] += jnp.sum(d0.astype(F32), axis=0, keepdims=True)
    gsmall[:, BV:BV + D] += jnp.sum(d2.astype(F32), axis=0, keepdims=True)
    e = da * small[:, G1:G1 + D]
    gin[...] = dr[...] + rs * (e - jnp.mean(e, axis=-1, keepdims=True) - xh * jnp.mean(e * xh, axis=-1, keepdims=True))
    ar = pl.ds(pl.multiple_of(i * 192, 192), 192)
    for c in range(3):
        gwq[:, c * D:(c + 1) * D] = nn(a_t[ar, :], dqkv[c]).astype(BF16)


def last(tok, lat, flags, small, gsm, dr, dqkv, a_t, wq):
    n = tok.shape[0]
    t = 256
    whole = lambda *s: pl.BlockSpec(s, lambda i: (0,) * len(s))
    return pl.pallas_call(
        last_body,
        grid=(n // t,),
        in_specs=[
            whole(n, D), whole(n, D), whole(1, n), whole(1, NSMALL), whole(1, NSMALL),
            pl.BlockSpec((t, D), lambda i: (i, 0)),
            whole(3, n, D), whole(D, n), whole(D, 3 * D),
        ],
        out_specs=[
            pl.BlockSpec((t, D), lambda i: (i, 0)),
            pl.BlockSpec((192, 3 * D), lambda i: (i, 0)),
            whole(1, NSMALL),
        ],
        out_shape=[
            jax.ShapeDtypeStruct((n, D), F32),
            jax.ShapeDtypeStruct((D, 3 * D), BF16),
            jax.ShapeDtypeStruct((1, NSMALL), F32),
        ],
        compiler_params=pltpu.CompilerParams(vmem_limit_bytes=VLIM),
        name="last",
    )(tok, lat, flags, small, gsm, dr, dqkv, a_t, wq)


MESH = pl.DeviceIdType.MESH
RQ = 24
NCH = 12


def remote(a, b, ssem, rsem, rr, ff):
    return pltpu.make_async_remote_copy(src_ref=a, dst_ref=b, send_sem=ssem, recv_sem=rsem,
                                        device_id=(rr, ff), device_id_type=MESH)


def first_kernel(sq, so, sf, sp, ss, tok_h, lat_h, flags, seg,
                 g, qkv_h, o_h, lse, small,
                 small8, wq, a_v, lat_v, qkv, o_v, bias,
                 z_s, z_r, x_s, x_r, y_s, y_r, dx_s, dx_r, dy_s, dy_r, c_s, c_r, own_s, own_r, sm_s, sm_r, loc, ld):
    r = lax.axis_index("rep")
    f = lax.axis_index("fsdp")
    n = a_v.shape[0]
    loads = [pltpu.make_async_copy(tok_h, a_v, ld.at[0]), pltpu.make_async_copy(lat_h, lat_v, ld.at[1])]
    for c in loads:
        c.start()
    bar = pltpu.get_barrier_semaphore()
    for d in range(1, 8):
        pl.semaphore_signal(bar, inc=1, device_id=(r, f ^ d), device_id_type=MESH)
    for d in (1, 2):
        pl.semaphore_signal(bar, inc=1, device_id=(r ^ d, f), device_id_type=MESH)
    pl.semaphore_wait(bar, 9)

    sources = [(sq, i) for i in range(3)] + [(so, 0)] + [(sf, i) for i in range(4)] + [(sp, i) for i in range(4)]

    def issue(k):
        ref, i = sources[k]
        cols = slice(i * D, (i + 1) * D)
        for d in (1, 2, 3):
            remote(ref.at[r, :, cols], g.at[k, f, r], z_s.at[k], z_r.at[k], r, f ^ (2 * d)).start()
        remote(ref.at[:, :, cols], g.at[k, f], own_s.at[k], own_r.at[k], r, f ^ 1).start()
        pltpu.make_async_copy(ref.at[:, :, cols], g.at[k, f], loc.at[k]).start()

    def piece(k, d, q):
        return g.at[k, f ^ (2 * d), q]

    def half(k, d, q, h):
        return g.at[k, f ^ (2 * d), q, :, h * 384:(h + 1) * 384]

    def core(k, q):
        for d in (1, 2, 3):
            remote(piece(k, d, q), piece(k, d, q), c_s.at[k], c_r.at[k], r, f ^ 1).start()

    def three(k):
        return g.at[k, 0:3, 0]

    def three_half(k):
        return g.at[k, 0:3, 0, :, 0:384]

    def got(ref, ssem, rsem):
        remote(ref, ref, ssem, rsem, r, f).wait_recv()

    def sent(ref, ssem, rsem):
        remote(ref, ref, ssem, rsem, r, f).wait_send()

    def first(k):
        got(three(k), z_s.at[k], z_r.at[k])
        for d in (1, 2, 3):
            p = piece(k, d, r)
            remote(p, p, x_s.at[k], x_r.at[k], r ^ 1, f).start()
            remote(p, p, y_s.at[k], y_r.at[k], r ^ 2, f).start()
        core(k, r)

    def second(k):
        got(three(k), x_s.at[k], x_r.at[k])
        for d in (1, 2, 3):
            h = half(k, d, r ^ 1, 0)
            remote(h, h, dy_s.at[k], dy_r.at[k], r ^ 2, f).start()
        core(k, r ^ 1)
        got(three(k), y_s.at[k], y_r.at[k])
        for d in (1, 2, 3):
            h = half(k, d, r ^ 2, 1)
            remote(h, h, dx_s.at[k], dx_r.at[k], r ^ 1, f).start()
        core(k, r ^ 2)

    def third(k):
        got(three_half(k), dy_s.at[k], dy_r.at[k])
        got(three_half(k), dx_s.at[k], dx_r.at[k])
        core(k, r ^ 3)

    def arrived(k):
        got(g.at[k, 0], own_s.at[k], own_r.at[k])
        got(g.at[k, 0:3], c_s.at[k], c_r.at[k])
        pltpu.make_async_copy(g.at[k, 0], g.at[k, 0], loc.at[k]).wait()

    issue(0)
    for d in range(1, 8):
        remote(ss, small8.at[f], sm_s.at[d - 1], sm_r.at[d - 1], r, f ^ d).start()
    own_row = pltpu.make_async_copy(ss, small8.at[f], ld.at[2])
    own_row.start()
    issue(1)
    issue(2)
    build_bias(seg, bias)
    for c in loads:
        c.wait()
    own_row.wait()
    for d in range(1, 8):
        remote(ss, small8.at[f ^ d], sm_s.at[d - 1], sm_r.at[d - 1], r, f).wait()
    sm = jnp.sum(small8[...].astype(F32), axis=0)
    small[...] = sm
    issue(3)

    t = 256

    def ln_tile(i, cc):
        rows = pl.ds(pl.multiple_of(i * t, t), t)
        x = pick_rows(flags[:, rows], a_v[rows, :], lat_v[rows, :])
        xh, _ = norm_stats(x)
        a_v[rows, :] = (xh * small[:, G1:G1 + D] + small[:, S1:S1 + D]).astype(BF16)
        return cc

    lax.fori_loop(0, n // t, ln_tile, 0)

    def step(i):
        for fn, lag in ((first, 0), (second, 1), (third, 2), (arrived, 3)):
            k = i - lag
            if isinstance(i, int):
                if 0 <= k < NCH:
                    fn(k)
            else:
                @pl.when(jnp.logical_and(k >= 0, k < NCH))
                def _(fn=fn, k=k):
                    fn(k)

    for i in range(6):
        step(i)
        if i < 4:
            issue(4 + 2 * i)
            issue(5 + 2 * i)
        if i >= 3:
            m = i - 3
            w = pltpu.make_async_copy(g.at[m], wq.at[m], ld.at[3])
            w.start()
            w.wait()

            def mm(j, cc, m=m):
                rows = pl.ds(pl.multiple_of(j * t, t), t)
                y = nn(a_v[rows, :], wq[m].reshape(D, D))
                if m == 0:
                    y = y + small[:, BQ:BQ + D]
                if m == 2:
                    y = y + small[:, BV:BV + D]
                qkv[m, rows, :] = y.astype(BF16)
                return cc

            lax.fori_loop(0, n // t, mm, 0)
    qout = pltpu.make_async_copy(qkv, qkv_h, ld.at[4])
    qout.start()

    def pair(p, cc):
        cols = pl.ds(pl.multiple_of(p * 128, 128), 128)
        qt = (qkv[0, :, cols] * 0.125).T
        vt = qkv[2, :, cols].T
        k = qkv[1, :, cols]
        lane = lax.broadcasted_iota(jnp.int32, k.shape, 1)
        zero = jnp.zeros_like(k)
        ks = [jnp.where(lane < 64, k, zero), jnp.where(lane < 64, zero, k)]
        for q in range(4):
            lo, size = span(q)
            outs = []
            for h in range(2):
                s = nn(ks[h][lo:lo + size], qt[:, q * TQ:(q + 1) * TQ]) + bias[q, 0:size, :]
                m = jnp.max(s, axis=0, keepdims=True)
                e = jnp.exp(s - m)
                l = jnp.sum(e, axis=0, keepdims=True)
                ot = nn(vt[h * 64:(h + 1) * 64, lo:lo + size], e.astype(BF16))
                outs.append(ot * (1.0 / l))
                lse[p, h:h + 1, q * TQ:(q + 1) * TQ] = m + jnp.log(l)
            o_v[q * TQ:(q + 1) * TQ, cols] = jnp.concatenate(outs, axis=0).T.astype(BF16)
            if q == 1:
                step(6 + 2 * p)
        step(7 + 2 * p)
        return cc

    lax.fori_loop(0, 6, pair, 0)
    oout = pltpu.make_async_copy(o_v, o_h, ld.at[5])
    oout.start()

    def drain(k, cc):
        sent(three(k), z_s.at[k], z_r.at[k])
        sent(three(k), x_s.at[k], x_r.at[k])
        sent(three(k), y_s.at[k], y_r.at[k])
        sent(three_half(k), dx_s.at[k], dx_r.at[k])
        sent(three_half(k), dy_s.at[k], dy_r.at[k])
        sent(g.at[k, 0], own_s.at[k], own_r.at[k])
        sent(g.at[k, 0:3], c_s.at[k], c_r.at[k])
        return cc

    lax.fori_loop(0, NCH, drain, 0)
    qout.wait()
    oout.wait()


def first_part(ws, row, tok, lat, flags, seg):
    dma = pltpu.SemaphoreType.DMA
    n = tok.shape[0]
    anyspec = pl.BlockSpec(memory_space=pl.ANY)
    vspec = pl.BlockSpec(memory_space=pltpu.VMEM)
    shards_ = [w.reshape(4, RQ, w.shape[1]) for w in ws]
    return pl.pallas_call(
        first_kernel,
        in_specs=[vspec] * 5 + [anyspec] * 2 + [vspec] * 2,
        out_specs=[anyspec] * 3 + [vspec] * 2,
        out_shape=[
            jax.ShapeDtypeStruct((NCH, 8, 4, RQ, D), BF16),
            jax.ShapeDtypeStruct((3, n, D), BF16),
            jax.ShapeDtypeStruct((n, D), BF16),
            jax.ShapeDtypeStruct((6, 2, n), F32),
            jax.ShapeDtypeStruct((1, NSMALL), F32),
        ],
        scratch_shapes=[
            pltpu.VMEM((8, 1, NSMALL), BF16),
            pltpu.VMEM((3, 8, 4, RQ, D), BF16),
            pltpu.VMEM((n, D), BF16),
            pltpu.VMEM((n, D), BF16),
            pltpu.VMEM((3, n, D), BF16),
            pltpu.VMEM((n, D), BF16),
            pltpu.VMEM((4, 768, TQ), F32),
        ] + [dma((NCH,))] * 14 + [dma((7,))] * 2 + [dma((NCH,)), dma((6,))],
        compiler_params=pltpu.CompilerParams(collective_id=1, has_side_effects=True, vmem_limit_bytes=VLIM),
        name="first_part",
    )(*shards_, row, tok, lat, flags, seg)


XB, DO, OO, CT_, HH, RH, GJ, DJ = range(8)
L1 = 6


def second_kernel(tok_h, lat_h, cot_h, o_h, qkv_h, g_h, flags, seg, small, lse,
                  out_h, gin_h, fin, gsm_out,
                  pool, tr, w, acc_o, acc_d, l1, snd, r1, r2e, r2o, r3, r4, dka, dva, ot, gsm, sbuf, srcv,
                  ld, wl, st, a_s, a_r, b_s, b_r, d_s, d_r, e_s, e_r, h_s, h_r, m_s, m_r):
    r = lax.axis_index("rep")
    f = lax.axis_index("fsdp")
    c, z, x, y = f & 1, f >> 1, r & 1, r >> 1
    n = tok_h.shape[0]
    loads = [pltpu.make_async_copy(s, pool.at[i], ld.at[i]) for i, s in ((XB, tok_h), (DJ, lat_h), (OO, o_h), (CT_, cot_h))]
    for cp in loads:
        cp.start()

    def wcopy(k, slot):
        return pltpu.make_async_copy(g_h.at[k], w.at[slot], wl.at[slot])

    wcopy(3, 8).start()
    for j in range(4):
        wcopy(4 + j, j).start()
        wcopy(8 + j, 4 + j).start()
    bar = pltpu.get_barrier_semaphore()
    for d in (1, 2, 4, 6):
        pl.semaphore_signal(bar, inc=1, device_id=(r, f ^ d), device_id_type=MESH)
    for d in (1, 2, 3):
        pl.semaphore_signal(bar, inc=1, device_id=(r ^ d, f), device_id_type=MESH)
    pl.semaphore_wait(bar, 7)
    gsm[...] = jnp.zeros_like(gsm)

    def xcols(v):
        return pl.ds(pl.multiple_of(v * 384, 128), 384)

    def num(kh, par):
        return 2 * kh + par

    def hop1(kh, par):
        k = num(kh, par)
        return remote(snd.at[par], r1.at[k], a_s.at[k], a_r.at[k], r, f ^ 1)

    def hop2(kh, par):
        k = num(kh, par)
        slot = lax.rem(k, L1)
        if par == 0:
            return remote(l1.at[slot, :, :, :, xcols(1 - x)], r2e.at[kh], b_s.at[k], b_r.at[k], r ^ 1, f)
        return remote(l1.at[slot, :, 1 - y], r2o.at[kh], b_s.at[k], b_r.at[k], r ^ 2, f)

    def hop3(kh, par):
        k = num(kh, par)
        if par == 0:
            return remote(r2e.at[kh, :, 1 - y], r3.at[k], d_s.at[k], d_r.at[k], r ^ 2, f)
        return remote(r2o.at[kh, :, :, xcols(1 - x)], r3.at[k], d_s.at[k], d_r.at[k], r ^ 1, f)

    def hop4(kh, par, d):
        k = num(kh, par)
        return remote(r3.at[k, z ^ d], r4.at[k, d - 1], e_s.at[k, d - 1], e_r.at[k, d - 1], r, f ^ (2 * d))

    def hop5(kh, par, d, far):
        k = num(kh, par)
        q = r ^ d if far else r
        ref = fin.at[k, q >> 1, q & 1]
        return remote(ref, ref, h_s.at[k, d - 1], h_r.at[k, d - 1], r ^ d, f)

    def go2(kh, par):
        k = num(kh, par)
        slot = lax.rem(k, L1)
        hop1(kh, par).wait()

        def add(i, cc):
            l1[slot, i] = (l1[slot, i].astype(F32) + r1[k, i].astype(F32)).astype(BF16)
            return cc

        lax.fori_loop(0, 4, add, 0)
        hop2(kh, par).start()

    def go3(kh, par):
        k = num(kh, par)
        slot = lax.rem(k, L1)
        hop2(kh, par).wait()

        def add(i, cc):
            if par == 0:
                r2e[kh, i] = (l1[slot, i, :, :, xcols(x)].astype(F32) + r2e[kh, i].astype(F32)).astype(BF16)
            else:
                r2o[kh, i] = (l1[slot, i, y].astype(F32) + r2o[kh, i].astype(F32)).astype(BF16)
            return cc

        lax.fori_loop(0, 4, add, 0)
        hop3(kh, par).start()

    def go4(kh, par):
        k = num(kh, par)
        hop3(kh, par).wait()

        def add(i, cc):
            own = r2e[kh, i, y] if par == 0 else r2o[kh, i, :, xcols(x)]
            r3[k, i] = (own.astype(F32) + r3[k, i].astype(F32)).astype(BF16)
            return cc

        lax.fori_loop(0, 4, add, 0)
        for d in (1, 2, 3):
            hop4(kh, par, d).start()

    def go5(kh, par):
        k = num(kh, par)
        total = r3[k, z].astype(F32)
        for d in (1, 2, 3):
            hop4(kh, par, d).wait()
            total = total + r4[k, d - 1].astype(F32)
        fin[k, y, x] = total.astype(BF16)
        for d in (1, 2, 3):
            hop5(kh, par, d, False).start()

    def go6(kh, par):
        for d in (1, 2, 3):
            hop5(kh, par, d, False).wait_send()
            hop5(kh, par, d, True).wait_recv()

    stages = ((go2, 1), (go3, 3), (go4, 4), (go5, 5), (go6, 7))

    def step(kh, par):
        for fn, lag in stages:
            q = (par - lag) % 2
            shift = (par - lag - q) // 2
            kk = kh + shift
            if isinstance(kk, int):
                if 0 <= 2 * kk + q < NCH:
                    fn(kk, q)
            else:
                @pl.when(kk >= 0)
                def _(fn=fn, kk=kk, q=q):
                    fn(kk, q)

    def grad_chunk(ts, rhs, kh, par):
        k = num(kh, par)
        slot = lax.rem(k, L1)

        def tile(i, cc):
            cols = pl.ds(pl.multiple_of(i * 256, 256), 256)
            b = rhs(i)
            snd[par, :, :, :, cols] = nn(tr[ts, 1].reshape(384, n), b).astype(BF16).reshape(4, 2, 48, 256)
            l1[slot, :, :, :, cols] = nn(tr[ts, 0].reshape(384, n), b).astype(BF16).reshape(4, 2, 48, 256)
            return cc

        lax.fori_loop(0, 3, tile, 0)
        hop1(kh, par).start()

    def put_t(ts, val, cols):
        for o in range(8):
            tr[ts, (o & 1) ^ c, o >> 1, :, cols] = val[o * 96:(o + 1) * 96]

    def addsum(at, v):
        gsm[:, at:at + v.shape[1]] += jnp.sum(v, axis=0, keepdims=True)

    t = 256
    for cp in loads:
        cp.wait()
    wcopy(3, 8).wait()

    def head(i, cc):
        rows = pl.ds(pl.multiple_of(i * t, t), t)
        xv = pick_rows(flags[:, rows], pool[XB, rows, :], pool[DJ, rows, :])
        pool[XB, rows, :] = xv.astype(BF16)
        rv = xv + nt(pool[OO, rows, :], w[8]) + small[:, BO:BO + D]
        rh, rs = norm_stats(rv)
        ot[rows, :] = jnp.broadcast_to(rs, (t, 128))
        pool[RH, rows, :] = rh.astype(BF16)
        h = (rh * small[:, G2:G2 + D] + small[:, S2:S2 + D]).astype(BF16)
        pool[HH, rows, :] = h
        put_t(1, h.T, rows)
        acc_o[rows, :] = rv + small[:, BP:BP + D]
        acc_d[rows, :] = jnp.zeros((t, D), F32)
        cv = pool[CT_, rows, :]
        put_t(0, cv.T, rows)
        addsum(BP, cv.astype(F32))
        return cc

    lax.fori_loop(0, n // t, head, 0)

    def ff_tile(j, cc):
        wcopy(4, j).wait()
        wcopy(8, 4 + j).wait()

        def body(i, cc2):
            rows = pl.ds(pl.multiple_of(i * t, t), t)
            bf = pl.ds(pl.multiple_of(BF + j * D, 128), D)
            fv = nn(pool[HH, rows, :], w[j]) + small[:, bf]
            u = nn(pool[CT_, rows, :], w[4 + j])
            f2 = fv * fv
            th = jnp.tanh(fv * (C0 + (C0 * C1) * f2))
            hp = 0.5 + 0.5 * th
            gv = fv * hp
            gp = hp + (gv * (2.0 - 2.0 * hp)) * (C0 + (3.0 * C0 * C1) * f2)
            gb = gv.astype(BF16)
            df = (u * gp).astype(BF16)
            pool[GJ, rows, :] = gb
            pool[DJ, rows, :] = df
            gsm[:, bf] += jnp.sum(df.astype(F32), axis=0, keepdims=True)
            acc_o[rows, :] += nt(gb, w[4 + j])
            acc_d[rows, :] += nt(df, w[j])
            return cc2

        lax.fori_loop(0, n // t, body, 0)
        grad_chunk(0, lambda i: pool[GJ, :, pl.ds(pl.multiple_of(i * 256, 256), 256)], j, 0)
        step(j, 0)
        grad_chunk(1, lambda i: pool[DJ, :, pl.ds(pl.multiple_of(i * 256, 256), 256)], j, 1)
        step(j, 1)
        return cc

    lax.fori_loop(0, 4, ff_tile, 0)
    for i in range(3):
        wcopy(i, i).start()

    def tail(i, cc):
        rows = pl.ds(pl.multiple_of(i * t, t), t)
        pool[GJ, rows, :] = acc_o[rows, :].astype(BF16)
        dh = acc_d[rows, :]
        rh = pool[RH, rows, :].astype(F32)
        addsum(G2, dh * rh)
        addsum(S2, dh)
        e = dh * small[:, G2:G2 + D]
        dr = pool[CT_, rows, :].astype(F32) + ot[rows, 0:1] * (
            e - jnp.mean(e, axis=-1, keepdims=True) - rh * jnp.mean(e * rh, axis=-1, keepdims=True))
        acc_d[rows, :] = dr
        dy = dr.astype(BF16)
        addsum(BO, dy.astype(F32))
        put_t(2, dy.T, rows)
        pool[DO, rows, :] = nn(dy, w[8]).astype(BF16)
        return cc

    lax.fori_loop(0, n // t, tail, 0)
    oout = pltpu.make_async_copy(pool.at[GJ], out_h, st.at[0])
    oout.start()
    grad_chunk(2, lambda i: pool[OO, :, pl.ds(pl.multiple_of(i * 256, 256), 256)], 4, 0)
    step(4, 0)
    qload = pltpu.make_async_copy(qkv_h, pool.at[pl.ds(OO, 3)], ld.at[0])
    qload.start()

    for q in range(4):
        lo, size = span(q)
        st_row = doc_starts(seg[...])
        for b in range(size // TQ):
            jj = lax.broadcasted_iota(jnp.int32, (TQ, TQ), 0) + (lo + b * TQ)
            ii = lax.broadcasted_iota(jnp.int32, (TQ, TQ), 1) + q * TQ
            ok = jnp.logical_and(jj >= st_row[:, q * TQ:(q + 1) * TQ], jj <= ii)
            acc_o[q * TQ:(q + 1) * TQ, b * TQ:(b + 1) * TQ] = jnp.where(ok, 0.0, NEG)

    def xhat(rows):
        xh, rs = norm_stats(pool[XB, rows, :].astype(F32))
        return xh, rs

    def a_tile(i, cc):
        rows = pl.ds(pl.multiple_of(i * t, t), t)
        xh, _ = xhat(rows)
        put_t(0, (xh * small[:, G1:G1 + D] + small[:, S1:S1 + D]).astype(BF16).T, rows)
        return cc

    lax.fori_loop(0, n // t, a_tile, 0)
    qload.wait()
    oout.wait()

    def pair(p, cc):
        cols = pl.ds(pl.multiple_of(p * 128, 128), 128)
        q8 = pool[OO, :, cols] * 0.125
        qt = q8.T
        k = pool[OO + 1, :, cols]
        kt = k.T
        v = pool[OO + 2, :, cols]
        dv = pool[DO, :, cols]
        dt = dv.T
        lane = lax.broadcasted_iota(jnp.int32, k.shape, 1)
        zero = jnp.zeros_like(k)
        ks = [jnp.where(lane < 64, k, zero), jnp.where(lane < 64, zero, k)]
        vs = [jnp.where(lane < 64, v, zero), jnp.where(lane < 64, zero, v)]
        dka[...] = jnp.zeros_like(dka)
        dva[...] = jnp.zeros_like(dva)
        for q in range(4):
            lo, size = span(q)
            tq = slice(q * TQ, (q + 1) * TQ)
            bias = jnp.concatenate([acc_o[tq, b * TQ:(b + 1) * TQ] for b in range(size // TQ)], axis=0)
            dqs, dks, dvs = [], [], []
            for h in range(2):
                s = nn(ks[h][lo:lo + size], qt[:, tq]) + bias
                pr = jnp.exp(s - lse[p, h:h + 1, tq])
                dp = nn(vs[h][lo:lo + size], dt[:, tq])
                dd = jnp.sum(dp * pr, axis=0, keepdims=True)
                ds = (pr * (dp - dd)).astype(BF16)
                dvs.append(nn(pr.astype(BF16), dv[tq, :]))
                dks.append(nn(ds, q8[tq, :]))
                dqs.append(nn(kt[h * 64:(h + 1) * 64, lo:lo + size], ds))
            lane2 = lax.broadcasted_iota(jnp.int32, (size, 128), 1)
            dka[lo:lo + size, :] += jnp.where(lane2 < 64, dks[0], dks[1])
            dva[lo:lo + size, :] += jnp.where(lane2 < 64, dvs[0], dvs[1])
            pool[RH, tq, cols] = (jnp.concatenate(dqs, axis=0).T * 0.125).astype(BF16)
        pool[RH + 1, :, cols] = dka[...].astype(BF16)
        pool[RH + 2, :, cols] = dva[...].astype(BF16)
        return cc

    for m in range(3):
        lax.fori_loop(2 * m, 2 * m + 2, pair, 0)
        kh, par = (9 + m) // 2, (9 + m) % 2
        grad_chunk(0, lambda i, m=m: pool[RH + i, :, m * 256:(m + 1) * 256], kh, par)
        step(kh, par)

    for i in range(3):
        wcopy(i, i).wait()

    def last_tile(i, cc):
        rows = pl.ds(pl.multiple_of(i * t, t), t)
        xh, rs = xhat(rows)
        ds_ = [pool[RH + b, rows, :] for b in range(3)]
        da = nt(ds_[0], w[0]) + nt(ds_[1], w[1]) + nt(ds_[2], w[2])
        addsum(G1, da * xh)
        addsum(S1, da)
        addsum(BQ, ds_[0].astype(F32))
        addsum(BV, ds_[2].astype(F32))
        e = da * small[:, G1:G1 + D]
        acc_d[rows, :] += rs * (e - jnp.mean(e, axis=-1, keepdims=True) - xh * jnp.mean(e * xh, axis=-1, keepdims=True))
        pltpu.make_async_copy(acc_d.at[rows, :], gin_h.at[rows, :], st.at[i + 1]).start()
        return cc

    lax.fori_loop(0, 2, last_tile, 0)
    step(6, 0)
    lax.fori_loop(2, 4, last_tile, 0)
    step(6, 1)

    partners = ((r, f ^ 1), (r ^ 1, f), (r ^ 2, f), (r, f ^ 2), (r, f ^ 4))

    def small_hop(i):
        return remote(sbuf.at[i], srcv.at[i], m_s.at[i], m_r.at[i], *partners[i])

    sbuf[0] = gsm[...]
    small_hop(0).start()
    for i in range(5):
        small_hop(i).wait()
        v = sbuf[i] + srcv[i]
        if i < 4:
            sbuf[i + 1] = v
            small_hop(i + 1).start()
        else:
            gsm_out[...] = v
        step(7 + i // 2, i % 2)
    for i in range(4):
        rows = pl.ds(i * t, t)
        pltpu.make_async_copy(acc_d.at[rows, :], gin_h.at[rows, :], st.at[i + 1]).wait()


def second_part(tok, lat, cot, o, qkv, g, flags, seg, small, lse):
    dma = pltpu.SemaphoreType.DMA
    n = tok.shape[0]
    anyspec = pl.BlockSpec(memory_space=pl.ANY)
    vspec = pl.BlockSpec(memory_space=pltpu.VMEM)
    return pl.pallas_call(
        second_kernel,
        in_specs=[anyspec] * 6 + [vspec] * 4,
        out_specs=[anyspec] * 2 + [vspec] * 2,
        out_shape=[
            jax.ShapeDtypeStruct((n, D), BF16),
            jax.ShapeDtypeStruct((n, D), F32),
            jax.ShapeDtypeStruct((NCH, 2, 2, 48, 384), BF16),
            jax.ShapeDtypeStruct((1, NSMALL), F32),
        ],
        scratch_shapes=[
            pltpu.VMEM((8, n, D), BF16),
            pltpu.VMEM((3, 2, 4, 96, n), BF16),
            pltpu.VMEM((9, D, D), BF16),
            pltpu.VMEM((n, D), F32),
            pltpu.VMEM((n, D), F32),
            pltpu.VMEM((L1, 4, 2, 48, D), BF16),
            pltpu.VMEM((2, 4, 2, 48, D), BF16),
            pltpu.VMEM((NCH, 4, 2, 48, D), BF16),
            pltpu.VMEM((6, 4, 2, 48, 384), BF16),
            pltpu.VMEM((6, 4, 48, D), BF16),
            pltpu.VMEM((NCH, 4, 48, 384), BF16),
            pltpu.VMEM((NCH, 3, 48, 384), BF16),
            pltpu.VMEM((n, 128), F32),
            pltpu.VMEM((n, 128), F32),
            pltpu.VMEM((n, 128), F32),
            pltpu.VMEM((1, NSMALL), F32),
            pltpu.VMEM((5, 1, NSMALL), F32),
            pltpu.VMEM((5, 1, NSMALL), F32),
            dma((8,)), dma((9,)), dma((5,)), dma((NCH,)), dma((NCH,)), dma((NCH,)), dma((NCH,)), dma((NCH,)), dma((NCH,)),
            dma((NCH, 3)), dma((NCH, 3)), dma((NCH, 3)), dma((NCH, 3)), dma((5,)), dma((5,)),
        ],
        compiler_params=pltpu.CompilerParams(collective_id=2, has_side_effects=True, vmem_limit_bytes=61 << 20),
        name="second_part",
    )(tok, lat, cot, o, qkv, g, flags, seg, small, lse)


def finish_kernel(fin, gwq, gwo, gwf, gwp):
    for xx in range(2):
        for j in range(4):
            cols = slice(j * D + xx * 384, j * D + (xx + 1) * 384)
            v = jnp.concatenate([fin[2 * j, 0, xx], fin[2 * j, 1, xx]], axis=0).astype(F32)
            gwp[cols, :] = v.T
            for yy in range(2):
                gwf[yy * 48:(yy + 1) * 48, cols] = fin[2 * j + 1, yy, xx].astype(F32)
        v = jnp.concatenate([fin[8, 0, xx], fin[8, 1, xx]], axis=0).astype(F32)
        gwo[xx * 384:(xx + 1) * 384, :] = v.T
    for m in range(3):
        for yy in range(2):
            v = jnp.concatenate([fin[9 + m, yy, 0], fin[9 + m, yy, 1]], axis=1).astype(F32)
            for b in range(3):
                gwq[yy * 48:(yy + 1) * 48, b * D + m * 256:b * D + (m + 1) * 256] = v[:, b * 256:(b + 1) * 256]


def finish(fin):
    vspec = pl.BlockSpec(memory_space=pltpu.VMEM)
    return pl.pallas_call(
        finish_kernel,
        in_specs=[vspec],
        out_specs=[vspec] * 4,
        out_shape=[
            jax.ShapeDtypeStruct((96, 3 * D), F32),
            jax.ShapeDtypeStruct((D, 96), F32),
            jax.ShapeDtypeStruct((96, FF), F32),
            jax.ShapeDtypeStruct((FF, 96), F32),
        ],
        compiler_params=pltpu.CompilerParams(vmem_limit_bytes=VLIM),
        name="finish",
    )(fin)


def own_slots(v, nf, f):
    m = v.shape[0]
    wide = jnp.broadcast_to(v[None, :], (nf, m))
    mine = lax.broadcasted_iota(jnp.int32, (nf, m), 0) == f
    return jnp.where(mine, wide, jnp.zeros_like(wide)).reshape(-1)


def shards(fast, tokens, latent, segment_ids, latent_flags, norm1_gain, norm1_shift, w_qkv, b_qv, w_out, b_out,
           norm2_gain, norm2_shift, w_fc, b_fc, w_proj, b_proj, cotangent):
    nf = lax.axis_size("fsdp")
    f = lax.axis_index("fsdp")
    vectors = (norm1_gain, norm1_shift, b_qv, b_out, norm2_gain, norm2_shift, b_fc, b_proj)
    row = jnp.concatenate([own_slots(v, nf, f) for v in vectors]).reshape(1, NSMALL)
    ws = (w_qkv, w_out.T, w_fc, w_proj.T)

    def mine(total, at, v):
        m = v.shape[0]
        return lax.dynamic_slice(total[0], (at + f * m,), (m,))

    if fast:
        g, qkv, o, lse, small = first_part(ws, row, tokens, latent, latent_flags, segment_ids)
        out, gin, fin, gsm = second_part(tokens, latent, cotangent, o, qkv, g.reshape(NCH, D, D), latent_flags,
                                         segment_ids, small, lse)
        tq, to, tf, tp = finish(fin)
    else:
        wq, wo, wf, wp = [lax.all_gather(w, "fsdp", axis=0, tiled=True) for w in ws]
        small8 = lax.all_gather(row, "fsdp", axis=0, tiled=True)
        qkv, a_t, small = ln_qkv(tokens, latent, latent_flags, small8, wq)
        o, lse = attn_fwd(segment_ids, qkv)
        out, dr, do, gffn, gsm = ffn(tokens, latent, latent_flags, small, o, cotangent, wo, wf, wp)
        dqkv = attn_bwd(segment_ids, qkv, do, lse)
        gin, gq, gsm = last(tokens, latent, latent_flags, small, gsm, dr, dqkv, a_t, wq)

        def scatter(v):
            part = lax.psum_scatter(v, "fsdp", scatter_dimension=0, tiled=True)
            return lax.psum(part, "rep")

        tq, tp, tf, to = [scatter(v) for v in (gq, gffn[:, :FF], gffn[:, FF:2 * FF], gffn[:, 2 * FF:])]
        tq, to, tf, tp = tq.astype(F32), to.astype(F32).T, tf.astype(F32), tp.astype(F32).T
        gsm = lax.psum(gsm, ("rep", "fsdp"))
    v = [mine(gsm, at, v) for at, v in zip((G1, S1, BQ, BO, G2, S2, BF, BP), vectors)]
    return (out, gin, v[0], v[1], tq, v[2], to, v[3], v[4], v[5], tf, v[6], tp, v[7])


def solution(mesh):
    fast = mesh.shape["rep"] == 4 and mesh.shape["fsdp"] == 8
    both = P(("rep", "fsdp"), None)
    one, row, col = P("fsdp"), P("fsdp", None), P(None, "fsdp")
    return jax.shard_map(
        partial(shards, fast),
        mesh=mesh,
        in_specs=(both, both, both, both, one, one, row, one, col, one, one, one, row, one, col, one, both),
        out_specs=(both, both, one, one, row, one, col, one, one, one, row, one, col, one),
        check_vma=False,
    )
```

```python
from functools import partial

import jax
import jax.numpy as jnp
from jax import lax
from jax.experimental import pallas as pl
from jax.experimental.pallas import tpu as pltpu
from jax.sharding import PartitionSpec as P

D = 768
FF = 3072
NSMALL = 9216
NFFN = 6912
EPS = 1e-05
NEG = -1e30
G1, S1, BQ, BV, BO, G2, S2, BF, BP = 0, 768, 1536, 2304, 3072, 3840, 4608, 5376, 8448
F32 = jnp.float32
BF16 = jnp.bfloat16
VLIM = 60 << 20


def nn(a, b):
    return jnp.dot(a, b, preferred_element_type=F32)


def nt(a, b):
    return lax.dot_general(a, b, (((1,), (1,)), ((), ())), preferred_element_type=F32)


def norm_stats(x):
    mean = jnp.mean(x, axis=-1, keepdims=True)
    center = x - mean
    var = jnp.mean(center * center, axis=-1, keepdims=True)
    rs = lax.rsqrt(var + EPS)
    return center * rs, rs


def pick_rows(flags_row, tok, lat):
    t = flags_row.shape[1]
    col = jnp.broadcast_to(flags_row.astype(F32), (128, t)).T
    wide = jnp.concatenate([col] * (D // 128), axis=1)
    return jnp.where(wide > 0.5, lat.astype(F32), tok.astype(F32))


def ln_qkv_kernel(tok, lat, flags, small8, wq, qkv, a_t, small):
    sm = jnp.sum(small8[...].astype(F32), axis=0, keepdims=True)

    @pl.when(pl.program_id(0) == 0)
    def _():
        small[...] = sm

    x = pick_rows(flags[...], tok[...], lat[...])
    xh, _ = norm_stats(x)
    a = (xh * sm[:, G1:G1 + D] + sm[:, S1:S1 + D]).astype(BF16)
    a_t[...] = a.T
    for i in range(3):
        y = nn(a, wq[:, i * D:(i + 1) * D])
        if i == 0:
            y = y + sm[:, BQ:BQ + D]
        if i == 2:
            y = y + sm[:, BV:BV + D]
        qkv[i] = y.astype(BF16)


def ln_qkv(tok, lat, flags, small8, wq):
    n = tok.shape[0]
    t = 256
    return pl.pallas_call(
        ln_qkv_kernel,
        grid=(n // t,),
        in_specs=[
            pl.BlockSpec((t, D), lambda i: (i, 0)),
            pl.BlockSpec((t, D), lambda i: (i, 0)),
            pl.BlockSpec((1, t), lambda i: (0, i)),
            pl.BlockSpec(small8.shape, lambda i: (0, 0)),
            pl.BlockSpec((D, 3 * D), lambda i: (0, 0)),
        ],
        out_specs=[
            pl.BlockSpec((3, t, D), lambda i: (0, i, 0)),
            pl.BlockSpec((D, t), lambda i: (0, i)),
            pl.BlockSpec((1, NSMALL), lambda i: (0, 0)),
        ],
        out_shape=[
            jax.ShapeDtypeStruct((3, n, D), BF16),
            jax.ShapeDtypeStruct((D, n), BF16),
            jax.ShapeDtypeStruct((1, NSMALL), F32),
        ],
        compiler_params=pltpu.CompilerParams(vmem_limit_bytes=VLIM),
        name="ln_qkv",
    )(tok, lat, flags, small8, wq)


TQ = 256


def span(t):
    lo = max(0, t - 2)
    return lo * TQ, (t + 1 - lo) * TQ


def doc_starts(seg):
    st = jnp.zeros(seg.shape, jnp.int32)
    for s in range(1, 8):
        cnt = jnp.sum((seg < s).astype(jnp.int32), axis=1, keepdims=True)
        st = jnp.where(seg == s, cnt, st)
    return st


def build_bias(seg_ref, bias):
    st = doc_starts(seg_ref[...])
    for t in range(4):
        lo, size = span(t)
        j = lax.broadcasted_iota(jnp.int32, (size, TQ), 0) + lo
        i = lax.broadcasted_iota(jnp.int32, (size, TQ), 1) + t * TQ
        ok = jnp.logical_and(j >= st[:, t * TQ:(t + 1) * TQ], j <= i)
        bias[t, 0:size, :] = jnp.where(ok, 0.0, NEG)


def attn_fwd_kernel(seg_ref, qkv, o, lse, bias):
    @pl.when(pl.program_id(0) == 0)
    def _():
        build_bias(seg_ref, bias)

    qt = (qkv[0] * 0.125).T
    vt = qkv[2].T
    k = qkv[1]
    lane = lax.broadcasted_iota(jnp.int32, k.shape, 1)
    zero = jnp.zeros_like(k)
    ks = [jnp.where(lane < 64, k, zero), jnp.where(lane < 64, zero, k)]
    for t in range(4):
        lo, size = span(t)
        outs = []
        for h in range(2):
            s = nn(ks[h][lo:lo + size], qt[:, t * TQ:(t + 1) * TQ]) + bias[t, 0:size, :]
            m = jnp.max(s, axis=0, keepdims=True)
            p = jnp.exp(s - m)
            l = jnp.sum(p, axis=0, keepdims=True)
            ot = nn(vt[h * 64:(h + 1) * 64, lo:lo + size], p.astype(BF16))
            outs.append(ot * (1.0 / l))
            lse[0, h:h + 1, t * TQ:(t + 1) * TQ] = m + jnp.log(l)
        o[t * TQ:(t + 1) * TQ, :] = jnp.concatenate(outs, axis=0).T.astype(BF16)


def attn_fwd(seg, qkv):
    n = qkv.shape[1]
    return pl.pallas_call(
        attn_fwd_kernel,
        grid=(6,),
        in_specs=[
            pl.BlockSpec((1, n), lambda p: (0, 0)),
            pl.BlockSpec((3, n, 128), lambda p: (0, 0, p)),
        ],
        out_specs=[
            pl.BlockSpec((n, 128), lambda p: (0, p)),
            pl.BlockSpec((1, 2, n), lambda p: (p, 0, 0)),
        ],
        out_shape=[
            jax.ShapeDtypeStruct((n, D), BF16),
            jax.ShapeDtypeStruct((6, 2, n), F32),
        ],
        scratch_shapes=[pltpu.VMEM((4, 768, TQ), F32)],
        compiler_params=pltpu.CompilerParams(vmem_limit_bytes=VLIM),
        name="attn_fwd",
    )(seg, qkv)


C0 = 0.7978845608028654
C1 = 0.044715
TR = 512
TC = 512


def ffn_kernel(tok, lat, flags, small, o_h, cot_h, wo_h, wf_h, wp_h,
               out_h, dr_h, do_h, gffn_h, gsmall,
               o, cot, wo, wf, wp, gs, dfs, ct, ht, dyt, xs, rs_s, outs, dos, gwo, gwf, gwp, isem, osem):
    n = o.shape[0]
    ins = [pltpu.make_async_copy(a, b, isem.at[i]) for i, (a, b) in enumerate(
        [(o_h, o), (wo_h, wo), (cot_h, cot), (wf_h, wf), (wp_h, wp)])]
    for c in ins:
        c.start()
    gsmall[...] = jnp.zeros_like(gsmall)
    ins[0].wait()
    ins[1].wait()
    ins[2].wait()
    ins[3].wait()
    ins[4].wait()

    def row_tile(i, carry):
        r0 = pl.multiple_of(i * TR, TR)
        rows = pl.ds(r0, TR)
        x = pick_rows(flags[:, rows], tok[rows, :], lat[rows, :])
        r = x + nt(o[rows, :], wo[...]) + small[:, BO:BO + D]
        rh, rs = norm_stats(r)
        h = (rh * small[:, G2:G2 + D] + small[:, S2:S2 + D]).astype(BF16)
        ht[:, rows] = h.T
        c_t = cot[rows, :]
        ct[:, rows] = c_t.T
        gsmall[:, BP:BP + D] += jnp.sum(c_t.astype(F32), axis=0, keepdims=True)

        xs[...] = jnp.zeros_like(xs)
        rs_s[...] = jnp.zeros_like(rs_s)

        def col_tile(j, cc):
            c0 = pl.multiple_of(j * TC, TC)
            cols = pl.ds(c0, TC)
            f = nn(h, wf[:, cols]) + small[:, pl.ds(pl.multiple_of(BF + c0, 128), TC)]
            u = nn(c_t, wp[:, cols])
            f2 = f * f
            th = jnp.tanh(f * (C0 + (C0 * C1) * f2))
            hp = 0.5 + 0.5 * th
            g = f * hp
            gp = hp + (g * (2.0 - 2.0 * hp)) * (C0 + (3.0 * C0 * C1) * f2)
            gb = g.astype(BF16)
            df = (u * gp).astype(BF16)
            gs[rows, cols] = gb
            dfs[rows, cols] = df
            sl = pl.ds(pl.multiple_of(BF + c0, 128), TC)
            gsmall[:, sl] += jnp.sum(df.astype(F32), axis=0, keepdims=True)
            xs[...] += nt(gb, wp[:, cols])
            rs_s[...] += nt(df, wf[:, cols])
            return cc

        lax.fori_loop(0, FF // TC, col_tile, 0)
        outs[rows, :] = (r + xs[...] + small[:, BP:BP + D]).astype(BF16)
        dh = rs_s[...]
        gsmall[:, G2:G2 + D] += jnp.sum(dh * rh, axis=0, keepdims=True)
        gsmall[:, S2:S2 + D] += jnp.sum(dh, axis=0, keepdims=True)
        e = dh * small[:, G2:G2 + D]
        dr = c_t.astype(F32) + rs * (e - jnp.mean(e, axis=-1, keepdims=True) - rh * jnp.mean(e * rh, axis=-1, keepdims=True))
        dy = dr.astype(BF16)
        gsmall[:, BO:BO + D] += jnp.sum(dy.astype(F32), axis=0, keepdims=True)
        dyt[:, rows] = dy.T
        xs[...] = dr
        cp = pltpu.make_async_copy(xs, dr_h.at[rows, :], isem.at[0])
        cp.start()
        dos[rows, :] = nn(dy, wo[...]).astype(BF16)
        cp.wait()
        return carry

    lax.fori_loop(0, n // TR, row_tile, 0)
    c1 = pltpu.make_async_copy(outs, out_h, osem.at[0])
    c1.start()
    c2 = pltpu.make_async_copy(dos, do_h, osem.at[1])
    c2.start()

    def grad_tile(j, cc):
        cols = pl.ds(pl.multiple_of(j * TC, TC), TC)
        gwp[:, cols] = nn(ct[...], gs[:, cols]).astype(BF16)
        gwf[:, cols] = nn(ht[...], dfs[:, cols]).astype(BF16)
        return cc

    lax.fori_loop(0, FF // TC, grad_tile, 0)
    c3 = pltpu.make_async_copy(gwp, gffn_h.at[:, 0:FF], osem.at[2])
    c3.start()
    c4 = pltpu.make_async_copy(gwf, gffn_h.at[:, FF:2 * FF], osem.at[3])
    c4.start()

    def gwo_tile(j, cc):
        cols = pl.ds(pl.multiple_of(j * 256, 256), 256)
        gwo[:, cols] = nn(dyt[...], o[:, cols]).astype(BF16)
        return cc

    lax.fori_loop(0, D // 256, gwo_tile, 0)
    c5 = pltpu.make_async_copy(gwo, gffn_h.at[:, 2 * FF:], osem.at[4])
    c5.start()
    for c in (c1, c2, c3, c4, c5):
        c.wait()


def ffn(tok, lat, flags, small, o, cot, wo, wf, wp):
    n = tok.shape[0]
    anyspec = pl.BlockSpec(memory_space=pl.ANY)
    vspec = pl.BlockSpec(memory_space=pltpu.VMEM)
    return pl.pallas_call(
        ffn_kernel,
        in_specs=[vspec] * 4 + [anyspec] * 5,
        out_specs=[anyspec] * 4 + [vspec],
        out_shape=[
            jax.ShapeDtypeStruct((n, D), BF16),
            jax.ShapeDtypeStruct((n, D), F32),
            jax.ShapeDtypeStruct((n, D), BF16),
            jax.ShapeDtypeStruct((D, NFFN), BF16),
            jax.ShapeDtypeStruct((1, NSMALL), F32),
        ],
        scratch_shapes=[
            pltpu.VMEM((n, D), BF16),
            pltpu.VMEM((n, D), BF16),
            pltpu.VMEM((D, D), BF16),
            pltpu.VMEM((D, FF), BF16),
            pltpu.VMEM((D, FF), BF16),
            pltpu.VMEM((n, FF), BF16),
            pltpu.VMEM((n, FF), BF16),
            pltpu.VMEM((D, n), BF16),
            pltpu.VMEM((D, n), BF16),
            pltpu.VMEM((D, n), BF16),
            pltpu.VMEM((TR, D), F32),
            pltpu.VMEM((TR, D), F32),
            pltpu.VMEM((n, D), BF16),
            pltpu.VMEM((n, D), BF16),
            pltpu.VMEM((D, D), BF16),
            pltpu.VMEM((D, FF), BF16),
            pltpu.VMEM((D, FF), BF16),
            pltpu.SemaphoreType.DMA((5,)),
            pltpu.SemaphoreType.DMA((5,)),
        ],
        compiler_params=pltpu.CompilerParams(vmem_limit_bytes=VLIM),
        name="ffn",
    )(tok, lat, flags, small, o, cot, wo, wf, wp)


def attn_bwd_kernel(seg_ref, qkv, do, lse, dqkv, bias, dk_acc, dv_acc):
    @pl.when(pl.program_id(0) == 0)
    def _():
        build_bias(seg_ref, bias)

    q8 = qkv[0] * 0.125
    qt = q8.T
    k = qkv[1]
    kt = k.T
    v = qkv[2]
    d = do[...]
    dt = d.T
    lane = lax.broadcasted_iota(jnp.int32, k.shape, 1)
    zero = jnp.zeros_like(k)
    ks = [jnp.where(lane < 64, k, zero), jnp.where(lane < 64, zero, k)]
    vs = [jnp.where(lane < 64, v, zero), jnp.where(lane < 64, zero, v)]
    dk_acc[...] = jnp.zeros_like(dk_acc)
    dv_acc[...] = jnp.zeros_like(dv_acc)
    for t in range(4):
        lo, size = span(t)
        tq = slice(t * TQ, (t + 1) * TQ)
        dqs, dks, dvs = [], [], []
        for h in range(2):
            s = nn(ks[h][lo:lo + size], qt[:, tq]) + bias[t, 0:size, :]
            p = jnp.exp(s - lse[0, h:h + 1, tq])
            dp = nn(vs[h][lo:lo + size], dt[:, tq])
            dd = jnp.sum(dp * p, axis=0, keepdims=True)
            ds = (p * (dp - dd)).astype(BF16)
            dvs.append(nn(p.astype(BF16), d[tq, :]))
            dks.append(nn(ds, q8[tq, :]))
            dqs.append(nn(kt[h * 64:(h + 1) * 64, lo:lo + size], ds))
        lane2 = lax.broadcasted_iota(jnp.int32, (size, 128), 1)
        dk_acc[lo:lo + size, :] += jnp.where(lane2 < 64, dks[0], dks[1])
        dv_acc[lo:lo + size, :] += jnp.where(lane2 < 64, dvs[0], dvs[1])
        dqkv[0, tq, :] = (jnp.concatenate(dqs, axis=0).T * 0.125).astype(BF16)
    dqkv[1] = dk_acc[...].astype(BF16)
    dqkv[2] = dv_acc[...].astype(BF16)


def attn_bwd(seg, qkv, do, lse):
    n = qkv.shape[1]
    return pl.pallas_call(
        attn_bwd_kernel,
        grid=(6,),
        in_specs=[
            pl.BlockSpec((1, n), lambda p: (0, 0)),
            pl.BlockSpec((3, n, 128), lambda p: (0, 0, p)),
            pl.BlockSpec((n, 128), lambda p: (0, p)),
            pl.BlockSpec((1, 2, n), lambda p: (p, 0, 0)),
        ],
        out_specs=pl.BlockSpec((3, n, 128), lambda p: (0, 0, p)),
        out_shape=jax.ShapeDtypeStruct((3, n, D), BF16),
        scratch_shapes=[
            pltpu.VMEM((4, 768, TQ), F32),
            pltpu.VMEM((n, 128), F32),
            pltpu.VMEM((n, 128), F32),
        ],
        compiler_params=pltpu.CompilerParams(vmem_limit_bytes=VLIM),
        name="attn_bwd",
    )(seg, qkv, do, lse)


def last_body(tok, lat, flags, small, gsm_in, dr, dqkv, a_t, wq, gin, gwq, gsmall):
    i = pl.program_id(0)
    t = 256

    @pl.when(i == 0)
    def _():
        gsmall[...] = gsm_in[...]

    rows = pl.ds(pl.multiple_of(i * t, t), t)
    x = pick_rows(flags[:, rows], tok[rows, :], lat[rows, :])
    xh, rs = norm_stats(x)
    d0, d1, d2 = dqkv[0, rows, :], dqkv[1, rows, :], dqkv[2, rows, :]
    da = nt(d0, wq[:, 0:D]) + nt(d1, wq[:, D:2 * D]) + nt(d2, wq[:, 2 * D:3 * D])
    gsmall[:, G1:G1 + D] += jnp.sum(da * xh, axis=0, keepdims=True)
    gsmall[:, S1:S1 + D] += jnp.sum(da, axis=0, keepdims=True)
    gsmall[:, BQ:BQ + D] += jnp.sum(d0.astype(F32), axis=0, keepdims=True)
    gsmall[:, BV:BV + D] += jnp.sum(d2.astype(F32), axis=0, keepdims=True)
    e = da * small[:, G1:G1 + D]
    gin[...] = dr[...] + rs * (e - jnp.mean(e, axis=-1, keepdims=True) - xh * jnp.mean(e * xh, axis=-1, keepdims=True))
    ar = pl.ds(pl.multiple_of(i * 192, 192), 192)
    for c in range(3):
        gwq[:, c * D:(c + 1) * D] = nn(a_t[ar, :], dqkv[c]).astype(BF16)


def last(tok, lat, flags, small, gsm, dr, dqkv, a_t, wq):
    n = tok.shape[0]
    t = 256
    whole = lambda *s: pl.BlockSpec(s, lambda i: (0,) * len(s))
    return pl.pallas_call(
        last_body,
        grid=(n // t,),
        in_specs=[
            whole(n, D), whole(n, D), whole(1, n), whole(1, NSMALL), whole(1, NSMALL),
            pl.BlockSpec((t, D), lambda i: (i, 0)),
            whole(3, n, D), whole(D, n), whole(D, 3 * D),
        ],
        out_specs=[
            pl.BlockSpec((t, D), lambda i: (i, 0)),
            pl.BlockSpec((192, 3 * D), lambda i: (i, 0)),
            whole(1, NSMALL),
        ],
        out_shape=[
            jax.ShapeDtypeStruct((n, D), F32),
            jax.ShapeDtypeStruct((D, 3 * D), BF16),
            jax.ShapeDtypeStruct((1, NSMALL), F32),
        ],
        compiler_params=pltpu.CompilerParams(vmem_limit_bytes=VLIM),
        name="last",
    )(tok, lat, flags, small, gsm, dr, dqkv, a_t, wq)


MESH = pl.DeviceIdType.MESH
RQ = 24
NCH = 12
XB, DO, OO, CT_, HH, RH, GJ, DJ = range(8)
QS = (RH, GJ, DO)
L1 = 5
R1 = 5


def remote(a, b, ssem, rsem, rr, ff):
    return pltpu.make_async_remote_copy(src_ref=a, dst_ref=b, send_sem=ssem, recv_sem=rsem,
                                        device_id=(rr, ff), device_id_type=MESH)


def layer_kernel(sq, so, sf, sp, v0, v1, v2, v3, v4, v5, v6, v7, tok_h, lat_h, cot_h, flags, seg,
                 g, qkv_h, out_h, gin_h, fin, gsm_out,
                 ss, small8, small, lse, pool, tr, w, acc_o, acc_d, l1, snd, r1, r2e, r2o, r3, r4, dka, dva, gsm, sbuf, srcv,
                 z_s, z_r, x_s, x_r, y_s, y_r, dx_s, dx_r, dy_s, dy_r, c_s, c_r, own_s, own_r, sm_s, sm_r, loc,
                 ld, wl, st, a_s, a_r, b_s, b_r, d_s, d_r, e_s, e_r, h_s, h_r, m_s, m_r):
    r = lax.axis_index("rep")
    f = lax.axis_index("fsdp")
    c, z, x, y = f & 1, f >> 1, r & 1, r >> 1
    n = tok_h.shape[0]
    t = 256
    loads = [pltpu.make_async_copy(s, pool.at[i], ld.at[i]) for i, s in ((XB, tok_h), (DJ, lat_h), (CT_, cot_h))]
    for cp in loads:
        cp.start()
    pieces = []
    for v in (v0, v1, v2, v3, v4, v5, v6, v7):
        val = v[...].astype(F32)
        pieces += [jnp.where(f == d, val, 0.0) for d in range(8)]
    ss[...] = jnp.concatenate(pieces, axis=1).astype(BF16)
    bar = pltpu.get_barrier_semaphore()
    for d in range(1, 8):
        pl.semaphore_signal(bar, inc=1, device_id=(r, f ^ d), device_id_type=MESH)
    for d in (1, 2, 3):
        pl.semaphore_signal(bar, inc=1, device_id=(r ^ d, f), device_id_type=MESH)
    pl.semaphore_wait(bar, 10)

    sources = [(sq, 0), (sq, 1), (sq, 2), (so, 0)] + [p for i in range(4) for p in ((sf, i), (sp, i))]

    def rows_of(owner, q):
        return pl.ds(pl.multiple_of(owner * 96 + q * RQ, 8), RQ)

    def issue(k):
        ref, i = sources[k]
        cols = slice(i * D, (i + 1) * D)
        for d in (1, 2, 3):
            remote(ref.at[r, :, cols], g.at[k, rows_of(f, r)], z_s.at[k], z_r.at[k], r, f ^ (2 * d)).start()
        for q in range(4):
            remote(ref.at[q, :, cols], g.at[k, rows_of(f, q)], own_s.at[k], own_r.at[k], r, f ^ 1).start()
            pltpu.make_async_copy(ref.at[q, :, cols], g.at[k, rows_of(f, q)], loc.at[k]).start()

    def piece(k, d, q):
        return g.at[k, rows_of(f ^ (2 * d), q)]

    def half(k, d, q, h):
        return g.at[k, rows_of(f ^ (2 * d), q), h * 384:(h + 1) * 384]

    def core(k, q):
        for d in (1, 2, 3):
            remote(piece(k, d, q), piece(k, d, q), c_s.at[k], c_r.at[k], r, f ^ 1).start()

    def three(k):
        return g.at[k, 0:72]

    def three_half(k):
        return g.at[k, 0:72, 0:384]

    def got(ref, ssem, rsem):
        remote(ref, ref, ssem, rsem, r, f).wait_recv()

    def sent(ref, ssem, rsem):
        remote(ref, ref, ssem, rsem, r, f).wait_send()

    def first(k):
        got(three(k), z_s.at[k], z_r.at[k])
        for d in (1, 2, 3):
            p = piece(k, d, r)
            remote(p, p, x_s.at[k], x_r.at[k], r ^ 1, f).start()
            remote(p, p, y_s.at[k], y_r.at[k], r ^ 2, f).start()
        core(k, r)

    def second(k):
        got(three(k), x_s.at[k], x_r.at[k])
        for d in (1, 2, 3):
            h = half(k, d, r ^ 1, 0)
            remote(h, h, dy_s.at[k], dy_r.at[k], r ^ 2, f).start()
        core(k, r ^ 1)
        got(three(k), y_s.at[k], y_r.at[k])
        for d in (1, 2, 3):
            h = half(k, d, r ^ 2, 1)
            remote(h, h, dx_s.at[k], dx_r.at[k], r ^ 1, f).start()
        core(k, r ^ 2)

    def third(k):
        got(three_half(k), dy_s.at[k], dy_r.at[k])
        got(three_half(k), dx_s.at[k], dx_r.at[k])
        core(k, r ^ 3)

    def arrived(k):
        got(g.at[k, 0:96], own_s.at[k], own_r.at[k])
        got(g.at[k, 0:288], c_s.at[k], c_r.at[k])
        pltpu.make_async_copy(g.at[k, 0:96], g.at[k, 0:96], loc.at[k]).wait()

    def wcopy(k, slot):
        return pltpu.make_async_copy(g.at[k], w.at[slot], wl.at[slot])

    for d in range(1, 8):
        remote(ss, small8.at[f], sm_s.at[d - 1], sm_r.at[d - 1], r, f ^ d).start()
    own_row = pltpu.make_async_copy(ss, small8.at[f], ld.at[1])
    own_row.start()
    issue(0)

    def build_blocks():
        row = doc_starts(seg[...])
        for q in range(4):
            lo, size = span(q)
            for b in range(size // TQ):
                jj = lax.broadcasted_iota(jnp.int32, (TQ, TQ), 0) + (lo + b * TQ)
                ii = lax.broadcasted_iota(jnp.int32, (TQ, TQ), 1) + q * TQ
                ok = jnp.logical_and(jj >= row[:, q * TQ:(q + 1) * TQ], jj <= ii)
                acc_o[q * TQ:(q + 1) * TQ, b * TQ:(b + 1) * TQ] = jnp.where(ok, 0.0, NEG)

    def blocks(q):
        size = span(q)[1]
        return jnp.concatenate([acc_o[q * TQ:(q + 1) * TQ, b * TQ:(b + 1) * TQ] for b in range(size // TQ)], axis=0)

    build_blocks()
    gsm[...] = jnp.zeros_like(gsm)
    own_row.wait()
    for d in range(1, 8):
        remote(ss, small8.at[f ^ d], sm_s.at[d - 1], sm_r.at[d - 1], r, f).wait()
    small[...] = jnp.sum(small8[...].astype(F32), axis=0)
    issue(1)
    first(0)
    issue(2)
    for cp in loads:
        cp.wait()

    def ln_tile(i, cc):
        rows = pl.ds(pl.multiple_of(i * t, t), t)
        xv = pick_rows(flags[:, rows], pool[XB, rows, :], pool[DJ, rows, :])
        pool[XB, rows, :] = xv.astype(BF16)
        xh, _ = norm_stats(xv)
        pool[HH, rows, :] = (xh * small[:, G1:G1 + D] + small[:, S1:S1 + D]).astype(BF16)
        return cc

    def normalise(k):
        lax.fori_loop(2 * k, 2 * k + 2, ln_tile, 0)

    def project(m):
        wcopy(m, m).start()
        wcopy(m, m).wait()

        for j in range(n // 512):
            rows = slice(j * 512, (j + 1) * 512)
            v = nn(pool[HH, rows, :], w[m])
            if m == 0:
                v = v + small[:, BQ:BQ + D]
            if m == 2:
                v = v + small[:, BV:BV + D]
            pool[QS[m], rows, :] = v.astype(BF16)
        pltpu.make_async_copy(pool.at[QS[m]], qkv_h.at[m], st.at[m]).start()

    for fn, k in ((normalise, 0), (first, 1), (normalise, 1), (second, 0), (first, 2), (second, 1), (third, 0), (first, 3),
                  (second, 2), (third, 1), (arrived, 0), (project, 0), (first, 4), (third, 2), (arrived, 1), (project, 1),
                  (second, 3), (arrived, 2), (project, 2)):
        fn(k)
        if fn is first:
            issue(k + 2)

    def tick(i):
        for fn, k in ((first, 5 + i), (second, 4 + i), (third, 3 + i)):
            if k < NCH:
                fn(k)
                if fn is first and k + 2 < NCH:
                    issue(k + 2)

    def at_point(p):
        for i in range(1, 6, 2):
            @pl.when(p == i)
            def _(i=i):
                tick(i // 2)

    def by_head(v):
        lane = lax.broadcasted_iota(jnp.int32, v.shape, 1)
        zero = jnp.zeros_like(v)
        return jnp.where(lane < 64, v, zero), jnp.where(lane < 64, zero, v)

    def by_head_t(v):
        row = lax.broadcasted_iota(jnp.int32, v.shape, 0)
        zero = jnp.zeros_like(v)
        return jnp.where(row < 64, v, zero), jnp.where(row < 64, zero, v)

    def stack(two, q):
        lo, size = span(q)
        return jnp.concatenate([v[lo:lo + size] for v in two], axis=0)

    def beside(two, q):
        lo, size = span(q)
        return jnp.concatenate([v[:, lo:lo + size] for v in two], axis=1)

    def pair_fwd(p, cc):
        cols = pl.ds(pl.multiple_of(p * 128, 128), 128)
        qt = (pool[QS[0], :, cols] * 0.125).T
        vts = by_head_t(pool[QS[2], :, cols].T)
        ks = by_head(pool[QS[1], :, cols])

        def scores(q):
            return nn(stack(ks, q), qt[:, q * TQ:(q + 1) * TQ])

        def soft(q, s):
            size = span(q)[1]
            bias = blocks(q)
            es, inv = [], []
            for h in range(2):
                sh = s[h * size:(h + 1) * size] + bias
                m = jnp.max(sh, axis=0, keepdims=True)
                e = jnp.exp(sh - m)
                l = jnp.sum(e, axis=0, keepdims=True)
                lse[p, h:h + 1, q * TQ:(q + 1) * TQ] = m + jnp.log(l)
                es.append(e.astype(BF16))
                inv.append(1.0 / l)
            return jnp.concatenate(es, axis=0), inv

        def mix(q, e, inv):
            ot = nn(beside(vts, q), e)
            ot = jnp.concatenate([ot[0:64] * inv[0], ot[64:128] * inv[1]], axis=0)
            pool[OO, q * TQ:(q + 1) * TQ, cols] = ot.T.astype(BF16)

        s, before = scores(0), None
        for q in range(4):
            ahead = scores(q + 1) if q < 3 else None
            after = soft(q, s)
            if before is not None:
                mix(*before)
            before, s = (q,) + after, ahead
        mix(*before)
        at_point(p)
        return cc

    lax.fori_loop(0, 6, pair_fwd, 0)
    for m in range(3):
        pltpu.make_async_copy(pool.at[QS[m]], qkv_h.at[m], st.at[m]).wait()
    arrived(3)
    wcopy(3, 4).start()
    arrived(4)
    wcopy(4, 0).start()
    tick(3)
    arrived(5)
    wcopy(5, 1).start()

    def xcols(v):
        return pl.ds(pl.multiple_of(v * 384, 128), 384)

    def num(kh, par):
        return 2 * kh + par

    def hop1(kh, par):
        k = num(kh, par)
        return remote(snd.at[par], r1.at[lax.rem(k, R1)], a_s.at[k], a_r.at[k], r, f ^ 1)

    def hop2(kh, par):
        k = num(kh, par)
        slot = lax.rem(k, L1)
        if par == 0:
            return remote(l1.at[slot, :, :, :, xcols(1 - x)], r2e.at[kh], b_s.at[k], b_r.at[k], r ^ 1, f)
        return remote(l1.at[slot, :, 1 - y], r2o.at[kh], b_s.at[k], b_r.at[k], r ^ 2, f)

    def hop3(kh, par):
        k = num(kh, par)
        if par == 0:
            return remote(r2e.at[kh, :, 1 - y], r3.at[k], d_s.at[k], d_r.at[k], r ^ 2, f)
        return remote(r2o.at[kh, :, :, xcols(1 - x)], r3.at[k], d_s.at[k], d_r.at[k], r ^ 1, f)

    def hop4(kh, par, d):
        k = num(kh, par)
        return remote(r3.at[k, z ^ d], r4.at[k, d - 1], e_s.at[k, d - 1], e_r.at[k, d - 1], r, f ^ (2 * d))

    def hop5(kh, par, d, far):
        k = num(kh, par)
        q = r ^ d if far else r
        ref = fin.at[k, q >> 1, q & 1]
        return remote(ref, ref, h_s.at[k, d - 1], h_r.at[k, d - 1], r ^ d, f)

    def go2(kh, par):
        k = num(kh, par)
        slot = lax.rem(k, L1)
        hop1(kh, par).wait()

        def add(i, cc):
            l1[slot, i] = (l1[slot, i].astype(F32) + r1[lax.rem(k, R1), i].astype(F32)).astype(BF16)
            return cc

        lax.fori_loop(0, 4, add, 0)
        hop2(kh, par).start()

    def go3(kh, par):
        k = num(kh, par)
        slot = lax.rem(k, L1)
        hop2(kh, par).wait()

        def add(i, cc):
            if par == 0:
                r2e[kh, i] = (l1[slot, i, :, :, xcols(x)].astype(F32) + r2e[kh, i].astype(F32)).astype(BF16)
            else:
                r2o[kh, i] = (l1[slot, i, y].astype(F32) + r2o[kh, i].astype(F32)).astype(BF16)
            return cc

        lax.fori_loop(0, 4, add, 0)
        hop3(kh, par).start()

    def go4(kh, par):
        k = num(kh, par)
        hop3(kh, par).wait()

        def add(i, cc):
            own = r2e[kh, i, y] if par == 0 else r2o[kh, i, :, xcols(x)]
            r3[k, i] = (own.astype(F32) + r3[k, i].astype(F32)).astype(BF16)
            return cc

        lax.fori_loop(0, 4, add, 0)
        for d in (1, 2, 3):
            hop4(kh, par, d).start()

    def go5(kh, par):
        k = num(kh, par)
        total = r3[k, z].astype(F32)
        for d in (1, 2, 3):
            hop4(kh, par, d).wait()
            total = total + r4[k, d - 1].astype(F32)
        fin[k, y, x] = total.astype(BF16)
        for d in (1, 2, 3):
            hop5(kh, par, d, False).start()

    def go6(kh, par):
        for d in (1, 2, 3):
            hop5(kh, par, d, False).wait_send()
            hop5(kh, par, d, True).wait_recv()

    def step(kh, par, what=((go3, 4), (go4, 6))):
        for fn, lag in what:
            kk = kh - lag // 2

            @pl.when(kk >= 0)
            def _(fn=fn, kk=kk):
                fn(kk, par)

    due = {
        0: ((go3, 4), (go4, 2), (go5, 0)),
        1: ((go3, 5), (go4, 3), (go5, 1), (go2, 8)),
        2: ((go3, 6), (go4, 4), (go5, 2)),
        3: ((go2, 9), (go3, 7), (go4, 5), (go5, 3)),
        4: ((go3, 8), (go4, 6), (go5, 4)),
        5: ((go2, 10), (go3, 9), (go4, 7), (go5, 5)),
        6: ((go4, 8), (go5, 6)),
        7: ((go2, 11), (go3, 10), (go4, 9), (go5, 7)),
        8: ((go5, 8),),
        9: ((go4, 10), (go5, 9)),
        10: (),
        11: ((go3, 11), (go5, 10)),
        12: ((go4, 11),),
        13: (),
        14: ((go5, 11),),
        15: tuple((go6, k) for k in range(NCH)),
    }

    def step_at(i):
        for fn, k in due[i]:
            fn(k // 2, k % 2)

    def grad_chunk(ts, rhs, kh, par):
        k = num(kh, par)
        slot = lax.rem(k, L1)

        for i in range(3):
            cols = slice(i * 256, (i + 1) * 256)
            b = rhs(i)
            snd[par, :, :, :, cols] = nn(tr[ts, 1].reshape(384, n), b).astype(BF16).reshape(4, 2, 48, 256)
            l1[slot, :, :, :, cols] = nn(tr[ts, 0].reshape(384, n), b).astype(BF16).reshape(4, 2, 48, 256)
        hop1(kh, par).start()

    def put_t(ts, val, cols):
        for o in range(8):
            tr[ts, (o & 1) ^ c, o >> 1, :, cols] = val[o * 96:(o + 1) * 96]

    def addsum(at, v):
        gsm[:, at:at + v.shape[1]] += jnp.sum(v, axis=0, keepdims=True)

    wcopy(3, 4).wait()

    def head(i, cc):
        rows = pl.ds(pl.multiple_of(i * t, t), t)
        rv = pool[XB, rows, :].astype(F32) + nt(pool[OO, rows, :], w[4]) + small[:, BO:BO + D]
        rh, rs = norm_stats(rv)
        dka[rows, :] = jnp.broadcast_to(rs, (t, 128))
        pool[RH, rows, :] = rh.astype(BF16)
        h = (rh * small[:, G2:G2 + D] + small[:, S2:S2 + D]).astype(BF16)
        pool[HH, rows, :] = h
        put_t(1, h.T, rows)
        acc_o[rows, :] = rv + small[:, BP:BP + D]
        acc_d[rows, :] = jnp.zeros((t, D), F32)
        cv = pool[CT_, rows, :]
        put_t(0, cv.T, rows)
        addsum(BP, cv.astype(F32))
        return cc

    lax.fori_loop(0, n // t, head, 0, unroll=2)
    tick(4)

    def ff_tile(j, cc):
        s0 = 2 * lax.rem(j, 2)
        wcopy(4 + 2 * j, s0).wait()
        wcopy(5 + 2 * j, s0 + 1).wait()

        bf = pl.ds(pl.multiple_of(BF + j * D, 128), D)
        shift = small[:, bf]

        def rows_at(i):
            return slice(i * t, (i + 1) * t)

        def products(i):
            return nn(pool[HH, rows_at(i), :], w[s0]) + shift, nn(pool[CT_, rows_at(i), :], w[s0 + 1])

        def gelu(i, fv, u):
            f2 = fv * fv
            th = jnp.tanh(fv * (C0 + (C0 * C1) * f2))
            hp = 0.5 + 0.5 * th
            gv = fv * hp
            gp = hp + (gv * (2.0 - 2.0 * hp)) * (C0 + (3.0 * C0 * C1) * f2)
            gb, df = gv.astype(BF16), (u * gp).astype(BF16)
            pool[GJ, rows_at(i), :] = gb
            pool[DJ, rows_at(i), :] = df
            return gb, df

        def gather_back(i, gb, df):
            acc_o[rows_at(i), :] += nt(gb, w[s0 + 1])
            acc_d[rows_at(i), :] += nt(df, w[s0])

        now, before = products(0), None
        sums = jnp.zeros((1, D), F32)
        for i in range(n // t):
            ahead = products(i + 1) if i + 1 < n // t else None
            gb, df = gelu(i, *now)
            sums = sums + jnp.sum(df.astype(F32), axis=0, keepdims=True)
            if before is not None:
                gather_back(*before)
            before, now = (i, gb, df), ahead
        gather_back(*before)
        gsm[:, bf] += sums

        for i in range(2):
            @pl.when(j == i)
            def _(i=i):
                tick(5 + 2 * i)

        @pl.when(j < 3)
        def _():
            arrived(6 + 2 * j)
            wcopy(6 + 2 * j, 2 - s0).start()
            arrived(7 + 2 * j)
            wcopy(7 + 2 * j, 3 - s0).start()

        step(j, 0, ((go2, 2),))
        grad_chunk(0, lambda i: pool[GJ, :, i * 256:(i + 1) * 256], j, 0)
        step(j, 0)
        step(j, 1, ((go2, 2),))
        grad_chunk(1, lambda i: pool[DJ, :, i * 256:(i + 1) * 256], j, 1)
        step(j, 1)

        for i in range(2):
            @pl.when(j == i)
            def _(i=i):
                tick(6 + 2 * i)

        return cc

    lax.fori_loop(0, 4, ff_tile, 0)
    for i in range(3):
        wcopy(i, i).start()

    def tail(i, cc):
        rows = pl.ds(pl.multiple_of(i * t, t), t)
        pool[GJ, rows, :] = acc_o[rows, :].astype(BF16)
        dh = acc_d[rows, :]
        rh = pool[RH, rows, :].astype(F32)
        addsum(G2, dh * rh)
        addsum(S2, dh)
        e = dh * small[:, G2:G2 + D]
        dr = pool[CT_, rows, :].astype(F32) + dka[rows, 0:1] * (
            e - jnp.mean(e, axis=-1, keepdims=True) - rh * jnp.mean(e * rh, axis=-1, keepdims=True))
        acc_d[rows, :] = dr
        dy = dr.astype(BF16)
        addsum(BO, dy.astype(F32))
        put_t(2, dy.T, rows)
        pool[DO, rows, :] = nn(dy, w[4]).astype(BF16)
        return cc

    lax.fori_loop(0, n // t, tail, 0, unroll=2)
    oout = pltpu.make_async_copy(pool.at[GJ], out_h, st.at[0])
    oout.start()
    go2(3, 0)
    go2(3, 1)
    grad_chunk(2, lambda i: pool[OO, :, i * 256:(i + 1) * 256], 4, 0)
    step_at(0)
    qload = pltpu.make_async_copy(qkv_h, pool.at[pl.ds(OO, 3)], ld.at[0])
    qload.start()

    build_blocks()

    def xhat(rows):
        return norm_stats(pool[XB, rows, :].astype(F32))

    def a_tile(i, cc):
        rows = pl.ds(pl.multiple_of(i * t, t), t)
        xh, _ = xhat(rows)
        put_t(0, (xh * small[:, G1:G1 + D] + small[:, S1:S1 + D]).astype(BF16).T, rows)
        return cc

    lax.fori_loop(0, n // t, a_tile, 0, unroll=2)
    qload.wait()
    oout.wait()

    def pair(p, cc):
        cols = pl.ds(pl.multiple_of(p * 128, 128), 128)
        q8 = pool[OO, :, cols] * 0.125
        qt = q8.T
        k = pool[OO + 1, :, cols]
        kts = by_head_t(k.T)
        ks = by_head(k)
        vs = by_head(pool[OO + 2, :, cols])
        dv = pool[DO, :, cols]
        dt = dv.T
        dka[...] = jnp.zeros_like(dka)
        dva[...] = jnp.zeros_like(dva)

        def scores(q):
            tq = slice(q * TQ, (q + 1) * TQ)
            return nn(stack(ks, q), qt[:, tq]), nn(stack(vs, q), dt[:, tq])

        def soft(q, s, dp):
            size = span(q)[1]
            tq = slice(q * TQ, (q + 1) * TQ)
            bias = blocks(q)
            ps, dss = [], []
            for h in range(2):
                sl = slice(h * size, (h + 1) * size)
                pr = jnp.exp(s[sl] + bias - lse[p, h:h + 1, tq])
                dd = jnp.sum(dp[sl] * pr, axis=0, keepdims=True)
                dss.append((pr * (dp[sl] - dd)).astype(BF16))
                ps.append(pr.astype(BF16))
            return jnp.concatenate(ps, axis=0), jnp.concatenate(dss, axis=0)

        def back(q, pr, ds):
            lo, size = span(q)
            tq = slice(q * TQ, (q + 1) * TQ)
            dvv, dkk = nn(pr, dv[tq, :]), nn(ds, q8[tq, :])
            dqt = nn(beside(kts, q), ds)
            lane = lax.broadcasted_iota(jnp.int32, (size, 128), 1)
            dka[lo:lo + size, :] += jnp.where(lane < 64, dkk[:size], dkk[size:])
            dva[lo:lo + size, :] += jnp.where(lane < 64, dvv[:size], dvv[size:])
            pool[RH, tq, cols] = (dqt.T * 0.125).astype(BF16)

        now, before = scores(0), None
        for q in range(4):
            ahead = scores(q + 1) if q < 3 else None
            after = soft(q, *now)
            if before is not None:
                back(*before)
            before, now = (q,) + after, ahead
        back(*before)
        pool[RH + 1, :, cols] = dka[...].astype(BF16)
        pool[RH + 2, :, cols] = dva[...].astype(BF16)

        for i in range(6):
            @pl.when(p == i)
            def _(i=i):
                if i % 2 == 1:
                    m = i // 2
                    grad_chunk(0, lambda b: pool[RH + b, :, m * 256:(m + 1) * 256], (9 + m) // 2, (9 + m) % 2)
                step_at(1 + i)

        return cc

    lax.fori_loop(0, 6, pair, 0)

    for i in range(3):
        wcopy(i, i).wait()

    def last_tile(i):
        rows = pl.ds(i * t, t)
        xh, rs = xhat(rows)
        ds_ = [pool[RH + b, rows, :] for b in range(3)]
        da = nt(ds_[0], w[0]) + nt(ds_[1], w[1]) + nt(ds_[2], w[2])
        addsum(G1, da * xh)
        addsum(S1, da)
        addsum(BQ, ds_[0].astype(F32))
        addsum(BV, ds_[2].astype(F32))
        e = da * small[:, G1:G1 + D]
        acc_d[rows, :] += rs * (e - jnp.mean(e, axis=-1, keepdims=True) - xh * jnp.mean(e * xh, axis=-1, keepdims=True))
        pltpu.make_async_copy(acc_d.at[rows, :], gin_h.at[rows, :], st.at[i]).start()

    for i in range(4):
        last_tile(i)
        step_at(7 + i)

    groups = (((r, f ^ 1),), tuple((r ^ d, f) for d in (1, 2, 3)), tuple((r, f ^ (2 * d)) for d in (1, 2, 3)))

    def small_hops(i):
        return [remote(sbuf.at[i], srcv.at[3 * i + j], m_s.at[3 * i + j], m_r.at[3 * i + j], *to) for j, to in enumerate(groups[i])]

    sbuf[0] = gsm[...]
    for cp in small_hops(0):
        cp.start()

    def drain(k, cc):
        sent(three(k), z_s.at[k], z_r.at[k])
        sent(three(k), x_s.at[k], x_r.at[k])
        sent(three(k), y_s.at[k], y_r.at[k])
        sent(three_half(k), dx_s.at[k], dx_r.at[k])
        sent(three_half(k), dy_s.at[k], dy_r.at[k])
        sent(g.at[k, 0:96], own_s.at[k], own_r.at[k])
        sent(g.at[k, 0:288], c_s.at[k], c_r.at[k])
        return cc

    lax.fori_loop(0, NCH, drain, 0)
    for i in range(3):
        v = sbuf[i]
        for j, cp in enumerate(small_hops(i)):
            cp.wait()
            v = v + srcv[3 * i + j]
        if i < 2:
            sbuf[i + 1] = v
            for cp in small_hops(i + 1):
                cp.start()
        else:
            gsm_out[...] = v
        step_at(11 + i)
    step_at(14)
    step_at(15)
    for i in range(4):
        rows = pl.ds(i * t, t)
        pltpu.make_async_copy(acc_d.at[rows, :], gin_h.at[rows, :], st.at[i]).wait()


def layer(ws, vectors, tok, lat, cot, flags, seg):
    dma = pltpu.SemaphoreType.DMA
    n = tok.shape[0]
    anyspec = pl.BlockSpec(memory_space=pl.ANY)
    vspec = pl.BlockSpec(memory_space=pltpu.VMEM)
    vmem = pltpu.VMEM
    shards_ = [u.reshape(4, RQ, u.shape[1]) for u in ws]
    return pl.pallas_call(
        layer_kernel,
        in_specs=[vspec] * 12 + [anyspec] * 3 + [vspec] * 2,
        out_specs=[anyspec] * 4 + [vspec] * 2,
        out_shape=[
            jax.ShapeDtypeStruct((NCH, D, D), BF16),
            jax.ShapeDtypeStruct((3, n, D), BF16),
            jax.ShapeDtypeStruct((n, D), BF16),
            jax.ShapeDtypeStruct((n, D), F32),
            jax.ShapeDtypeStruct((NCH, 2, 2, 48, 384), BF16),
            jax.ShapeDtypeStruct((1, NSMALL), F32),
        ],
        scratch_shapes=[
            vmem((1, NSMALL), BF16), vmem((8, 1, NSMALL), BF16), vmem((1, NSMALL), F32), vmem((6, 2, n), F32),
            vmem((8, n, D), BF16), vmem((3, 2, 4, 96, n), BF16), vmem((5, D, D), BF16), vmem((n, D), F32), vmem((n, D), F32),
            vmem((L1, 4, 2, 48, D), BF16), vmem((2, 4, 2, 48, D), BF16), vmem((R1, 4, 2, 48, D), BF16),
            vmem((6, 4, 2, 48, 384), BF16), vmem((6, 4, 48, D), BF16), vmem((NCH, 4, 48, 384), BF16),
            vmem((NCH, 3, 48, 384), BF16), vmem((n, 128), F32), vmem((n, 128), F32), vmem((1, NSMALL), F32),
            vmem((3, 1, NSMALL), F32), vmem((9, 1, NSMALL), F32),
        ] + [dma((NCH,))] * 14 + [dma((7,))] * 2 + [dma((NCH,))]
        + [dma((8,)), dma((5,)), dma((4,))] + [dma((NCH,))] * 6 + [dma((NCH, 3))] * 4 + [dma((9,))] * 2,
        compiler_params=pltpu.CompilerParams(collective_id=1, has_side_effects=True, vmem_limit_bytes=61 << 20),
        name="layer",
    )(*shards_, *[v.reshape(1, -1) for v in vectors], tok, lat, cot, flags, seg)


def finish_kernel(fin, gsm, out_h, gin_h, gwq, gwo, gwf, gwp, v0, v1, v2, v3, v4, v5, v6, v7, out_o, gin_o,
                  ob, gb, isem, osem):
    f = lax.axis_index("fsdp")
    n = ob.shape[0]
    parts = []
    for i in range(2):
        rows = slice(i * (n // 2), (i + 1) * (n // 2))
        for src, buf, dst in ((gin_h, gb, gin_o), (out_h, ob, out_o)):
            k = len(parts)
            parts.append((pltpu.make_async_copy(src.at[rows], buf.at[rows], isem.at[k]),
                          pltpu.make_async_copy(buf.at[rows], dst.at[rows], osem.at[k])))
    for a, _ in parts:
        a.start()
    for v, at in zip((v0, v1, v2, v3, v4, v5, v6, v7), (G1, S1, BQ, BO, G2, S2, BF, BP)):
        m = v.shape[1]
        total = jnp.zeros((1, m), F32)
        for d in range(8):
            total = total + jnp.where(f == d, gsm[:, at + d * m:at + (d + 1) * m], 0.0)
        v[...] = total
    for a, b in parts:
        a.wait()
        b.start()
    for yy in range(2):
        rows = slice(yy * 48, (yy + 1) * 48)
        for xx in range(2):
            for j in range(4):
                cols = slice(j * D + xx * 384, j * D + (xx + 1) * 384)
                gwp[rows, cols] = fin[2 * j, yy, xx].astype(F32)
                gwf[rows, cols] = fin[2 * j + 1, yy, xx].astype(F32)
            gwo[rows, xx * 384:(xx + 1) * 384] = fin[8, yy, xx].astype(F32)
        for m in range(3):
            v = jnp.concatenate([fin[9 + m, yy, 0], fin[9 + m, yy, 1]], axis=1).astype(F32)
            for b in range(3):
                gwq[rows, b * D + m * 256:b * D + (m + 1) * 256] = v[:, b * 256:(b + 1) * 256]
    for _, b in parts:
        b.wait()


def finish(fin, gsm, out, gin, sizes):
    anyspec = pl.BlockSpec(memory_space=pl.ANY)
    vspec = pl.BlockSpec(memory_space=pltpu.VMEM)
    dma = pltpu.SemaphoreType.DMA
    shape = jax.ShapeDtypeStruct
    return pl.pallas_call(
        finish_kernel,
        in_specs=[vspec, vspec, anyspec, anyspec],
        out_specs=[vspec] * 12 + [anyspec] * 2,
        out_shape=[shape((96, 3 * D), F32), shape((96, D), F32), shape((96, FF), F32), shape((96, FF), F32)]
        + [shape((1, m), F32) for m in sizes] + [shape(out.shape, BF16), shape(gin.shape, F32)],
        scratch_shapes=[pltpu.VMEM(out.shape, BF16), pltpu.VMEM(gin.shape, F32), dma((4,)), dma((4,))],
        compiler_params=pltpu.CompilerParams(vmem_limit_bytes=VLIM),
        name="finish",
    )(fin, gsm, out, gin)


def own_slots(v, nf, f):
    m = v.shape[0]
    wide = jnp.broadcast_to(v[None, :], (nf, m))
    mine = lax.broadcasted_iota(jnp.int32, (nf, m), 0) == f
    return jnp.where(mine, wide, jnp.zeros_like(wide)).reshape(-1)


def shards(fast, tokens, latent, segment_ids, latent_flags, norm1_gain, norm1_shift, w_qkv, b_qv, w_out, b_out,
           norm2_gain, norm2_shift, w_fc, b_fc, w_proj, b_proj, cotangent):
    nf = lax.axis_size("fsdp")
    f = lax.axis_index("fsdp")
    vectors = (norm1_gain, norm1_shift, b_qv, b_out, norm2_gain, norm2_shift, b_fc, b_proj)
    ws = (w_qkv, w_out.T, w_fc, w_proj.T)

    def mine(total, at, v):
        m = v.shape[0]
        return lax.dynamic_slice(total[0], (at + f * m,), (m,))

    if fast:
        _, _, out, gin, fin, gsm = layer(ws, vectors, tokens, latent, cotangent, latent_flags, segment_ids)
        tq, to, tf, tp, *v, out, gin = finish(fin, gsm, out, gin, [v.shape[0] for v in vectors])
        to, tp, v = to.T, tp.T, [u.reshape(-1) for u in v]
    else:
        row = jnp.concatenate([own_slots(v, nf, f) for v in vectors]).reshape(1, NSMALL)
        wq, wo, wf, wp = [lax.all_gather(w, "fsdp", axis=0, tiled=True) for w in ws]
        small8 = lax.all_gather(row, "fsdp", axis=0, tiled=True)
        qkv, a_t, small = ln_qkv(tokens, latent, latent_flags, small8, wq)
        o, lse = attn_fwd(segment_ids, qkv)
        out, dr, do, gffn, gsm = ffn(tokens, latent, latent_flags, small, o, cotangent, wo, wf, wp)
        dqkv = attn_bwd(segment_ids, qkv, do, lse)
        gin, gq, gsm = last(tokens, latent, latent_flags, small, gsm, dr, dqkv, a_t, wq)

        def scatter(v):
            part = lax.psum_scatter(v, "fsdp", scatter_dimension=0, tiled=True)
            return lax.psum(part, "rep")

        tq, tp, tf, to = [scatter(v) for v in (gq, gffn[:, :FF], gffn[:, FF:2 * FF], gffn[:, 2 * FF:])]
        tq, to, tf, tp = tq.astype(F32), to.astype(F32).T, tf.astype(F32), tp.astype(F32).T
        gsm = lax.psum(gsm, ("rep", "fsdp"))
        v = [mine(gsm, at, v) for at, v in zip((G1, S1, BQ, BO, G2, S2, BF, BP), vectors)]
    return (out, gin, v[0], v[1], tq, v[2], to, v[3], v[4], v[5], tf, v[6], tp, v[7])


def solution(mesh):
    fast = mesh.shape["rep"] == 4 and mesh.shape["fsdp"] == 8
    both = P(("rep", "fsdp"), None)
    one, row, col = P("fsdp"), P("fsdp", None), P(None, "fsdp")
    return jax.shard_map(
        partial(shards, fast),
        mesh=mesh,
        in_specs=(both, both, both, both, one, one, row, one, col, one, one, one, row, one, col, one, both),
        out_specs=(both, both, one, one, row, one, col, one, one, one, row, one, col, one),
        check_vma=False,
    )
```

```python
from functools import partial

import jax
import jax.numpy as jnp
from jax import lax
from jax.experimental import pallas as pl
from jax.experimental.pallas import tpu as pltpu
from jax.sharding import PartitionSpec as P

D = 768
FF = 3072
NSMALL = 9216
NFFN = 6912
EPS = 1e-05
NEG = -1e30
G1, S1, BQ, BV, BO, G2, S2, BF, BP = 0, 768, 1536, 2304, 3072, 3840, 4608, 5376, 8448
F32 = jnp.float32
BF16 = jnp.bfloat16
VLIM = 60 << 20


def nn(a, b):
    return jnp.dot(a, b, preferred_element_type=F32)


def nt(a, b):
    return lax.dot_general(a, b, (((1,), (1,)), ((), ())), preferred_element_type=F32)


def norm_stats(x):
    mean = jnp.mean(x, axis=-1, keepdims=True)
    center = x - mean
    var = jnp.mean(center * center, axis=-1, keepdims=True)
    rs = lax.rsqrt(var + EPS)
    return center * rs, rs


def pick_rows(flags_row, tok, lat):
    t = flags_row.shape[1]
    col = jnp.broadcast_to(flags_row.astype(F32), (128, t)).T
    wide = jnp.concatenate([col] * (D // 128), axis=1)
    return jnp.where(wide > 0.5, lat.astype(F32), tok.astype(F32))


def ln_qkv_kernel(tok, lat, flags, small8, wq, qkv, a_t, small):
    sm = jnp.sum(small8[...].astype(F32), axis=0, keepdims=True)

    @pl.when(pl.program_id(0) == 0)
    def _():
        small[...] = sm

    x = pick_rows(flags[...], tok[...], lat[...])
    xh, _ = norm_stats(x)
    a = (xh * sm[:, G1:G1 + D] + sm[:, S1:S1 + D]).astype(BF16)
    a_t[...] = a.T
    for i in range(3):
        y = nn(a, wq[:, i * D:(i + 1) * D])
        if i == 0:
            y = y + sm[:, BQ:BQ + D]
        if i == 2:
            y = y + sm[:, BV:BV + D]
        qkv[i] = y.astype(BF16)


def ln_qkv(tok, lat, flags, small8, wq):
    n = tok.shape[0]
    t = 256
    return pl.pallas_call(
        ln_qkv_kernel,
        grid=(n // t,),
        in_specs=[
            pl.BlockSpec((t, D), lambda i: (i, 0)),
            pl.BlockSpec((t, D), lambda i: (i, 0)),
            pl.BlockSpec((1, t), lambda i: (0, i)),
            pl.BlockSpec(small8.shape, lambda i: (0, 0)),
            pl.BlockSpec((D, 3 * D), lambda i: (0, 0)),
        ],
        out_specs=[
            pl.BlockSpec((3, t, D), lambda i: (0, i, 0)),
            pl.BlockSpec((D, t), lambda i: (0, i)),
            pl.BlockSpec((1, NSMALL), lambda i: (0, 0)),
        ],
        out_shape=[
            jax.ShapeDtypeStruct((3, n, D), BF16),
            jax.ShapeDtypeStruct((D, n), BF16),
            jax.ShapeDtypeStruct((1, NSMALL), F32),
        ],
        compiler_params=pltpu.CompilerParams(vmem_limit_bytes=VLIM),
        name="ln_qkv",
    )(tok, lat, flags, small8, wq)


TQ = 256


def span(t):
    lo = max(0, t - 2)
    return lo * TQ, (t + 1 - lo) * TQ


def doc_starts(seg):
    st = jnp.zeros(seg.shape, jnp.int32)
    for s in range(1, 8):
        cnt = jnp.sum((seg < s).astype(jnp.int32), axis=1, keepdims=True)
        st = jnp.where(seg == s, cnt, st)
    return st


def build_bias(seg_ref, bias):
    st = doc_starts(seg_ref[...])
    for t in range(4):
        lo, size = span(t)
        j = lax.broadcasted_iota(jnp.int32, (size, TQ), 0) + lo
        i = lax.broadcasted_iota(jnp.int32, (size, TQ), 1) + t * TQ
        ok = jnp.logical_and(j >= st[:, t * TQ:(t + 1) * TQ], j <= i)
        bias[t, 0:size, :] = jnp.where(ok, 0.0, NEG)


def attn_fwd_kernel(seg_ref, qkv, o, lse, bias):
    @pl.when(pl.program_id(0) == 0)
    def _():
        build_bias(seg_ref, bias)

    qt = (qkv[0] * 0.125).T
    vt = qkv[2].T
    k = qkv[1]
    lane = lax.broadcasted_iota(jnp.int32, k.shape, 1)
    zero = jnp.zeros_like(k)
    ks = [jnp.where(lane < 64, k, zero), jnp.where(lane < 64, zero, k)]
    for t in range(4):
        lo, size = span(t)
        outs = []
        for h in range(2):
            s = nn(ks[h][lo:lo + size], qt[:, t * TQ:(t + 1) * TQ]) + bias[t, 0:size, :]
            m = jnp.max(s, axis=0, keepdims=True)
            p = jnp.exp(s - m)
            l = jnp.sum(p, axis=0, keepdims=True)
            ot = nn(vt[h * 64:(h + 1) * 64, lo:lo + size], p.astype(BF16))
            outs.append(ot * (1.0 / l))
            lse[0, h:h + 1, t * TQ:(t + 1) * TQ] = m + jnp.log(l)
        o[t * TQ:(t + 1) * TQ, :] = jnp.concatenate(outs, axis=0).T.astype(BF16)


def attn_fwd(seg, qkv):
    n = qkv.shape[1]
    return pl.pallas_call(
        attn_fwd_kernel,
        grid=(6,),
        in_specs=[
            pl.BlockSpec((1, n), lambda p: (0, 0)),
            pl.BlockSpec((3, n, 128), lambda p: (0, 0, p)),
        ],
        out_specs=[
            pl.BlockSpec((n, 128), lambda p: (0, p)),
            pl.BlockSpec((1, 2, n), lambda p: (p, 0, 0)),
        ],
        out_shape=[
            jax.ShapeDtypeStruct((n, D), BF16),
            jax.ShapeDtypeStruct((6, 2, n), F32),
        ],
        scratch_shapes=[pltpu.VMEM((4, 768, TQ), F32)],
        compiler_params=pltpu.CompilerParams(vmem_limit_bytes=VLIM),
        name="attn_fwd",
    )(seg, qkv)


C0 = 0.7978845608028654
C1 = 0.044715
TR = 512
TC = 512


def ffn_kernel(tok, lat, flags, small, o_h, cot_h, wo_h, wf_h, wp_h,
               out_h, dr_h, do_h, gffn_h, gsmall,
               o, cot, wo, wf, wp, gs, dfs, ct, ht, dyt, xs, rs_s, outs, dos, gwo, gwf, gwp, isem, osem):
    n = o.shape[0]
    ins = [pltpu.make_async_copy(a, b, isem.at[i]) for i, (a, b) in enumerate(
        [(o_h, o), (wo_h, wo), (cot_h, cot), (wf_h, wf), (wp_h, wp)])]
    for c in ins:
        c.start()
    gsmall[...] = jnp.zeros_like(gsmall)
    ins[0].wait()
    ins[1].wait()
    ins[2].wait()
    ins[3].wait()
    ins[4].wait()

    def row_tile(i, carry):
        r0 = pl.multiple_of(i * TR, TR)
        rows = pl.ds(r0, TR)
        x = pick_rows(flags[:, rows], tok[rows, :], lat[rows, :])
        r = x + nt(o[rows, :], wo[...]) + small[:, BO:BO + D]
        rh, rs = norm_stats(r)
        h = (rh * small[:, G2:G2 + D] + small[:, S2:S2 + D]).astype(BF16)
        ht[:, rows] = h.T
        c_t = cot[rows, :]
        ct[:, rows] = c_t.T
        gsmall[:, BP:BP + D] += jnp.sum(c_t.astype(F32), axis=0, keepdims=True)

        xs[...] = jnp.zeros_like(xs)
        rs_s[...] = jnp.zeros_like(rs_s)

        def col_tile(j, cc):
            c0 = pl.multiple_of(j * TC, TC)
            cols = pl.ds(c0, TC)
            f = nn(h, wf[:, cols]) + small[:, pl.ds(pl.multiple_of(BF + c0, 128), TC)]
            u = nn(c_t, wp[:, cols])
            f2 = f * f
            th = jnp.tanh(f * (C0 + (C0 * C1) * f2))
            hp = 0.5 + 0.5 * th
            g = f * hp
            gp = hp + (g * (2.0 - 2.0 * hp)) * (C0 + (3.0 * C0 * C1) * f2)
            gb = g.astype(BF16)
            df = (u * gp).astype(BF16)
            gs[rows, cols] = gb
            dfs[rows, cols] = df
            sl = pl.ds(pl.multiple_of(BF + c0, 128), TC)
            gsmall[:, sl] += jnp.sum(df.astype(F32), axis=0, keepdims=True)
            xs[...] += nt(gb, wp[:, cols])
            rs_s[...] += nt(df, wf[:, cols])
            return cc

        lax.fori_loop(0, FF // TC, col_tile, 0)
        outs[rows, :] = (r + xs[...] + small[:, BP:BP + D]).astype(BF16)
        dh = rs_s[...]
        gsmall[:, G2:G2 + D] += jnp.sum(dh * rh, axis=0, keepdims=True)
        gsmall[:, S2:S2 + D] += jnp.sum(dh, axis=0, keepdims=True)
        e = dh * small[:, G2:G2 + D]
        dr = c_t.astype(F32) + rs * (e - jnp.mean(e, axis=-1, keepdims=True) - rh * jnp.mean(e * rh, axis=-1, keepdims=True))
        dy = dr.astype(BF16)
        gsmall[:, BO:BO + D] += jnp.sum(dy.astype(F32), axis=0, keepdims=True)
        dyt[:, rows] = dy.T
        xs[...] = dr
        cp = pltpu.make_async_copy(xs, dr_h.at[rows, :], isem.at[0])
        cp.start()
        dos[rows, :] = nn(dy, wo[...]).astype(BF16)
        cp.wait()
        return carry

    lax.fori_loop(0, n // TR, row_tile, 0)
    c1 = pltpu.make_async_copy(outs, out_h, osem.at[0])
    c1.start()
    c2 = pltpu.make_async_copy(dos, do_h, osem.at[1])
    c2.start()

    def grad_tile(j, cc):
        cols = pl.ds(pl.multiple_of(j * TC, TC), TC)
        gwp[:, cols] = nn(ct[...], gs[:, cols]).astype(BF16)
        gwf[:, cols] = nn(ht[...], dfs[:, cols]).astype(BF16)
        return cc

    lax.fori_loop(0, FF // TC, grad_tile, 0)
    c3 = pltpu.make_async_copy(gwp, gffn_h.at[:, 0:FF], osem.at[2])
    c3.start()
    c4 = pltpu.make_async_copy(gwf, gffn_h.at[:, FF:2 * FF], osem.at[3])
    c4.start()

    def gwo_tile(j, cc):
        cols = pl.ds(pl.multiple_of(j * 256, 256), 256)
        gwo[:, cols] = nn(dyt[...], o[:, cols]).astype(BF16)
        return cc

    lax.fori_loop(0, D // 256, gwo_tile, 0)
    c5 = pltpu.make_async_copy(gwo, gffn_h.at[:, 2 * FF:], osem.at[4])
    c5.start()
    for c in (c1, c2, c3, c4, c5):
        c.wait()


def ffn(tok, lat, flags, small, o, cot, wo, wf, wp):
    n = tok.shape[0]
    anyspec = pl.BlockSpec(memory_space=pl.ANY)
    vspec = pl.BlockSpec(memory_space=pltpu.VMEM)
    return pl.pallas_call(
        ffn_kernel,
        in_specs=[vspec] * 4 + [anyspec] * 5,
        out_specs=[anyspec] * 4 + [vspec],
        out_shape=[
            jax.ShapeDtypeStruct((n, D), BF16),
            jax.ShapeDtypeStruct((n, D), F32),
            jax.ShapeDtypeStruct((n, D), BF16),
            jax.ShapeDtypeStruct((D, NFFN), BF16),
            jax.ShapeDtypeStruct((1, NSMALL), F32),
        ],
        scratch_shapes=[
            pltpu.VMEM((n, D), BF16),
            pltpu.VMEM((n, D), BF16),
            pltpu.VMEM((D, D), BF16),
            pltpu.VMEM((D, FF), BF16),
            pltpu.VMEM((D, FF), BF16),
            pltpu.VMEM((n, FF), BF16),
            pltpu.VMEM((n, FF), BF16),
            pltpu.VMEM((D, n), BF16),
            pltpu.VMEM((D, n), BF16),
            pltpu.VMEM((D, n), BF16),
            pltpu.VMEM((TR, D), F32),
            pltpu.VMEM((TR, D), F32),
            pltpu.VMEM((n, D), BF16),
            pltpu.VMEM((n, D), BF16),
            pltpu.VMEM((D, D), BF16),
            pltpu.VMEM((D, FF), BF16),
            pltpu.VMEM((D, FF), BF16),
            pltpu.SemaphoreType.DMA((5,)),
            pltpu.SemaphoreType.DMA((5,)),
        ],
        compiler_params=pltpu.CompilerParams(vmem_limit_bytes=VLIM),
        name="ffn",
    )(tok, lat, flags, small, o, cot, wo, wf, wp)


def attn_bwd_kernel(seg_ref, qkv, do, lse, dqkv, bias, dk_acc, dv_acc):
    @pl.when(pl.program_id(0) == 0)
    def _():
        build_bias(seg_ref, bias)

    q8 = qkv[0] * 0.125
    qt = q8.T
    k = qkv[1]
    kt = k.T
    v = qkv[2]
    d = do[...]
    dt = d.T
    lane = lax.broadcasted_iota(jnp.int32, k.shape, 1)
    zero = jnp.zeros_like(k)
    ks = [jnp.where(lane < 64, k, zero), jnp.where(lane < 64, zero, k)]
    vs = [jnp.where(lane < 64, v, zero), jnp.where(lane < 64, zero, v)]
    dk_acc[...] = jnp.zeros_like(dk_acc)
    dv_acc[...] = jnp.zeros_like(dv_acc)
    for t in range(4):
        lo, size = span(t)
        tq = slice(t * TQ, (t + 1) * TQ)
        dqs, dks, dvs = [], [], []
        for h in range(2):
            s = nn(ks[h][lo:lo + size], qt[:, tq]) + bias[t, 0:size, :]
            p = jnp.exp(s - lse[0, h:h + 1, tq])
            dp = nn(vs[h][lo:lo + size], dt[:, tq])
            dd = jnp.sum(dp * p, axis=0, keepdims=True)
            ds = (p * (dp - dd)).astype(BF16)
            dvs.append(nn(p.astype(BF16), d[tq, :]))
            dks.append(nn(ds, q8[tq, :]))
            dqs.append(nn(kt[h * 64:(h + 1) * 64, lo:lo + size], ds))
        lane2 = lax.broadcasted_iota(jnp.int32, (size, 128), 1)
        dk_acc[lo:lo + size, :] += jnp.where(lane2 < 64, dks[0], dks[1])
        dv_acc[lo:lo + size, :] += jnp.where(lane2 < 64, dvs[0], dvs[1])
        dqkv[0, tq, :] = (jnp.concatenate(dqs, axis=0).T * 0.125).astype(BF16)
    dqkv[1] = dk_acc[...].astype(BF16)
    dqkv[2] = dv_acc[...].astype(BF16)


def attn_bwd(seg, qkv, do, lse):
    n = qkv.shape[1]
    return pl.pallas_call(
        attn_bwd_kernel,
        grid=(6,),
        in_specs=[
            pl.BlockSpec((1, n), lambda p: (0, 0)),
            pl.BlockSpec((3, n, 128), lambda p: (0, 0, p)),
            pl.BlockSpec((n, 128), lambda p: (0, p)),
            pl.BlockSpec((1, 2, n), lambda p: (p, 0, 0)),
        ],
        out_specs=pl.BlockSpec((3, n, 128), lambda p: (0, 0, p)),
        out_shape=jax.ShapeDtypeStruct((3, n, D), BF16),
        scratch_shapes=[
            pltpu.VMEM((4, 768, TQ), F32),
            pltpu.VMEM((n, 128), F32),
            pltpu.VMEM((n, 128), F32),
        ],
        compiler_params=pltpu.CompilerParams(vmem_limit_bytes=VLIM),
        name="attn_bwd",
    )(seg, qkv, do, lse)


def last_body(tok, lat, flags, small, gsm_in, dr, dqkv, a_t, wq, gin, gwq, gsmall):
    i = pl.program_id(0)
    t = 256

    @pl.when(i == 0)
    def _():
        gsmall[...] = gsm_in[...]

    rows = pl.ds(pl.multiple_of(i * t, t), t)
    x = pick_rows(flags[:, rows], tok[rows, :], lat[rows, :])
    xh, rs = norm_stats(x)
    d0, d1, d2 = dqkv[0, rows, :], dqkv[1, rows, :], dqkv[2, rows, :]
    da = nt(d0, wq[:, 0:D]) + nt(d1, wq[:, D:2 * D]) + nt(d2, wq[:, 2 * D:3 * D])
    gsmall[:, G1:G1 + D] += jnp.sum(da * xh, axis=0, keepdims=True)
    gsmall[:, S1:S1 + D] += jnp.sum(da, axis=0, keepdims=True)
    gsmall[:, BQ:BQ + D] += jnp.sum(d0.astype(F32), axis=0, keepdims=True)
    gsmall[:, BV:BV + D] += jnp.sum(d2.astype(F32), axis=0, keepdims=True)
    e = da * small[:, G1:G1 + D]
    gin[...] = dr[...] + rs * (e - jnp.mean(e, axis=-1, keepdims=True) - xh * jnp.mean(e * xh, axis=-1, keepdims=True))
    ar = pl.ds(pl.multiple_of(i * 192, 192), 192)
    for c in range(3):
        gwq[:, c * D:(c + 1) * D] = nn(a_t[ar, :], dqkv[c]).astype(BF16)


def last(tok, lat, flags, small, gsm, dr, dqkv, a_t, wq):
    n = tok.shape[0]
    t = 256
    whole = lambda *s: pl.BlockSpec(s, lambda i: (0,) * len(s))
    return pl.pallas_call(
        last_body,
        grid=(n // t,),
        in_specs=[
            whole(n, D), whole(n, D), whole(1, n), whole(1, NSMALL), whole(1, NSMALL),
            pl.BlockSpec((t, D), lambda i: (i, 0)),
            whole(3, n, D), whole(D, n), whole(D, 3 * D),
        ],
        out_specs=[
            pl.BlockSpec((t, D), lambda i: (i, 0)),
            pl.BlockSpec((192, 3 * D), lambda i: (i, 0)),
            whole(1, NSMALL),
        ],
        out_shape=[
            jax.ShapeDtypeStruct((n, D), F32),
            jax.ShapeDtypeStruct((D, 3 * D), BF16),
            jax.ShapeDtypeStruct((1, NSMALL), F32),
        ],
        compiler_params=pltpu.CompilerParams(vmem_limit_bytes=VLIM),
        name="last",
    )(tok, lat, flags, small, gsm, dr, dqkv, a_t, wq)


MESH = pl.DeviceIdType.MESH
RQ = 24
NCH = 12
XB, DO, OO, CT_, HH, RH, GJ, DJ = range(8)
QS = (GJ, DO, DJ)
L1 = 5
R1 = 5
SCHEDULE = {
    "p0": (("F", 0),),
    "p1": (("S", 0),),
    "p2": (("T", 0), ("F", 1), ("F", 2),),
    "q0": (("S", 1), ("F", 3),),
    "q1": (("T", 1), ("S", 2), ("S", 3), ("F", 4), ("F", 5),),
    "q2": (("T", 2), ("T", 3), ("S", 4), ("F", 6),),
    "q3": (("A", 3), ("S", 5), ("F", 7),),
    "q4": (("T", 4), ("F", 8),),
    "q5": (("T", 5), ("S", 6), ("S", 7), ("F", 9),),
    "h0": (("A", 4), ("T", 6), ("S", 8),),
    "h1": (("F", 10), ("F", 11),),
    "b0": (("T", 7), ("S", 9),),
    "g0": (("A", 6), ("T", 8), ("S", 10),),
    "e0": (("A", 7), ("T", 9), ("S", 11),),
    "b1": (("2", 0), ("T", 10),),
    "g1": (("2", 1), ("T", 11),),
    "e1": (("A", 8), ("A", 9),),
    "b2": (("2", 2), ("2", 3),),
    "g2": (("A", 10), ("3", 0), ("3", 1),),
    "e2": (("A", 11),),
    "b3": (("2", 4), ("2", 5), ("3", 2), ("3", 3),),
    "t0": (("2", 6), ("2", 7), ("4", 0), ("3", 4), ("3", 5),),
    "t1": (("4", 1),),
    "r0": (("2", 8), ("4", 2),),
    "r1": (("4", 3), ("4", 4), ("3", 6),),
    "r2": (("2", 9), ("4", 5), ("3", 7), ("3", 8), ("5", 0), ("5", 1),),
    "r3": (("4", 6), ("4", 7), ("5", 2), ("5", 3),),
    "r4": (("2", 10), ("3", 9),),
    "r5": (("4", 8), ("5", 4), ("5", 6),),
    "s0": (("3", 10),),
    "s1": (("2", 11), ("4", 9),),
    "s2": (("5", 7),),
    "s3": (("A", 5), ("4", 10),),
    "u0": (("5", 5),),
    "u1": (("3", 11), ("5", 8), ("5", 9), ("5", 10),),
    "end": (("5", 11),),
}


def remote(a, b, ssem, rsem, rr, ff):
    return pltpu.make_async_remote_copy(src_ref=a, dst_ref=b, send_sem=ssem, recv_sem=rsem,
                                        device_id=(rr, ff), device_id_type=MESH)


def layer_kernel(sq, so, sf, sp, v0, v1, v2, v3, v4, v5, v6, v7, tok_h, lat_h, cot_h, flags, seg,
                 g, qkv_h, out_h, gin_h, fin, gsm_out,
                 ss, small8, small, lse, pool, tr, w, acc_o, acc_d, l1, snd, r1, r2e, r2o, r3, r4, rd, dka, dva, gsm, sbuf, srcv,
                 z_s, z_r, x_s, x_r, y_s, y_r, dx_s, dx_r, dy_s, dy_r, c_s, c_r, own_s, own_r, sm_s, sm_r, loc,
                 ld, wl, st, a_s, a_r, b_s, b_r, d_s, d_r, e_s, e_r, h_s, h_r, w_s, w_r, m_s, m_r):
    r = lax.axis_index("rep")
    f = lax.axis_index("fsdp")
    c, z, x, y = f & 1, f >> 1, r & 1, r >> 1
    n = tok_h.shape[0]
    t = 256
    loads = [pltpu.make_async_copy(s, pool.at[i], ld.at[i]) for i, s in ((XB, tok_h), (DJ, lat_h), (CT_, cot_h))]
    for cp in loads:
        cp.start()
    pieces = []
    for v in (v0, v1, v2, v3, v4, v5, v6, v7):
        val = v[...].astype(F32)
        pieces += [jnp.where(f == d, val, 0.0) for d in range(8)]
    ss[...] = jnp.concatenate(pieces, axis=1).astype(BF16)
    bar = pltpu.get_barrier_semaphore()
    for d in range(1, 8):
        pl.semaphore_signal(bar, inc=1, device_id=(r, f ^ d), device_id_type=MESH)
    for d in (1, 2, 3):
        pl.semaphore_signal(bar, inc=1, device_id=(r ^ d, f), device_id_type=MESH)
    pl.semaphore_wait(bar, 10)

    def rows_of(q):
        return pl.ds(pl.multiple_of(c * 96 + q * RQ, 8), RQ)

    def source(k):
        if k < 3:
            return [(sq, slice(b * D + k * 256, b * D + (k + 1) * 256), slice(b * 256, (b + 1) * 256)) for b in range(3)]
        if k == 3:
            return [(so, slice(0, D), slice(0, D))]
        i = (k - 4) // 2
        return [((sf, sp)[k % 2], slice(i * D, (i + 1) * D), slice(0, D))]

    def issue(k):
        quarter = pl.ds(pl.multiple_of(r * RQ, 8), RQ)
        mine = pl.ds(pl.multiple_of(c * 96, 8), 96)
        for ref, cols, to in source(k):
            for d in (1, 2, 3):
                remote(ref.at[quarter, cols], g.at[k, d, rows_of(r), to], z_s.at[k], z_r.at[k], r, f ^ (2 * d)).start()
        for ref, cols, to in source(k):
            remote(ref.at[:, cols], g.at[k, 0, mine, to], own_s.at[k], own_r.at[k], r, f ^ 1).start()
            pltpu.make_async_copy(ref.at[:, cols], g.at[k, 0, mine, to], loc.at[k]).start()

    def group(k, q):
        return g.at[k, 1:4, rows_of(q)]

    def half(k, q, h):
        return g.at[k, 1:4, rows_of(q), h * 384:(h + 1) * 384]

    def core(k, q):
        p = group(k, q)
        remote(p, p, c_s.at[k], c_r.at[k], r, f ^ 1).start()

    def got(ref, ssem, rsem):
        remote(ref, ref, ssem, rsem, r, f).wait_recv()

    def sent(ref, ssem, rsem):
        remote(ref, ref, ssem, rsem, r, f).wait_send()

    def first(k):
        p = group(k, r)
        got(p, z_s.at[k], z_r.at[k])
        remote(p, p, x_s.at[k], x_r.at[k], r ^ 1, f).start()
        remote(p, p, y_s.at[k], y_r.at[k], r ^ 2, f).start()
        core(k, r)

    def second(k):
        got(group(k, r ^ 1), x_s.at[k], x_r.at[k])
        h = half(k, r ^ 1, 0)
        remote(h, h, dy_s.at[k], dy_r.at[k], r ^ 2, f).start()
        core(k, r ^ 1)
        got(group(k, r ^ 2), y_s.at[k], y_r.at[k])
        h = half(k, r ^ 2, 1)
        remote(h, h, dx_s.at[k], dx_r.at[k], r ^ 1, f).start()
        core(k, r ^ 2)

    def third(k):
        got(half(k, r ^ 3, 0), dy_s.at[k], dy_r.at[k])
        got(half(k, r ^ 3, 1), dx_s.at[k], dx_r.at[k])
        core(k, r ^ 3)

    def own_rows(k):
        return g.at[k, 0, 0:96]

    def other_rows(k):
        return g.at[k, 1:4, 0:96]

    def arrived(k):
        got(own_rows(k), own_s.at[k], own_r.at[k])
        got(other_rows(k), c_s.at[k], c_r.at[k])
        pltpu.make_async_copy(own_rows(k), own_rows(k), loc.at[k]).wait()

    def wload(k, slot):
        for d in range(4):
            rows = pl.ds(pl.multiple_of((z ^ d) * 192, 64), 192)
            pltpu.make_async_copy(g.at[k, d], w.at[slot, rows], wl.at[slot]).start()

    def wwait(slot):
        pltpu.make_async_copy(w.at[slot], w.at[slot], wl.at[slot]).wait()

    for d in range(1, 8):
        remote(ss, small8.at[f], sm_s.at[d - 1], sm_r.at[d - 1], r, f ^ d).start()
    own_row = pltpu.make_async_copy(ss, small8.at[f], ld.at[1])
    own_row.start()
    issue(0)

    def build_blocks():
        row = doc_starts(seg[...])
        for q in range(4):
            lo, size = span(q)
            for b in range(size // TQ):
                jj = lax.broadcasted_iota(jnp.int32, (TQ, TQ), 0) + (lo + b * TQ)
                ii = lax.broadcasted_iota(jnp.int32, (TQ, TQ), 1) + q * TQ
                ok = jnp.logical_and(jj >= row[:, q * TQ:(q + 1) * TQ], jj <= ii)
                acc_o[q * TQ:(q + 1) * TQ, b * TQ:(b + 1) * TQ] = jnp.where(ok, 0.0, NEG)

    def blocks(q):
        size = span(q)[1]
        return jnp.concatenate([acc_o[q * TQ:(q + 1) * TQ, b * TQ:(b + 1) * TQ] for b in range(size // TQ)], axis=0)

    build_blocks()
    gsm[...] = jnp.zeros_like(gsm)
    own_row.wait()
    for d in range(1, 8):
        remote(ss, small8.at[f ^ d], sm_s.at[d - 1], sm_r.at[d - 1], r, f).wait()
    small[...] = jnp.sum(small8[...].astype(F32), axis=0)
    issue(1)
    for cp in loads:
        cp.wait()

    def ln_tile(i, cc):
        rows = pl.ds(pl.multiple_of(i * t, t), t)
        xv = pick_rows(flags[:, rows], pool[XB, rows, :], pool[DJ, rows, :])
        pool[XB, rows, :] = xv.astype(BF16)
        xh, _ = norm_stats(xv)
        pool[HH, rows, :] = (xh * small[:, G1:G1 + D] + small[:, S1:S1 + D]).astype(BF16)
        return cc

    def normalise(k):
        lax.fori_loop(2 * k, 2 * k + 2, ln_tile, 0)

    def project(m):
        wload(m, m)
        at = pl.multiple_of(m * 256, 256)
        row = jnp.concatenate([small[:, pl.ds(BQ + at, 256)], jnp.zeros((1, 256), F32), small[:, pl.ds(BV + at, 256)]], axis=1)
        wwait(m)
        for j in range(n // 512):
            rows = slice(j * 512, (j + 1) * 512)
            v = (nn(pool[HH, rows, :], w[m]) + row).astype(BF16)
            for b in range(3):
                pool[QS[b], rows, pl.ds(at, 256)] = v[:, b * 256:(b + 1) * 256]

    here = set()

    def load_of(k):
        slot = 4 if k == 3 else 2 * ((k - 4) // 2 % 2) + k % 2
        if k not in here:
            here.add(k)
            arrived(k)
            wload(k, slot)

    def at(point):
        for name, k in SCHEDULE.get(point, ()):
            if name == "F":
                first(k)
                if k + 2 < NCH:
                    issue(k + 2)
            elif name == "S":
                second(k)
            elif name == "T":
                third(k)
            elif name == "A":
                load_of(k)
            elif k == NCH - 1 and name in "23":
                (dgo2 if name == "2" else dgo3)(k)
            else:
                {"2": go2, "3": go3, "4": go4, "5": go5}[name](k // 2, k % 2)

    def at_one(index, names):
        for i, name in enumerate(names):
            @pl.when(index == i)
            def _(name=name):
                at(name)

    at("p0")
    normalise(0)
    at("p1")
    normalise(1)
    at("p2")

    def by_head(v):
        lane = lax.broadcasted_iota(jnp.int32, v.shape, 1)
        zero = jnp.zeros_like(v)
        return jnp.where(lane < 64, v, zero), jnp.where(lane < 64, zero, v)

    def by_head_t(v):
        row = lax.broadcasted_iota(jnp.int32, v.shape, 0)
        zero = jnp.zeros_like(v)
        return jnp.where(row < 64, v, zero), jnp.where(row < 64, zero, v)

    def stack(two, q):
        lo, size = span(q)
        return jnp.concatenate([v[lo:lo + size] for v in two], axis=0)

    def beside(two, q):
        lo, size = span(q)
        return jnp.concatenate([v[:, lo:lo + size] for v in two], axis=1)

    def pair_fwd(p, cc):
        @pl.when(lax.rem(p, 2) == 0)
        def _():
            m = p // 2
            arrived(m)
            project(m)

        cols = pl.ds(pl.multiple_of(p * 128, 128), 128)
        qt = (pool[QS[0], :, cols] * 0.125).T
        vts = by_head_t(pool[QS[2], :, cols].T)
        ks = by_head(pool[QS[1], :, cols])

        def scores(q):
            return nn(stack(ks, q), qt[:, q * TQ:(q + 1) * TQ])

        def soft(q, s):
            size = span(q)[1]
            bias = blocks(q)
            es, inv = [], []
            for h in range(2):
                sh = s[h * size:(h + 1) * size] + bias
                m = jnp.max(sh, axis=0, keepdims=True)
                e = jnp.exp(sh - m)
                l = jnp.sum(e, axis=0, keepdims=True)
                lse[p, h:h + 1, q * TQ:(q + 1) * TQ] = m + jnp.log(l)
                es.append(e.astype(BF16))
                inv.append(1.0 / l)
            return jnp.concatenate(es, axis=0), inv

        def mix(q, e, inv):
            ot = nn(beside(vts, q), e)
            ot = jnp.concatenate([ot[0:64] * inv[0], ot[64:128] * inv[1]], axis=0)
            pool[OO, q * TQ:(q + 1) * TQ, cols] = ot.T.astype(BF16)

        s, before = scores(0), None
        for q in range(4):
            ahead = scores(q + 1) if q < 3 else None
            after = soft(q, s)
            if before is not None:
                mix(*before)
            before, s = (q,) + after, ahead
        mix(*before)
        at_one(p, ["q%d" % i for i in range(6)])
        return cc

    lax.fori_loop(0, 6, pair_fwd, 0)
    for m in range(3):
        pltpu.make_async_copy(pool.at[QS[m]], qkv_h.at[m], st.at[m]).start()
    load_of(3)

    def xcols(v):
        return pl.ds(pl.multiple_of(v * 384, 128), 384)

    def num(kh, par):
        return 2 * kh + par

    def hop1(k):
        return remote(snd.at[lax.rem(k, 2)], r1.at[lax.rem(k, R1)], a_s.at[k], a_r.at[k], r, f ^ 1)

    def hop2(kh, par):
        k = num(kh, par)
        slot = lax.rem(k, L1)
        if par == 0:
            return remote(l1.at[slot, :, :, :, xcols(1 - x)], r2e.at[kh], b_s.at[k], b_r.at[k], r ^ 1, f)
        return remote(l1.at[slot, :, 1 - y], r2o.at[kh], b_s.at[k], b_r.at[k], r ^ 2, f)

    def hop3(kh, par):
        k = num(kh, par)
        if par == 0:
            return remote(r2e.at[kh, :, 1 - y], r3.at[k], d_s.at[k], d_r.at[k], r ^ 2, f)
        return remote(r2o.at[kh, :, :, xcols(1 - x)], r3.at[k], d_s.at[k], d_r.at[k], r ^ 1, f)

    def hop4(kh, par, d):
        k = num(kh, par)
        return remote(r3.at[k, z ^ d], r4.at[k, d - 1], e_s.at[k, d - 1], e_r.at[k, d - 1], r, f ^ (2 * d))

    def hop5(kh, par, d, far):
        k = num(kh, par)
        q = r ^ d if far else r
        ref = fin.at[k, q >> 1, q & 1]
        return remote(ref, ref, h_s.at[k, d - 1], h_r.at[k, d - 1], r ^ d, f)

    def go2(kh, par):
        k = num(kh, par)
        slot = lax.rem(k, L1)
        hop1(k).wait()

        def add(i, cc):
            l1[slot, i] = (l1[slot, i].astype(F32) + r1[lax.rem(k, R1), i].astype(F32)).astype(BF16)
            return cc

        lax.fori_loop(0, 4, add, 0)
        hop2(kh, par).start()

    def go3(kh, par):
        k = num(kh, par)
        slot = lax.rem(k, L1)
        hop2(kh, par).wait()

        def add(i, cc):
            if par == 0:
                r2e[kh, i] = (l1[slot, i, :, :, xcols(x)].astype(F32) + r2e[kh, i].astype(F32)).astype(BF16)
            else:
                r2o[kh, i] = (l1[slot, i, y].astype(F32) + r2o[kh, i].astype(F32)).astype(BF16)
            return cc

        lax.fori_loop(0, 4, add, 0)
        hop3(kh, par).start()

    def go4(kh, par):
        k = num(kh, par)
        hop3(kh, par).wait()

        def add(i, cc):
            own = r2e[kh, i, y] if par == 0 else r2o[kh, i, :, xcols(x)]
            r3[k, i] = (own.astype(F32) + r3[k, i].astype(F32)).astype(BF16)
            return cc

        lax.fori_loop(0, 4, add, 0)
        for d in (1, 2, 3):
            hop4(kh, par, d).start()

    def go5(kh, par):
        k = num(kh, par)
        total = r3[k, z].astype(F32)
        for d in (1, 2, 3):
            hop4(kh, par, d).wait()
            total = total + r4[k, d - 1].astype(F32)
        fin[k, y, x] = total.astype(BF16)
        for d in (1, 2, 3):
            hop5(kh, par, d, False).start()

    def go6(kh, par):
        for d in (1, 2, 3):
            hop5(kh, par, d, False).wait_send()
            hop5(kh, par, d, True).wait_recv()

    def own_add(k):
        slot = k % L1
        hop1(k).wait()

        def add(i, cc):
            l1[slot, i] = (l1[slot, i].astype(F32) + r1[k % R1, i].astype(F32)).astype(BF16)
            return cc

        lax.fori_loop(0, 4, add, 0)

    def direct(k, d):
        q = r ^ d
        return remote(l1.at[k % L1, :, q >> 1, :, xcols(q & 1)], rd.at[d - 1], w_s.at[d - 1], w_r.at[d - 1], q, f)

    def dgo2(k):
        own_add(k)
        for d in (1, 2, 3):
            direct(k, d).start()

    def dgo3(k):
        for d in (1, 2, 3):
            direct(k, d).wait()

        def add(i, cc):
            v = l1[k % L1, i, y, :, xcols(x)].astype(F32)
            for d in range(3):
                v = v + rd[d, i].astype(F32)
            r3[k, i] = v.astype(BF16)
            return cc

        lax.fori_loop(0, 4, add, 0)
        for d in (1, 2, 3):
            hop4(k // 2, k % 2, d).start()

    def grad_chunk(ts, rhs, k):
        slot, par = lax.rem(k, L1), lax.rem(k, 2)

        for i in range(3):
            cols = slice(i * 256, (i + 1) * 256)
            b = rhs(i)
            snd[par, :, :, :, cols] = nn(tr[ts, 1].reshape(384, n), b).astype(BF16).reshape(4, 2, 48, 256)
            l1[slot, :, :, :, cols] = nn(tr[ts, 0].reshape(384, n), b).astype(BF16).reshape(4, 2, 48, 256)
        hop1(k).start()

    def put_t(ts, val, cols):
        for o in range(8):
            tr[ts, (o & 1) ^ c, o >> 1, :, cols] = val[o * 96:(o + 1) * 96]

    def addsum(at, v):
        gsm[:, at:at + v.shape[1]] += jnp.sum(v, axis=0, keepdims=True)

    wwait(4)

    def head(i, cc):
        rows = pl.ds(pl.multiple_of(i * t, t), t)
        rv = pool[XB, rows, :].astype(F32) + nt(pool[OO, rows, :], w[4]) + small[:, BO:BO + D]
        rh, rs = norm_stats(rv)
        dka[rows, :] = jnp.broadcast_to(rs, (t, 128))
        pool[RH, rows, :] = rh.astype(BF16)
        h = (rh * small[:, G2:G2 + D] + small[:, S2:S2 + D]).astype(BF16)
        pool[HH, rows, :] = h
        put_t(1, h.T, rows)
        acc_o[rows, :] = rv + small[:, BP:BP + D]
        acc_d[rows, :] = jnp.zeros((t, D), F32)
        cv = pool[CT_, rows, :]
        put_t(0, cv.T, rows)
        addsum(BP, cv.astype(F32))
        return cc

    lax.fori_loop(0, 2, head, 0, unroll=2)
    at("h0")
    lax.fori_loop(2, 4, head, 0, unroll=2)
    at("h1")
    for m in range(3):
        pltpu.make_async_copy(pool.at[QS[m]], qkv_h.at[m], st.at[m]).wait()

    def ff_tile(j, cc):
        s0 = 2 * lax.rem(j, 2)
        for i in range(4):
            @pl.when(j == i)
            def _(i=i):
                load_of(4 + 2 * i)
                load_of(5 + 2 * i)

        wwait(s0)
        wwait(s0 + 1)
        bf = pl.ds(pl.multiple_of(BF + j * D, 128), D)
        shift = small[:, bf]

        def rows_at(i):
            return slice(i * t, (i + 1) * t)

        def products(i):
            return nn(pool[HH, rows_at(i), :], w[s0]) + shift, nn(pool[CT_, rows_at(i), :], w[s0 + 1])

        def gelu(i, fv, u):
            f2 = fv * fv
            th = jnp.tanh(fv * (C0 + (C0 * C1) * f2))
            hp = 0.5 + 0.5 * th
            gv = fv * hp
            gp = hp + (gv * (2.0 - 2.0 * hp)) * (C0 + (3.0 * C0 * C1) * f2)
            gb, df = gv.astype(BF16), (u * gp).astype(BF16)
            pool[GJ, rows_at(i), :] = gb
            pool[DJ, rows_at(i), :] = df
            return gb, df

        def gather_back(i, gb, df):
            acc_o[rows_at(i), :] += nt(gb, w[s0 + 1])
            acc_d[rows_at(i), :] += nt(df, w[s0])

        now, before = products(0), None
        sums = jnp.zeros((1, D), F32)
        for i in range(n // t):
            ahead = products(i + 1) if i + 1 < n // t else None
            gb, df = gelu(i, *now)
            sums = sums + jnp.sum(df.astype(F32), axis=0, keepdims=True)
            if before is not None:
                gather_back(*before)
            before, now = (i, gb, df), ahead
        gather_back(*before)
        gsm[:, bf] += sums

        at_one(j, ["b%d" % i for i in range(4)])
        grad_chunk(0, lambda i: pool[GJ, :, i * 256:(i + 1) * 256], 2 * j)
        at_one(j, ["g%d" % i for i in range(4)])
        grad_chunk(1, lambda i: pool[DJ, :, i * 256:(i + 1) * 256], 2 * j + 1)
        at_one(j, ["e%d" % i for i in range(4)])
        return cc

    lax.fori_loop(0, 4, ff_tile, 0)
    for i in range(3):
        wload(i, i)

    def tail(i, cc):
        rows = pl.ds(pl.multiple_of(i * t, t), t)
        pool[GJ, rows, :] = acc_o[rows, :].astype(BF16)
        dh = acc_d[rows, :]
        rh = pool[RH, rows, :].astype(F32)
        addsum(G2, dh * rh)
        addsum(S2, dh)
        e = dh * small[:, G2:G2 + D]
        dr = pool[CT_, rows, :].astype(F32) + dka[rows, 0:1] * (
            e - jnp.mean(e, axis=-1, keepdims=True) - rh * jnp.mean(e * rh, axis=-1, keepdims=True))
        acc_d[rows, :] = dr
        dy = dr.astype(BF16)
        addsum(BO, dy.astype(F32))
        put_t(2, dy.T, rows)
        pool[DO, rows, :] = nn(dy, w[4]).astype(BF16)
        return cc

    lax.fori_loop(0, n // t, tail, 0, unroll=2)
    oout = pltpu.make_async_copy(pool.at[GJ], out_h, st.at[0])
    oout.start()
    at("t0")
    grad_chunk(2, lambda i: pool[OO, :, i * 256:(i + 1) * 256], 8)
    at("t1a")
    qload = pltpu.make_async_copy(qkv_h, pool.at[pl.ds(OO, 3)], ld.at[0])
    qload.start()

    build_blocks()

    def xhat(rows):
        return norm_stats(pool[XB, rows, :].astype(F32))

    def a_tile(i, cc):
        rows = pl.ds(pl.multiple_of(i * t, t), t)
        xh, _ = xhat(rows)
        put_t(0, (xh * small[:, G1:G1 + D] + small[:, S1:S1 + D]).astype(BF16).T, rows)
        return cc

    lax.fori_loop(0, n // t, a_tile, 0, unroll=2)
    qload.wait()
    oout.wait()
    at("t1")

    def pair(p, cc):
        cols = pl.ds(pl.multiple_of(p * 128, 128), 128)
        q8 = pool[OO, :, cols] * 0.125
        qt = q8.T
        k = pool[OO + 1, :, cols]
        kts = by_head_t(k.T)
        ks = by_head(k)
        vs = by_head(pool[OO + 2, :, cols])
        dv = pool[DO, :, cols]
        dt = dv.T
        dka[...] = jnp.zeros_like(dka)
        dva[...] = jnp.zeros_like(dva)

        def scores(q):
            tq = slice(q * TQ, (q + 1) * TQ)
            return nn(stack(ks, q), qt[:, tq]), nn(stack(vs, q), dt[:, tq])

        def soft(q, s, dp):
            size = span(q)[1]
            tq = slice(q * TQ, (q + 1) * TQ)
            bias = blocks(q)
            ps, dss = [], []
            for h in range(2):
                sl = slice(h * size, (h + 1) * size)
                pr = jnp.exp(s[sl] + bias - lse[p, h:h + 1, tq])
                dd = jnp.sum(dp[sl] * pr, axis=0, keepdims=True)
                dss.append((pr * (dp[sl] - dd)).astype(BF16))
                ps.append(pr.astype(BF16))
            return jnp.concatenate(ps, axis=0), jnp.concatenate(dss, axis=0)

        def back(q, pr, ds):
            lo, size = span(q)
            tq = slice(q * TQ, (q + 1) * TQ)
            dvv, dkk = nn(pr, dv[tq, :]), nn(ds, q8[tq, :])
            dqt = nn(beside(kts, q), ds)
            lane = lax.broadcasted_iota(jnp.int32, (size, 128), 1)
            dka[lo:lo + size, :] += jnp.where(lane < 64, dkk[:size], dkk[size:])
            dva[lo:lo + size, :] += jnp.where(lane < 64, dvv[:size], dvv[size:])
            pool[RH, tq, cols] = (dqt.T * 0.125).astype(BF16)

        now, before = scores(0), None
        for q in range(4):
            ahead = scores(q + 1) if q < 3 else None
            after = soft(q, *now)
            if before is not None:
                back(*before)
            before, now = (q,) + after, ahead
        back(*before)
        pool[RH + 1, :, cols] = dka[...].astype(BF16)
        pool[RH + 2, :, cols] = dva[...].astype(BF16)

        @pl.when(lax.rem(p, 2) == 1)
        def _():
            m = p // 2
            grad_chunk(0, lambda b: pool[RH + b, :, pl.ds(pl.multiple_of(m * 256, 256), 256)], 9 + m)

        at_one(p, ["r%d" % i for i in range(6)])
        return cc

    lax.fori_loop(0, 6, pair, 0)

    for i in range(3):
        wwait(i)

    def last_tile(i, cc):
        rows = pl.ds(pl.multiple_of(i * t, t), t)
        xh, rs = xhat(rows)
        ds_ = [pool[RH + b, rows, :] for b in range(3)]
        da = sum(nt(jnp.concatenate([v[:, m * 256:(m + 1) * 256] for v in ds_], axis=1), w[m]) for m in range(3))
        addsum(G1, da * xh)
        addsum(S1, da)
        addsum(BQ, ds_[0].astype(F32))
        addsum(BV, ds_[2].astype(F32))
        e = da * small[:, G1:G1 + D]
        acc_d[rows, :] += rs * (e - jnp.mean(e, axis=-1, keepdims=True) - xh * jnp.mean(e * xh, axis=-1, keepdims=True))
        pltpu.make_async_copy(acc_d.at[rows, :], gin_h.at[rows, :], st.at[i]).start()
        at_one(i, ["s%d" % b for b in range(4)])
        return cc

    lax.fori_loop(0, 4, last_tile, 0)

    groups = (((r, f ^ 1),), tuple((r ^ d, f) for d in (1, 2, 3)), tuple((r, f ^ (2 * d)) for d in (1, 2, 3)))

    def small_hops(i):
        return [remote(sbuf.at[i], srcv.at[3 * i + j], m_s.at[3 * i + j], m_r.at[3 * i + j], *to) for j, to in enumerate(groups[i])]

    sbuf[0] = gsm[...]
    for cp in small_hops(0):
        cp.start()

    def drain(k, cc):
        sent(group(k, r), z_s.at[k], z_r.at[k])
        sent(group(k, r), x_s.at[k], x_r.at[k])
        sent(group(k, r), y_s.at[k], y_r.at[k])
        sent(half(k, r, 0), dx_s.at[k], dx_r.at[k])
        sent(half(k, r, 0), dy_s.at[k], dy_r.at[k])
        sent(own_rows(k), own_s.at[k], own_r.at[k])
        sent(other_rows(k), c_s.at[k], c_r.at[k])
        return cc

    lax.fori_loop(0, NCH, drain, 0)
    for i in range(3):
        v = sbuf[i]
        for j, cp in enumerate(small_hops(i)):
            cp.wait()
            v = v + srcv[3 * i + j]
        if i < 2:
            sbuf[i + 1] = v
            for cp in small_hops(i + 1):
                cp.start()
        else:
            gsm_out[...] = v
        at("u%d" % i)
    at("end")
    for k in range(NCH):
        go6(k // 2, k % 2)
    for i in range(4):
        rows = pl.ds(i * t, t)
        pltpu.make_async_copy(acc_d.at[rows, :], gin_h.at[rows, :], st.at[i]).wait()


def layer(ws, vectors, tok, lat, cot, flags, seg):
    dma = pltpu.SemaphoreType.DMA
    n = tok.shape[0]
    anyspec = pl.BlockSpec(memory_space=pl.ANY)
    vspec = pl.BlockSpec(memory_space=pltpu.VMEM)
    vmem = pltpu.VMEM
    return pl.pallas_call(
        layer_kernel,
        in_specs=[vspec] * 12 + [anyspec] * 3 + [vspec] * 2,
        out_specs=[anyspec] * 4 + [vspec] * 2,
        out_shape=[
            jax.ShapeDtypeStruct((NCH, 4, 192, D), BF16),
            jax.ShapeDtypeStruct((3, n, D), BF16),
            jax.ShapeDtypeStruct((n, D), BF16),
            jax.ShapeDtypeStruct((n, D), F32),
            jax.ShapeDtypeStruct((NCH, 2, 2, 48, 384), BF16),
            jax.ShapeDtypeStruct((1, NSMALL), F32),
        ],
        scratch_shapes=[
            vmem((1, NSMALL), BF16), vmem((8, 1, NSMALL), BF16), vmem((1, NSMALL), F32), vmem((6, 2, n), F32),
            vmem((8, n, D), BF16), vmem((3, 2, 4, 96, n), BF16), vmem((5, D, D), BF16), vmem((n, D), F32), vmem((n, D), F32),
            vmem((L1, 4, 2, 48, D), BF16), vmem((2, 4, 2, 48, D), BF16), vmem((R1, 4, 2, 48, D), BF16),
            vmem((6, 4, 2, 48, 384), BF16), vmem((5, 4, 48, D), BF16), vmem((NCH, 4, 48, 384), BF16),
            vmem((NCH, 3, 48, 384), BF16), vmem((3, 4, 48, 384), BF16), vmem((n, 128), F32), vmem((n, 128), F32), vmem((1, NSMALL), F32),
            vmem((3, 1, NSMALL), F32), vmem((9, 1, NSMALL), F32),
        ] + [dma((NCH,))] * 14 + [dma((7,))] * 2 + [dma((NCH,))]
        + [dma((8,)), dma((5,)), dma((4,))] + [dma((NCH,))] * 6 + [dma((NCH, 3))] * 4 + [dma((3,))] * 2 + [dma((9,))] * 2,
        compiler_params=pltpu.CompilerParams(collective_id=1, has_side_effects=True, vmem_limit_bytes=61 << 20),
        name="layer",
    )(*ws, *[v.reshape(1, -1) for v in vectors], tok, lat, cot, flags, seg)


def finish_kernel(fin, gsm, out_h, gin_h, gwq, gwo, gwf, gwp, v0, v1, v2, v3, v4, v5, v6, v7, out_o, gin_o,
                  ob, gb, isem, osem):
    f = lax.axis_index("fsdp")
    n = ob.shape[0]
    parts = []
    for i in range(2):
        rows = slice(i * (n // 2), (i + 1) * (n // 2))
        for src, buf, dst in ((gin_h, gb, gin_o), (out_h, ob, out_o)):
            k = len(parts)
            parts.append((pltpu.make_async_copy(src.at[rows], buf.at[rows], isem.at[k]),
                          pltpu.make_async_copy(buf.at[rows], dst.at[rows], osem.at[k])))
    for a, _ in parts:
        a.start()
    for v, at in zip((v0, v1, v2, v3, v4, v5, v6, v7), (G1, S1, BQ, BO, G2, S2, BF, BP)):
        m = v.shape[1]
        total = jnp.zeros((1, m), F32)
        for d in range(8):
            total = total + jnp.where(f == d, gsm[:, at + d * m:at + (d + 1) * m], 0.0)
        v[...] = total
    for a, b in parts:
        a.wait()
        b.start()
    for yy in range(2):
        rows = slice(yy * 48, (yy + 1) * 48)
        for xx in range(2):
            for j in range(4):
                cols = slice(j * D + xx * 384, j * D + (xx + 1) * 384)
                gwp[rows, cols] = fin[2 * j, yy, xx].astype(F32)
                gwf[rows, cols] = fin[2 * j + 1, yy, xx].astype(F32)
            gwo[rows, xx * 384:(xx + 1) * 384] = fin[8, yy, xx].astype(F32)
        for m in range(3):
            v = jnp.concatenate([fin[9 + m, yy, 0], fin[9 + m, yy, 1]], axis=1).astype(F32)
            for b in range(3):
                gwq[rows, b * D + m * 256:b * D + (m + 1) * 256] = v[:, b * 256:(b + 1) * 256]
    for _, b in parts:
        b.wait()


def finish(fin, gsm, out, gin, sizes):
    anyspec = pl.BlockSpec(memory_space=pl.ANY)
    vspec = pl.BlockSpec(memory_space=pltpu.VMEM)
    dma = pltpu.SemaphoreType.DMA
    shape = jax.ShapeDtypeStruct
    return pl.pallas_call(
        finish_kernel,
        in_specs=[vspec, vspec, anyspec, anyspec],
        out_specs=[vspec] * 12 + [anyspec] * 2,
        out_shape=[shape((96, 3 * D), F32), shape((96, D), F32), shape((96, FF), F32), shape((96, FF), F32)]
        + [shape((1, m), F32) for m in sizes] + [shape(out.shape, BF16), shape(gin.shape, F32)],
        scratch_shapes=[pltpu.VMEM(out.shape, BF16), pltpu.VMEM(gin.shape, F32), dma((4,)), dma((4,))],
        compiler_params=pltpu.CompilerParams(vmem_limit_bytes=VLIM),
        name="finish",
    )(fin, gsm, out, gin)


def own_slots(v, nf, f):
    m = v.shape[0]
    wide = jnp.broadcast_to(v[None, :], (nf, m))
    mine = lax.broadcasted_iota(jnp.int32, (nf, m), 0) == f
    return jnp.where(mine, wide, jnp.zeros_like(wide)).reshape(-1)


def shards(fast, tokens, latent, segment_ids, latent_flags, norm1_gain, norm1_shift, w_qkv, b_qv, w_out, b_out,
           norm2_gain, norm2_shift, w_fc, b_fc, w_proj, b_proj, cotangent):
    nf = lax.axis_size("fsdp")
    f = lax.axis_index("fsdp")
    vectors = (norm1_gain, norm1_shift, b_qv, b_out, norm2_gain, norm2_shift, b_fc, b_proj)
    ws = (w_qkv, w_out.T, w_fc, w_proj.T)

    def mine(total, at, v):
        m = v.shape[0]
        return lax.dynamic_slice(total[0], (at + f * m,), (m,))

    if fast:
        _, _, out, gin, fin, gsm = layer(ws, vectors, tokens, latent, cotangent, latent_flags, segment_ids)
        tq, to, tf, tp, *v, out, gin = finish(fin, gsm, out, gin, [v.shape[0] for v in vectors])
        to, tp, v = to.T, tp.T, [u.reshape(-1) for u in v]
    else:
        row = jnp.concatenate([own_slots(v, nf, f) for v in vectors]).reshape(1, NSMALL)
        wq, wo, wf, wp = [lax.all_gather(w, "fsdp", axis=0, tiled=True) for w in ws]
        small8 = lax.all_gather(row, "fsdp", axis=0, tiled=True)
        qkv, a_t, small = ln_qkv(tokens, latent, latent_flags, small8, wq)
        o, lse = attn_fwd(segment_ids, qkv)
        out, dr, do, gffn, gsm = ffn(tokens, latent, latent_flags, small, o, cotangent, wo, wf, wp)
        dqkv = attn_bwd(segment_ids, qkv, do, lse)
        gin, gq, gsm = last(tokens, latent, latent_flags, small, gsm, dr, dqkv, a_t, wq)

        def scatter(v):
            part = lax.psum_scatter(v, "fsdp", scatter_dimension=0, tiled=True)
            return lax.psum(part, "rep")

        tq, tp, tf, to = [scatter(v) for v in (gq, gffn[:, :FF], gffn[:, FF:2 * FF], gffn[:, 2 * FF:])]
        tq, to, tf, tp = tq.astype(F32), to.astype(F32).T, tf.astype(F32), tp.astype(F32).T
        gsm = lax.psum(gsm, ("rep", "fsdp"))
        v = [mine(gsm, at, v) for at, v in zip((G1, S1, BQ, BO, G2, S2, BF, BP), vectors)]
    return (out, gin, v[0], v[1], tq, v[2], to, v[3], v[4], v[5], tf, v[6], tp, v[7])


def solution(mesh):
    fast = mesh.shape["rep"] == 4 and mesh.shape["fsdp"] == 8
    both = P(("rep", "fsdp"), None)
    one, row, col = P("fsdp"), P("fsdp", None), P(None, "fsdp")
    return jax.shard_map(
        partial(shards, fast),
        mesh=mesh,
        in_specs=(both, both, both, both, one, one, row, one, col, one, one, one, row, one, col, one, both),
        out_specs=(both, both, one, one, row, one, col, one, one, one, row, one, col, one),
        check_vma=False,
    )
```

```python
from functools import partial

import jax
import jax.numpy as jnp
from jax import lax
from jax.experimental import pallas as pl
from jax.experimental.pallas import tpu as pltpu
from jax.sharding import PartitionSpec as P

D = 768
FF = 3072
NSMALL = 9216
NFFN = 6912
EPS = 1e-05
NEG = -1e30
G1, S1, BQ, BV, BO, G2, S2, BF, BP = 0, 768, 1536, 2304, 3072, 3840, 4608, 5376, 8448
F32 = jnp.float32
BF16 = jnp.bfloat16
VLIM = 60 << 20


def nn(a, b):
    return jnp.dot(a, b, preferred_element_type=F32)


def nt(a, b):
    return lax.dot_general(a, b, (((1,), (1,)), ((), ())), preferred_element_type=F32)


def norm_stats(x):
    mean = jnp.mean(x, axis=-1, keepdims=True)
    center = x - mean
    var = jnp.mean(center * center, axis=-1, keepdims=True)
    rs = lax.rsqrt(var + EPS)
    return center * rs, rs


def pick_rows(flags_row, tok, lat):
    t = flags_row.shape[1]
    col = jnp.broadcast_to(flags_row.astype(F32), (128, t)).T
    wide = jnp.concatenate([col] * (D // 128), axis=1)
    return jnp.where(wide > 0.5, lat.astype(F32), tok.astype(F32))


def ln_qkv_kernel(tok, lat, flags, small8, wq, qkv, a_t, small):
    sm = jnp.sum(small8[...].astype(F32), axis=0, keepdims=True)

    @pl.when(pl.program_id(0) == 0)
    def _():
        small[...] = sm

    x = pick_rows(flags[...], tok[...], lat[...])
    xh, _ = norm_stats(x)
    a = (xh * sm[:, G1:G1 + D] + sm[:, S1:S1 + D]).astype(BF16)
    a_t[...] = a.T
    for i in range(3):
        y = nn(a, wq[:, i * D:(i + 1) * D])
        if i == 0:
            y = y + sm[:, BQ:BQ + D]
        if i == 2:
            y = y + sm[:, BV:BV + D]
        qkv[i] = y.astype(BF16)


def ln_qkv(tok, lat, flags, small8, wq):
    n = tok.shape[0]
    t = 256
    return pl.pallas_call(
        ln_qkv_kernel,
        grid=(n // t,),
        in_specs=[
            pl.BlockSpec((t, D), lambda i: (i, 0)),
            pl.BlockSpec((t, D), lambda i: (i, 0)),
            pl.BlockSpec((1, t), lambda i: (0, i)),
            pl.BlockSpec(small8.shape, lambda i: (0, 0)),
            pl.BlockSpec((D, 3 * D), lambda i: (0, 0)),
        ],
        out_specs=[
            pl.BlockSpec((3, t, D), lambda i: (0, i, 0)),
            pl.BlockSpec((D, t), lambda i: (0, i)),
            pl.BlockSpec((1, NSMALL), lambda i: (0, 0)),
        ],
        out_shape=[
            jax.ShapeDtypeStruct((3, n, D), BF16),
            jax.ShapeDtypeStruct((D, n), BF16),
            jax.ShapeDtypeStruct((1, NSMALL), F32),
        ],
        compiler_params=pltpu.CompilerParams(vmem_limit_bytes=VLIM),
        name="ln_qkv",
    )(tok, lat, flags, small8, wq)


TQ = 256


def span(t):
    lo = max(0, t - 2)
    return lo * TQ, (t + 1 - lo) * TQ


def doc_starts(seg):
    st = jnp.zeros(seg.shape, jnp.int32)
    for s in range(1, 8):
        cnt = jnp.sum((seg < s).astype(jnp.int32), axis=1, keepdims=True)
        st = jnp.where(seg == s, cnt, st)
    return st


def build_bias(seg_ref, bias):
    st = doc_starts(seg_ref[...])
    for t in range(4):
        lo, size = span(t)
        j = lax.broadcasted_iota(jnp.int32, (size, TQ), 0) + lo
        i = lax.broadcasted_iota(jnp.int32, (size, TQ), 1) + t * TQ
        ok = jnp.logical_and(j >= st[:, t * TQ:(t + 1) * TQ], j <= i)
        bias[t, 0:size, :] = jnp.where(ok, 0.0, NEG)


def attn_fwd_kernel(seg_ref, qkv, o, lse, bias):
    @pl.when(pl.program_id(0) == 0)
    def _():
        build_bias(seg_ref, bias)

    qt = (qkv[0] * 0.125).T
    vt = qkv[2].T
    k = qkv[1]
    lane = lax.broadcasted_iota(jnp.int32, k.shape, 1)
    zero = jnp.zeros_like(k)
    ks = [jnp.where(lane < 64, k, zero), jnp.where(lane < 64, zero, k)]
    for t in range(4):
        lo, size = span(t)
        outs = []
        for h in range(2):
            s = nn(ks[h][lo:lo + size], qt[:, t * TQ:(t + 1) * TQ]) + bias[t, 0:size, :]
            m = jnp.max(s, axis=0, keepdims=True)
            p = jnp.exp(s - m)
            l = jnp.sum(p, axis=0, keepdims=True)
            ot = nn(vt[h * 64:(h + 1) * 64, lo:lo + size], p.astype(BF16))
            outs.append(ot * (1.0 / l))
            lse[0, h:h + 1, t * TQ:(t + 1) * TQ] = m + jnp.log(l)
        o[t * TQ:(t + 1) * TQ, :] = jnp.concatenate(outs, axis=0).T.astype(BF16)


def attn_fwd(seg, qkv):
    n = qkv.shape[1]
    return pl.pallas_call(
        attn_fwd_kernel,
        grid=(6,),
        in_specs=[
            pl.BlockSpec((1, n), lambda p: (0, 0)),
            pl.BlockSpec((3, n, 128), lambda p: (0, 0, p)),
        ],
        out_specs=[
            pl.BlockSpec((n, 128), lambda p: (0, p)),
            pl.BlockSpec((1, 2, n), lambda p: (p, 0, 0)),
        ],
        out_shape=[
            jax.ShapeDtypeStruct((n, D), BF16),
            jax.ShapeDtypeStruct((6, 2, n), F32),
        ],
        scratch_shapes=[pltpu.VMEM((4, 768, TQ), F32)],
        compiler_params=pltpu.CompilerParams(vmem_limit_bytes=VLIM),
        name="attn_fwd",
    )(seg, qkv)


C0 = 0.7978845608028654
C1 = 0.044715
TR = 512
TC = 512


def ffn_kernel(tok, lat, flags, small, o_h, cot_h, wo_h, wf_h, wp_h,
               out_h, dr_h, do_h, gffn_h, gsmall,
               o, cot, wo, wf, wp, gs, dfs, ct, ht, dyt, xs, rs_s, outs, dos, gwo, gwf, gwp, isem, osem):
    n = o.shape[0]
    ins = [pltpu.make_async_copy(a, b, isem.at[i]) for i, (a, b) in enumerate(
        [(o_h, o), (wo_h, wo), (cot_h, cot), (wf_h, wf), (wp_h, wp)])]
    for c in ins:
        c.start()
    gsmall[...] = jnp.zeros_like(gsmall)
    ins[0].wait()
    ins[1].wait()
    ins[2].wait()
    ins[3].wait()
    ins[4].wait()

    def row_tile(i, carry):
        r0 = pl.multiple_of(i * TR, TR)
        rows = pl.ds(r0, TR)
        x = pick_rows(flags[:, rows], tok[rows, :], lat[rows, :])
        r = x + nt(o[rows, :], wo[...]) + small[:, BO:BO + D]
        rh, rs = norm_stats(r)
        h = (rh * small[:, G2:G2 + D] + small[:, S2:S2 + D]).astype(BF16)
        ht[:, rows] = h.T
        c_t = cot[rows, :]
        ct[:, rows] = c_t.T
        gsmall[:, BP:BP + D] += jnp.sum(c_t.astype(F32), axis=0, keepdims=True)

        xs[...] = jnp.zeros_like(xs)
        rs_s[...] = jnp.zeros_like(rs_s)

        def col_tile(j, cc):
            c0 = pl.multiple_of(j * TC, TC)
            cols = pl.ds(c0, TC)
            f = nn(h, wf[:, cols]) + small[:, pl.ds(pl.multiple_of(BF + c0, 128), TC)]
            u = nn(c_t, wp[:, cols])
            f2 = f * f
            th = jnp.tanh(f * (C0 + (C0 * C1) * f2))
            hp = 0.5 + 0.5 * th
            g = f * hp
            gp = hp + (g * (2.0 - 2.0 * hp)) * (C0 + (3.0 * C0 * C1) * f2)
            gb = g.astype(BF16)
            df = (u * gp).astype(BF16)
            gs[rows, cols] = gb
            dfs[rows, cols] = df
            sl = pl.ds(pl.multiple_of(BF + c0, 128), TC)
            gsmall[:, sl] += jnp.sum(df.astype(F32), axis=0, keepdims=True)
            xs[...] += nt(gb, wp[:, cols])
            rs_s[...] += nt(df, wf[:, cols])
            return cc

        lax.fori_loop(0, FF // TC, col_tile, 0)
        outs[rows, :] = (r + xs[...] + small[:, BP:BP + D]).astype(BF16)
        dh = rs_s[...]
        gsmall[:, G2:G2 + D] += jnp.sum(dh * rh, axis=0, keepdims=True)
        gsmall[:, S2:S2 + D] += jnp.sum(dh, axis=0, keepdims=True)
        e = dh * small[:, G2:G2 + D]
        dr = c_t.astype(F32) + rs * (e - jnp.mean(e, axis=-1, keepdims=True) - rh * jnp.mean(e * rh, axis=-1, keepdims=True))
        dy = dr.astype(BF16)
        gsmall[:, BO:BO + D] += jnp.sum(dy.astype(F32), axis=0, keepdims=True)
        dyt[:, rows] = dy.T
        xs[...] = dr
        cp = pltpu.make_async_copy(xs, dr_h.at[rows, :], isem.at[0])
        cp.start()
        dos[rows, :] = nn(dy, wo[...]).astype(BF16)
        cp.wait()
        return carry

    lax.fori_loop(0, n // TR, row_tile, 0)
    c1 = pltpu.make_async_copy(outs, out_h, osem.at[0])
    c1.start()
    c2 = pltpu.make_async_copy(dos, do_h, osem.at[1])
    c2.start()

    def grad_tile(j, cc):
        cols = pl.ds(pl.multiple_of(j * TC, TC), TC)
        gwp[:, cols] = nn(ct[...], gs[:, cols]).astype(BF16)
        gwf[:, cols] = nn(ht[...], dfs[:, cols]).astype(BF16)
        return cc

    lax.fori_loop(0, FF // TC, grad_tile, 0)
    c3 = pltpu.make_async_copy(gwp, gffn_h.at[:, 0:FF], osem.at[2])
    c3.start()
    c4 = pltpu.make_async_copy(gwf, gffn_h.at[:, FF:2 * FF], osem.at[3])
    c4.start()

    def gwo_tile(j, cc):
        cols = pl.ds(pl.multiple_of(j * 256, 256), 256)
        gwo[:, cols] = nn(dyt[...], o[:, cols]).astype(BF16)
        return cc

    lax.fori_loop(0, D // 256, gwo_tile, 0)
    c5 = pltpu.make_async_copy(gwo, gffn_h.at[:, 2 * FF:], osem.at[4])
    c5.start()
    for c in (c1, c2, c3, c4, c5):
        c.wait()


def ffn(tok, lat, flags, small, o, cot, wo, wf, wp):
    n = tok.shape[0]
    anyspec = pl.BlockSpec(memory_space=pl.ANY)
    vspec = pl.BlockSpec(memory_space=pltpu.VMEM)
    return pl.pallas_call(
        ffn_kernel,
        in_specs=[vspec] * 4 + [anyspec] * 5,
        out_specs=[anyspec] * 4 + [vspec],
        out_shape=[
            jax.ShapeDtypeStruct((n, D), BF16),
            jax.ShapeDtypeStruct((n, D), F32),
            jax.ShapeDtypeStruct((n, D), BF16),
            jax.ShapeDtypeStruct((D, NFFN), BF16),
            jax.ShapeDtypeStruct((1, NSMALL), F32),
        ],
        scratch_shapes=[
            pltpu.VMEM((n, D), BF16),
            pltpu.VMEM((n, D), BF16),
            pltpu.VMEM((D, D), BF16),
            pltpu.VMEM((D, FF), BF16),
            pltpu.VMEM((D, FF), BF16),
            pltpu.VMEM((n, FF), BF16),
            pltpu.VMEM((n, FF), BF16),
            pltpu.VMEM((D, n), BF16),
            pltpu.VMEM((D, n), BF16),
            pltpu.VMEM((D, n), BF16),
            pltpu.VMEM((TR, D), F32),
            pltpu.VMEM((TR, D), F32),
            pltpu.VMEM((n, D), BF16),
            pltpu.VMEM((n, D), BF16),
            pltpu.VMEM((D, D), BF16),
            pltpu.VMEM((D, FF), BF16),
            pltpu.VMEM((D, FF), BF16),
            pltpu.SemaphoreType.DMA((5,)),
            pltpu.SemaphoreType.DMA((5,)),
        ],
        compiler_params=pltpu.CompilerParams(vmem_limit_bytes=VLIM),
        name="ffn",
    )(tok, lat, flags, small, o, cot, wo, wf, wp)


def attn_bwd_kernel(seg_ref, qkv, do, lse, dqkv, bias, dk_acc, dv_acc):
    @pl.when(pl.program_id(0) == 0)
    def _():
        build_bias(seg_ref, bias)

    q8 = qkv[0] * 0.125
    qt = q8.T
    k = qkv[1]
    kt = k.T
    v = qkv[2]
    d = do[...]
    dt = d.T
    lane = lax.broadcasted_iota(jnp.int32, k.shape, 1)
    zero = jnp.zeros_like(k)
    ks = [jnp.where(lane < 64, k, zero), jnp.where(lane < 64, zero, k)]
    vs = [jnp.where(lane < 64, v, zero), jnp.where(lane < 64, zero, v)]
    dk_acc[...] = jnp.zeros_like(dk_acc)
    dv_acc[...] = jnp.zeros_like(dv_acc)
    for t in range(4):
        lo, size = span(t)
        tq = slice(t * TQ, (t + 1) * TQ)
        dqs, dks, dvs = [], [], []
        for h in range(2):
            s = nn(ks[h][lo:lo + size], qt[:, tq]) + bias[t, 0:size, :]
            p = jnp.exp(s - lse[0, h:h + 1, tq])
            dp = nn(vs[h][lo:lo + size], dt[:, tq])
            dd = jnp.sum(dp * p, axis=0, keepdims=True)
            ds = (p * (dp - dd)).astype(BF16)
            dvs.append(nn(p.astype(BF16), d[tq, :]))
            dks.append(nn(ds, q8[tq, :]))
            dqs.append(nn(kt[h * 64:(h + 1) * 64, lo:lo + size], ds))
        lane2 = lax.broadcasted_iota(jnp.int32, (size, 128), 1)
        dk_acc[lo:lo + size, :] += jnp.where(lane2 < 64, dks[0], dks[1])
        dv_acc[lo:lo + size, :] += jnp.where(lane2 < 64, dvs[0], dvs[1])
        dqkv[0, tq, :] = (jnp.concatenate(dqs, axis=0).T * 0.125).astype(BF16)
    dqkv[1] = dk_acc[...].astype(BF16)
    dqkv[2] = dv_acc[...].astype(BF16)


def attn_bwd(seg, qkv, do, lse):
    n = qkv.shape[1]
    return pl.pallas_call(
        attn_bwd_kernel,
        grid=(6,),
        in_specs=[
            pl.BlockSpec((1, n), lambda p: (0, 0)),
            pl.BlockSpec((3, n, 128), lambda p: (0, 0, p)),
            pl.BlockSpec((n, 128), lambda p: (0, p)),
            pl.BlockSpec((1, 2, n), lambda p: (p, 0, 0)),
        ],
        out_specs=pl.BlockSpec((3, n, 128), lambda p: (0, 0, p)),
        out_shape=jax.ShapeDtypeStruct((3, n, D), BF16),
        scratch_shapes=[
            pltpu.VMEM((4, 768, TQ), F32),
            pltpu.VMEM((n, 128), F32),
            pltpu.VMEM((n, 128), F32),
        ],
        compiler_params=pltpu.CompilerParams(vmem_limit_bytes=VLIM),
        name="attn_bwd",
    )(seg, qkv, do, lse)


def last_body(tok, lat, flags, small, gsm_in, dr, dqkv, a_t, wq, gin, gwq, gsmall):
    i = pl.program_id(0)
    t = 256

    @pl.when(i == 0)
    def _():
        gsmall[...] = gsm_in[...]

    rows = pl.ds(pl.multiple_of(i * t, t), t)
    x = pick_rows(flags[:, rows], tok[rows, :], lat[rows, :])
    xh, rs = norm_stats(x)
    d0, d1, d2 = dqkv[0, rows, :], dqkv[1, rows, :], dqkv[2, rows, :]
    da = nt(d0, wq[:, 0:D]) + nt(d1, wq[:, D:2 * D]) + nt(d2, wq[:, 2 * D:3 * D])
    gsmall[:, G1:G1 + D] += jnp.sum(da * xh, axis=0, keepdims=True)
    gsmall[:, S1:S1 + D] += jnp.sum(da, axis=0, keepdims=True)
    gsmall[:, BQ:BQ + D] += jnp.sum(d0.astype(F32), axis=0, keepdims=True)
    gsmall[:, BV:BV + D] += jnp.sum(d2.astype(F32), axis=0, keepdims=True)
    e = da * small[:, G1:G1 + D]
    gin[...] = dr[...] + rs * (e - jnp.mean(e, axis=-1, keepdims=True) - xh * jnp.mean(e * xh, axis=-1, keepdims=True))
    ar = pl.ds(pl.multiple_of(i * 192, 192), 192)
    for c in range(3):
        gwq[:, c * D:(c + 1) * D] = nn(a_t[ar, :], dqkv[c]).astype(BF16)


def last(tok, lat, flags, small, gsm, dr, dqkv, a_t, wq):
    n = tok.shape[0]
    t = 256
    whole = lambda *s: pl.BlockSpec(s, lambda i: (0,) * len(s))
    return pl.pallas_call(
        last_body,
        grid=(n // t,),
        in_specs=[
            whole(n, D), whole(n, D), whole(1, n), whole(1, NSMALL), whole(1, NSMALL),
            pl.BlockSpec((t, D), lambda i: (i, 0)),
            whole(3, n, D), whole(D, n), whole(D, 3 * D),
        ],
        out_specs=[
            pl.BlockSpec((t, D), lambda i: (i, 0)),
            pl.BlockSpec((192, 3 * D), lambda i: (i, 0)),
            whole(1, NSMALL),
        ],
        out_shape=[
            jax.ShapeDtypeStruct((n, D), F32),
            jax.ShapeDtypeStruct((D, 3 * D), BF16),
            jax.ShapeDtypeStruct((1, NSMALL), F32),
        ],
        compiler_params=pltpu.CompilerParams(vmem_limit_bytes=VLIM),
        name="last",
    )(tok, lat, flags, small, gsm, dr, dqkv, a_t, wq)


MESH = pl.DeviceIdType.MESH
RQ = 24
NCH = 12
XB, DO, OO, CT_, HH, RH, GJ, DJ = range(8)
QS = (GJ, DO, DJ)
L1 = 5
R1 = 5
SCHEDULE = {
    "p0": (("F", 0),),
    "p1": (("S", 0), ("F", 2),),
    "p2": (("T", 0), ("F", 1),),
    "q0": (("S", 1), ("F", 3), ("F", 4),),
    "q1": (("T", 1), ("S", 2), ("S", 3), ("F", 5),),
    "q2": (("T", 2), ("T", 3), ("S", 4), ("F", 6),),
    "q3": (("S", 5), ("F", 7),),
    "q4": (("T", 4), ("T", 5), ("F", 8),),
    "q5": (("A", 3), ("S", 6),),
    "h0": (("A", 4), ("S", 7), ("S", 8), ("F", 9), ("F", 10),),
    "b0": (("T", 6), ("T", 7), ("T", 8),),
    "g0": (("S", 9),),
    "e0": (("A", 6), ("A", 7), ("S", 10), ("F", 11),),
    "b1": (("2", 0), ("2", 1), ("T", 9), ("S", 11),),
    "g1": (("A", 8),),
    "e1": (("T", 10),),
    "b2": (("2", 2), ("T", 11), ("3", 0),),
    "g2": (("2", 3), ("A", 10),),
    "e2": (("A", 11), ("3", 1),),
    "b3": (("2", 4), ("2", 5),),
    "g3": (("4", 0), ("3", 2),),
    "t0": (("2", 6), ("3", 3),),
    "t1a": (("A", 5), ("4", 1), ("3", 4), ("3", 5), ("5", 0),),
    "t1": (("2", 7),),
    "r0": (("2", 8), ("4", 2),),
    "r1": (("4", 3), ("3", 6),),
    "r2": (("2", 9), ("4", 4), ("3", 7),),
    "r3": (("4", 5), ("5", 2), ("5", 3), ("5", 4),),
    "r4": (("2", 10), ("4", 6), ("4", 7), ("3", 8), ("3", 9), ("5", 5),),
    "r5": (("5", 6),),
    "s0": (("A", 9), ("3", 10),),
    "s1": (("2", 11), ("4", 8), ("4", 9), ("5", 1),),
    "s2": (("5", 7),),
    "s3": (("4", 10), ("5", 8),),
    "u0": (("3", 11),),
    "u1": (("5", 9), ("5", 10), ("5", 11),),
}


def remote(a, b, ssem, rsem, rr, ff):
    return pltpu.make_async_remote_copy(src_ref=a, dst_ref=b, send_sem=ssem, recv_sem=rsem,
                                        device_id=(rr, ff), device_id_type=MESH)


def layer_kernel(sq, so, sf, sp, v0, v1, v2, v3, v4, v5, v6, v7, tok_h, lat_h, cot_h, flags, seg,
                 g, qkv_h, out_h, gin_h, fin, gsm_out,
                 ss, small8, small, lse, pool, tr, w, acc_o, acc_d, l1, snd, r1, r2e, r2o, r3, r4, rd, dka, dva, gsm, sbuf, srcv,
                 z_s, z_r, x_s, x_r, y_s, y_r, dx_s, dx_r, dy_s, dy_r, c_s, c_r, own_s, own_r, sm_s, sm_r, loc,
                 ld, wl, st, a_s, a_r, b_s, b_r, d_s, d_r, e_s, e_r, h_s, h_r, w_s, w_r, m_s, m_r):
    r = lax.axis_index("rep")
    f = lax.axis_index("fsdp")
    c, z, x, y = f & 1, f >> 1, r & 1, r >> 1
    n = tok_h.shape[0]
    t = 256
    loads = [pltpu.make_async_copy(s, pool.at[i], ld.at[i]) for i, s in ((XB, tok_h), (DJ, lat_h), (CT_, cot_h))]
    for cp in loads:
        cp.start()
    pieces = []
    for v in (v0, v1, v2, v3, v4, v5, v6, v7):
        val = v[...].astype(F32).reshape(1, -1)
        pieces += [jnp.where(f == d, val, 0.0) for d in range(8)]
    ss[...] = jnp.concatenate(pieces, axis=1).astype(BF16)
    bar = pltpu.get_barrier_semaphore()
    for d in range(1, 8):
        pl.semaphore_signal(bar, inc=1, device_id=(r, f ^ d), device_id_type=MESH)
    for d in (1, 2, 3):
        pl.semaphore_signal(bar, inc=1, device_id=(r ^ d, f), device_id_type=MESH)
    pl.semaphore_wait(bar, 10)

    def rows_of(q):
        return pl.ds(pl.multiple_of(c * 96 + q * RQ, 8), RQ)

    def source(k):
        if k < 3:
            return [(sq, slice(b * D + k * 256, b * D + (k + 1) * 256), slice(b * 256, (b + 1) * 256)) for b in range(3)]
        if k == 3:
            return [(so, slice(0, D), slice(0, D))]
        i = (k - 4) // 2
        return [((sf, sp)[k % 2], slice(i * D, (i + 1) * D), slice(0, D))]

    def issue(k):
        quarter = pl.ds(pl.multiple_of(r * RQ, 8), RQ)
        mine = pl.ds(pl.multiple_of(c * 96, 8), 96)
        for ref, cols, to in source(k):
            for d in (1, 2, 3):
                remote(ref.at[quarter, cols], g.at[k, d, rows_of(r), to], z_s.at[k], z_r.at[k], r, f ^ (2 * d)).start()
        for ref, cols, to in source(k):
            remote(ref.at[:, cols], g.at[k, 0, mine, to], own_s.at[k], own_r.at[k], r, f ^ 1).start()
            pltpu.make_async_copy(ref.at[:, cols], g.at[k, 0, mine, to], loc.at[k]).start()

    def group(k, q):
        return g.at[k, 1:4, rows_of(q)]

    def half(k, q, h):
        return g.at[k, 1:4, rows_of(q), h * 384:(h + 1) * 384]

    def core(k, q):
        p = group(k, q)
        remote(p, p, c_s.at[k], c_r.at[k], r, f ^ 1).start()

    def got(ref, ssem, rsem):
        remote(ref, ref, ssem, rsem, r, f).wait_recv()

    def sent(ref, ssem, rsem):
        remote(ref, ref, ssem, rsem, r, f).wait_send()

    def first(k):
        p = group(k, r)
        got(p, z_s.at[k], z_r.at[k])
        remote(p, p, x_s.at[k], x_r.at[k], r ^ 1, f).start()
        remote(p, p, y_s.at[k], y_r.at[k], r ^ 2, f).start()
        core(k, r)

    def second(k):
        got(group(k, r ^ 1), x_s.at[k], x_r.at[k])
        h = half(k, r ^ 1, 0)
        remote(h, h, dy_s.at[k], dy_r.at[k], r ^ 2, f).start()
        core(k, r ^ 1)
        got(group(k, r ^ 2), y_s.at[k], y_r.at[k])
        h = half(k, r ^ 2, 1)
        remote(h, h, dx_s.at[k], dx_r.at[k], r ^ 1, f).start()
        core(k, r ^ 2)

    def third(k):
        got(half(k, r ^ 3, 0), dy_s.at[k], dy_r.at[k])
        got(half(k, r ^ 3, 1), dx_s.at[k], dx_r.at[k])
        core(k, r ^ 3)

    def own_rows(k):
        return g.at[k, 0, 0:96]

    def other_rows(k):
        return g.at[k, 1:4, 0:96]

    def arrived(k):
        got(own_rows(k), own_s.at[k], own_r.at[k])
        got(other_rows(k), c_s.at[k], c_r.at[k])
        pltpu.make_async_copy(own_rows(k), own_rows(k), loc.at[k]).wait()

    def wload(k, slot):
        for d in range(4):
            rows = pl.ds(pl.multiple_of((z ^ d) * 192, 64), 192)
            pltpu.make_async_copy(g.at[k, d], w.at[slot, rows], wl.at[slot]).start()

    def wwait(slot):
        pltpu.make_async_copy(w.at[slot], w.at[slot], wl.at[slot]).wait()

    for d in range(1, 8):
        remote(ss, small8.at[f], sm_s.at[d - 1], sm_r.at[d - 1], r, f ^ d).start()
    own_row = pltpu.make_async_copy(ss, small8.at[f], ld.at[1])
    own_row.start()
    issue(0)

    def build_blocks():
        row = doc_starts(seg[...])
        for q in range(4):
            lo, size = span(q)
            for b in range(size // TQ):
                jj = lax.broadcasted_iota(jnp.int32, (TQ, TQ), 0) + (lo + b * TQ)
                ii = lax.broadcasted_iota(jnp.int32, (TQ, TQ), 1) + q * TQ
                ok = jnp.logical_and(jj >= row[:, q * TQ:(q + 1) * TQ], jj <= ii)
                acc_o[q * TQ:(q + 1) * TQ, b * TQ:(b + 1) * TQ] = jnp.where(ok, 0.0, NEG)

    def blocks(q):
        size = span(q)[1]
        return jnp.concatenate([acc_o[q * TQ:(q + 1) * TQ, b * TQ:(b + 1) * TQ] for b in range(size // TQ)], axis=0)

    build_blocks()
    gsm[...] = jnp.zeros_like(gsm)
    own_row.wait()
    for d in range(1, 8):
        remote(ss, small8.at[f ^ d], sm_s.at[d - 1], sm_r.at[d - 1], r, f).wait()
    small[...] = jnp.sum(small8[...].astype(F32), axis=0)
    issue(1)
    for cp in loads:
        cp.wait()

    def put_t(ts, val, cols):
        for o in range(8):
            tr[ts, (o & 1) ^ c, o >> 1, :, cols] = val[o * 96:(o + 1) * 96]

    def addsum(at, v):
        gsm[:, at:at + v.shape[1]] += jnp.sum(v, axis=0, keepdims=True)

    def ln_tile(i, cc):
        rows = pl.ds(pl.multiple_of(i * t, t), t)
        xv = pick_rows(flags[:, rows], pool[XB, rows, :], pool[DJ, rows, :])
        pool[XB, rows, :] = xv.astype(BF16)
        xh, _ = norm_stats(xv)
        a = (xh * small[:, G1:G1 + D] + small[:, S1:S1 + D]).astype(BF16)
        pool[HH, rows, :] = a
        put_t(3, a.T, rows)
        return cc

    def turn_tile(i, cc):
        rows = pl.ds(pl.multiple_of(i * t, t), t)
        cv = pool[CT_, rows, :]
        put_t(0, cv.T, rows)
        addsum(BP, cv.astype(F32))
        return cc

    def normalise(k):
        lax.fori_loop(2 * k, 2 * k + 2, ln_tile, 0)

    def project(m):
        wload(m, m)
        at = pl.multiple_of(m * 256, 256)
        row = jnp.concatenate([small[:, pl.ds(BQ + at, 256)], jnp.zeros((1, 256), F32), small[:, pl.ds(BV + at, 256)]], axis=1)
        wwait(m)
        for j in range(n // 512):
            rows = slice(j * 512, (j + 1) * 512)
            v = (nn(pool[HH, rows, :], w[m]) + row).astype(BF16)
            for b in range(3):
                pool[QS[b], rows, pl.ds(at, 256)] = v[:, b * 256:(b + 1) * 256]

    here = set()

    def load_of(k):
        slot = 4 if k == 3 else 2 * ((k - 4) // 2 % 2) + k % 2
        if k not in here:
            here.add(k)
            arrived(k)
            wload(k, slot)

    def at(point):
        for name, k in SCHEDULE.get(point, ()):
            if name == "F":
                first(k)
                if k + 2 < NCH:
                    issue(k + 2)
            elif name == "S":
                second(k)
            elif name == "T":
                third(k)
            elif name == "A":
                load_of(k)
            elif k == NCH - 1 and name in "23":
                (dgo2 if name == "2" else dgo3)(k)
            else:
                {"2": go2, "3": go3, "4": go4, "5": go5}[name](k // 2, k % 2)

    def at_one(index, names):
        for i, name in enumerate(names):
            @pl.when(index == i)
            def _(name=name):
                at(name)

    lax.fori_loop(0, n // t, turn_tile, 0)
    at("p0")
    normalise(0)
    at("p1")
    normalise(1)
    at("p2")

    def by_head(v):
        lane = lax.broadcasted_iota(jnp.int32, v.shape, 1)
        zero = jnp.zeros_like(v)
        return jnp.where(lane < 64, v, zero), jnp.where(lane < 64, zero, v)

    def by_head_t(v):
        row = lax.broadcasted_iota(jnp.int32, v.shape, 0)
        zero = jnp.zeros_like(v)
        return jnp.where(row < 64, v, zero), jnp.where(row < 64, zero, v)

    def stack(two, q):
        lo, size = span(q)
        return jnp.concatenate([v[lo:lo + size] for v in two], axis=0)

    def beside(two, q):
        lo, size = span(q)
        return jnp.concatenate([v[:, lo:lo + size] for v in two], axis=1)

    def pair_fwd(p, cc):
        @pl.when(lax.rem(p, 2) == 0)
        def _():
            m = p // 2
            arrived(m)
            project(m)

        cols = pl.ds(pl.multiple_of(p * 128, 128), 128)
        qt = (pool[QS[0], :, cols] * 0.125).T
        vts = by_head_t(pool[QS[2], :, cols].T)
        ks = by_head(pool[QS[1], :, cols])

        def scores(q):
            return nn(stack(ks, q), qt[:, q * TQ:(q + 1) * TQ])

        def soft(q, s):
            size = span(q)[1]
            bias = blocks(q)
            es, inv = [], []
            for h in range(2):
                sh = s[h * size:(h + 1) * size] + bias
                m = jnp.max(sh, axis=0, keepdims=True)
                e = jnp.exp(sh - m)
                l = jnp.sum(e, axis=0, keepdims=True)
                lse[p, h:h + 1, q * TQ:(q + 1) * TQ] = m + jnp.log(l)
                es.append(e.astype(BF16))
                inv.append(1.0 / l)
            return jnp.concatenate(es, axis=0), inv

        def mix(q, e, inv):
            ot = nn(beside(vts, q), e)
            ot = jnp.concatenate([ot[0:64] * inv[0], ot[64:128] * inv[1]], axis=0)
            pool[OO, q * TQ:(q + 1) * TQ, cols] = ot.T.astype(BF16)

        s, before = scores(0), None
        for q in range(4):
            ahead = scores(q + 1) if q < 3 else None
            after = soft(q, s)
            if before is not None:
                mix(*before)
            before, s = (q,) + after, ahead
        mix(*before)
        at_one(p, ["q%d" % i for i in range(6)])
        return cc

    lax.fori_loop(0, 6, pair_fwd, 0)
    for m in range(3):
        pltpu.make_async_copy(pool.at[QS[m]], qkv_h.at[m], st.at[m]).start()
    load_of(3)

    def xcols(v):
        return pl.ds(pl.multiple_of(v * 384, 128), 384)

    def num(kh, par):
        return 2 * kh + par

    def hop1(k):
        return remote(snd.at[lax.rem(k, 2)], r1.at[lax.rem(k, R1)], a_s.at[k], a_r.at[k], r, f ^ 1)

    def hop2(kh, par):
        k = num(kh, par)
        slot = lax.rem(k, L1)
        if par == 0:
            return remote(l1.at[slot, :, :, :, xcols(1 - x)], r2e.at[kh], b_s.at[k], b_r.at[k], r ^ 1, f)
        return remote(l1.at[slot, :, 1 - y], r2o.at[kh], b_s.at[k], b_r.at[k], r ^ 2, f)

    def hop3(kh, par):
        k = num(kh, par)
        if par == 0:
            return remote(r2e.at[kh, :, 1 - y], r3.at[k], d_s.at[k], d_r.at[k], r ^ 2, f)
        return remote(r2o.at[kh, :, :, xcols(1 - x)], r3.at[k], d_s.at[k], d_r.at[k], r ^ 1, f)

    def hop4(kh, par, d):
        k = num(kh, par)
        return remote(r3.at[k, z ^ d], r4.at[k, d - 1], e_s.at[k, d - 1], e_r.at[k, d - 1], r, f ^ (2 * d))

    def hop5(kh, par, d, far):
        k = num(kh, par)
        q = r ^ d if far else r
        ref = fin.at[k, q >> 1, q & 1]
        return remote(ref, ref, h_s.at[k, d - 1], h_r.at[k, d - 1], r ^ d, f)

    def go2(kh, par):
        k = num(kh, par)
        slot = lax.rem(k, L1)
        hop1(k).wait()

        def add(i, cc):
            l1[slot, i] = (l1[slot, i].astype(F32) + r1[lax.rem(k, R1), i].astype(F32)).astype(BF16)
            return cc

        lax.fori_loop(0, 4, add, 0)
        hop2(kh, par).start()

    def go3(kh, par):
        k = num(kh, par)
        slot = lax.rem(k, L1)
        hop2(kh, par).wait()

        def add(i, cc):
            if par == 0:
                r2e[kh, i] = (l1[slot, i, :, :, xcols(x)].astype(F32) + r2e[kh, i].astype(F32)).astype(BF16)
            else:
                r2o[kh, i] = (l1[slot, i, y].astype(F32) + r2o[kh, i].astype(F32)).astype(BF16)
            return cc

        lax.fori_loop(0, 4, add, 0)
        hop3(kh, par).start()

    def go4(kh, par):
        k = num(kh, par)
        hop3(kh, par).wait()

        def add(i, cc):
            own = r2e[kh, i, y] if par == 0 else r2o[kh, i, :, xcols(x)]
            r3[k, i] = (own.astype(F32) + r3[k, i].astype(F32)).astype(BF16)
            return cc

        lax.fori_loop(0, 4, add, 0)
        for d in (1, 2, 3):
            hop4(kh, par, d).start()

    def go5(kh, par):
        k = num(kh, par)
        total = r3[k, z].astype(F32)
        for d in (1, 2, 3):
            hop4(kh, par, d).wait()
            total = total + r4[k, d - 1].astype(F32)
        fin[k, y, x] = total.astype(BF16)
        for d in (1, 2, 3):
            hop5(kh, par, d, False).start()

    def go6(kh, par):
        for d in (1, 2, 3):
            hop5(kh, par, d, False).wait_send()
            hop5(kh, par, d, True).wait_recv()

    def own_add(k):
        slot = k % L1
        hop1(k).wait()

        def add(i, cc):
            l1[slot, i] = (l1[slot, i].astype(F32) + r1[k % R1, i].astype(F32)).astype(BF16)
            return cc

        lax.fori_loop(0, 4, add, 0)

    def direct(k, d):
        q = r ^ d
        return remote(l1.at[k % L1, :, q >> 1, :, xcols(q & 1)], rd.at[d - 1], w_s.at[d - 1], w_r.at[d - 1], q, f)

    def dgo2(k):
        own_add(k)
        for d in (1, 2, 3):
            direct(k, d).start()

    def dgo3(k):
        for d in (1, 2, 3):
            direct(k, d).wait()

        def add(i, cc):
            v = l1[k % L1, i, y, :, xcols(x)].astype(F32)
            for d in range(3):
                v = v + rd[d, i].astype(F32)
            r3[k, i] = v.astype(BF16)
            return cc

        lax.fori_loop(0, 4, add, 0)
        for d in (1, 2, 3):
            hop4(k // 2, k % 2, d).start()

    def grad_chunk(ts, rhs, k):
        slot, par = lax.rem(k, L1), lax.rem(k, 2)

        for i in range(3):
            cols = slice(i * 256, (i + 1) * 256)
            b = rhs(i)
            snd[par, :, :, :, cols] = nn(tr[ts, 1].reshape(384, n), b).astype(BF16).reshape(4, 2, 48, 256)
            l1[slot, :, :, :, cols] = nn(tr[ts, 0].reshape(384, n), b).astype(BF16).reshape(4, 2, 48, 256)
        hop1(k).start()

    wwait(4)

    def head(i, cc):
        rows = pl.ds(pl.multiple_of(i * t, t), t)
        rv = pool[XB, rows, :].astype(F32) + nt(pool[OO, rows, :], w[4]) + small[:, BO:BO + D]
        rh, rs = norm_stats(rv)
        dka[rows, :] = jnp.broadcast_to(rs, (t, 128))
        pool[RH, rows, :] = rh.astype(BF16)
        h = (rh * small[:, G2:G2 + D] + small[:, S2:S2 + D]).astype(BF16)
        pool[HH, rows, :] = h
        put_t(1, h.T, rows)
        acc_o[rows, :] = rv + small[:, BP:BP + D]
        acc_d[rows, :] = jnp.zeros((t, D), F32)
        return cc

    lax.fori_loop(0, 2, head, 0, unroll=2)
    at("h0")
    lax.fori_loop(2, 4, head, 0, unroll=2)
    at("h1")
    for m in range(3):
        pltpu.make_async_copy(pool.at[QS[m]], qkv_h.at[m], st.at[m]).wait()

    def ff_tile(j, cc):
        s0 = 2 * lax.rem(j, 2)
        for i in range(4):
            @pl.when(j == i)
            def _(i=i):
                load_of(4 + 2 * i)
                load_of(5 + 2 * i)

        wwait(s0)
        wwait(s0 + 1)
        bf = pl.ds(pl.multiple_of(BF + j * D, 128), D)
        shift = small[:, bf]

        def rows_at(i):
            return slice(i * t, (i + 1) * t)

        def products(i):
            return nn(pool[HH, rows_at(i), :], w[s0]) + shift, nn(pool[CT_, rows_at(i), :], w[s0 + 1])

        def gelu(i, fv, u):
            f2 = fv * fv
            th = jnp.tanh(fv * (C0 + (C0 * C1) * f2))
            hp = 0.5 + 0.5 * th
            gv = fv * hp
            gp = hp + (gv * (2.0 - 2.0 * hp)) * (C0 + (3.0 * C0 * C1) * f2)
            gb, df = gv.astype(BF16), (u * gp).astype(BF16)
            pool[GJ, rows_at(i), :] = gb
            pool[DJ, rows_at(i), :] = df
            return gb, df

        def gather_back(i, gb, df):
            acc_o[rows_at(i), :] += nt(gb, w[s0 + 1])
            acc_d[rows_at(i), :] += nt(df, w[s0])

        now, before = products(0), None
        sums = jnp.zeros((1, D), F32)
        for i in range(n // t):
            ahead = products(i + 1) if i + 1 < n // t else None
            gb, df = gelu(i, *now)
            sums = sums + jnp.sum(df.astype(F32), axis=0, keepdims=True)
            if before is not None:
                gather_back(*before)
            before, now = (i, gb, df), ahead
        gather_back(*before)
        gsm[:, bf] += sums

        at_one(j, ["b%d" % i for i in range(4)])
        grad_chunk(0, lambda i: pool[GJ, :, i * 256:(i + 1) * 256], 2 * j)
        at_one(j, ["g%d" % i for i in range(4)])
        grad_chunk(1, lambda i: pool[DJ, :, i * 256:(i + 1) * 256], 2 * j + 1)
        at_one(j, ["e%d" % i for i in range(4)])
        return cc

    lax.fori_loop(0, 4, ff_tile, 0)
    for i in range(3):
        wload(i, i)

    def tail(i, cc):
        rows = pl.ds(pl.multiple_of(i * t, t), t)
        pool[GJ, rows, :] = acc_o[rows, :].astype(BF16)
        dh = acc_d[rows, :]
        rh = pool[RH, rows, :].astype(F32)
        addsum(G2, dh * rh)
        addsum(S2, dh)
        e = dh * small[:, G2:G2 + D]
        dr = pool[CT_, rows, :].astype(F32) + dka[rows, 0:1] * (
            e - jnp.mean(e, axis=-1, keepdims=True) - rh * jnp.mean(e * rh, axis=-1, keepdims=True))
        acc_d[rows, :] = dr
        dy = dr.astype(BF16)
        addsum(BO, dy.astype(F32))
        put_t(2, dy.T, rows)
        pool[DO, rows, :] = nn(dy, w[4]).astype(BF16)
        return cc

    lax.fori_loop(0, n // t, tail, 0, unroll=2)
    oout = pltpu.make_async_copy(pool.at[GJ], out_h, st.at[0])
    oout.start()
    at("t0")
    grad_chunk(2, lambda i: pool[OO, :, i * 256:(i + 1) * 256], 8)
    at("t1a")
    qload = pltpu.make_async_copy(qkv_h, pool.at[pl.ds(OO, 3)], ld.at[0])
    qload.start()

    build_blocks()

    def xhat(rows):
        return norm_stats(pool[XB, rows, :].astype(F32))

    qload.wait()
    oout.wait()
    at("t1")

    def pair(p, cc):
        cols = pl.ds(pl.multiple_of(p * 128, 128), 128)
        q8 = pool[OO, :, cols] * 0.125
        qt = q8.T
        k = pool[OO + 1, :, cols]
        kts = by_head_t(k.T)
        ks = by_head(k)
        vs = by_head(pool[OO + 2, :, cols])
        dv = pool[DO, :, cols]
        dt = dv.T
        dka[...] = jnp.zeros_like(dka)
        dva[...] = jnp.zeros_like(dva)

        def scores(q):
            tq = slice(q * TQ, (q + 1) * TQ)
            return nn(stack(ks, q), qt[:, tq]), nn(stack(vs, q), dt[:, tq])

        def soft(q, s, dp):
            size = span(q)[1]
            tq = slice(q * TQ, (q + 1) * TQ)
            bias = blocks(q)
            ps, dss = [], []
            for h in range(2):
                sl = slice(h * size, (h + 1) * size)
                pr = jnp.exp(s[sl] + bias - lse[p, h:h + 1, tq])
                dd = jnp.sum(dp[sl] * pr, axis=0, keepdims=True)
                dss.append((pr * (dp[sl] - dd)).astype(BF16))
                ps.append(pr.astype(BF16))
            return jnp.concatenate(ps, axis=0), jnp.concatenate(dss, axis=0)

        def back(q, pr, ds):
            lo, size = span(q)
            tq = slice(q * TQ, (q + 1) * TQ)
            dvv, dkk = nn(pr, dv[tq, :]), nn(ds, q8[tq, :])
            dqt = nn(beside(kts, q), ds)
            lane = lax.broadcasted_iota(jnp.int32, (size, 128), 1)
            dka[lo:lo + size, :] += jnp.where(lane < 64, dkk[:size], dkk[size:])
            dva[lo:lo + size, :] += jnp.where(lane < 64, dvv[:size], dvv[size:])
            pool[RH, tq, cols] = (dqt.T * 0.125).astype(BF16)

        now, before = scores(0), None
        for q in range(4):
            ahead = scores(q + 1) if q < 3 else None
            after = soft(q, *now)
            if before is not None:
                back(*before)
            before, now = (q,) + after, ahead
        back(*before)
        pool[RH + 1, :, cols] = dka[...].astype(BF16)
        pool[RH + 2, :, cols] = dva[...].astype(BF16)

        @pl.when(lax.rem(p, 2) == 1)
        def _():
            m = p // 2
            grad_chunk(3, lambda b: pool[RH + b, :, pl.ds(pl.multiple_of(m * 256, 256), 256)], 9 + m)

        at_one(p, ["r%d" % i for i in range(6)])
        return cc

    lax.fori_loop(0, 6, pair, 0)

    for i in range(3):
        wwait(i)

    def last_tile(i, cc):
        rows = pl.ds(pl.multiple_of(i * t, t), t)
        xh, rs = xhat(rows)
        ds_ = [pool[RH + b, rows, :] for b in range(3)]
        da = sum(nt(jnp.concatenate([v[:, m * 256:(m + 1) * 256] for v in ds_], axis=1), w[m]) for m in range(3))
        addsum(G1, da * xh)
        addsum(S1, da)
        addsum(BQ, ds_[0].astype(F32))
        addsum(BV, ds_[2].astype(F32))
        e = da * small[:, G1:G1 + D]
        acc_d[rows, :] += rs * (e - jnp.mean(e, axis=-1, keepdims=True) - xh * jnp.mean(e * xh, axis=-1, keepdims=True))
        pltpu.make_async_copy(acc_d.at[rows, :], gin_h.at[rows, :], st.at[i]).start()
        at_one(i, ["s%d" % b for b in range(4)])
        return cc

    lax.fori_loop(0, 4, last_tile, 0)

    groups = (((r, f ^ 1),), tuple((r ^ d, f) for d in (1, 2, 3)), tuple((r, f ^ (2 * d)) for d in (1, 2, 3)))

    def small_hops(i):
        return [remote(sbuf.at[i], srcv.at[3 * i + j], m_s.at[3 * i + j], m_r.at[3 * i + j], *to) for j, to in enumerate(groups[i])]

    sbuf[0] = gsm[...]
    for cp in small_hops(0):
        cp.start()

    def drain(k, cc):
        sent(group(k, r), z_s.at[k], z_r.at[k])
        sent(group(k, r), x_s.at[k], x_r.at[k])
        sent(group(k, r), y_s.at[k], y_r.at[k])
        sent(half(k, r, 0), dx_s.at[k], dx_r.at[k])
        sent(half(k, r, 0), dy_s.at[k], dy_r.at[k])
        sent(own_rows(k), own_s.at[k], own_r.at[k])
        sent(other_rows(k), c_s.at[k], c_r.at[k])
        return cc

    lax.fori_loop(0, NCH, drain, 0)
    for i in range(3):
        v = sbuf[i]
        for j, cp in enumerate(small_hops(i)):
            cp.wait()
            v = v + srcv[3 * i + j]
        if i < 2:
            sbuf[i + 1] = v
            for cp in small_hops(i + 1):
                cp.start()
        else:
            gsm_out[...] = v
        at("u%d" % i)
    at("end")
    for k in range(NCH):
        go6(k // 2, k % 2)
    for i in range(4):
        rows = pl.ds(i * t, t)
        pltpu.make_async_copy(acc_d.at[rows, :], gin_h.at[rows, :], st.at[i]).wait()


def layer(ws, vectors, tok, lat, cot, flags, seg):
    dma = pltpu.SemaphoreType.DMA
    n = tok.shape[0]
    anyspec = pl.BlockSpec(memory_space=pl.ANY)
    vspec = pl.BlockSpec(memory_space=pltpu.VMEM)
    vmem = pltpu.VMEM
    return pl.pallas_call(
        layer_kernel,
        in_specs=[vspec] * 12 + [anyspec] * 3 + [vspec] * 2,
        out_specs=[anyspec] * 4 + [vspec] * 2,
        out_shape=[
            jax.ShapeDtypeStruct((NCH, 4, 192, D), BF16),
            jax.ShapeDtypeStruct((3, n, D), BF16),
            jax.ShapeDtypeStruct((n, D), BF16),
            jax.ShapeDtypeStruct((n, D), F32),
            jax.ShapeDtypeStruct((NCH, 2, 2, 48, 384), BF16),
            jax.ShapeDtypeStruct((1, NSMALL), F32),
        ],
        scratch_shapes=[
            vmem((1, NSMALL), BF16), vmem((8, 1, NSMALL), BF16), vmem((1, NSMALL), F32), vmem((6, 2, n), F32),
            vmem((8, n, D), BF16), vmem((4, 2, 4, 96, n), BF16), vmem((5, D, D), BF16), vmem((n, D), F32), vmem((n, D), F32),
            vmem((L1, 4, 2, 48, D), BF16), vmem((2, 4, 2, 48, D), BF16), vmem((R1, 4, 2, 48, D), BF16),
            vmem((6, 4, 2, 48, 384), BF16), vmem((5, 4, 48, D), BF16), vmem((NCH, 4, 48, 384), BF16),
            vmem((NCH, 3, 48, 384), BF16), vmem((3, 4, 48, 384), BF16), vmem((n, 128), F32), vmem((n, 128), F32), vmem((1, NSMALL), F32),
            vmem((3, 1, NSMALL), F32), vmem((9, 1, NSMALL), F32),
        ] + [dma((NCH,))] * 14 + [dma((7,))] * 2 + [dma((NCH,))]
        + [dma((8,)), dma((5,)), dma((4,))] + [dma((NCH,))] * 6 + [dma((NCH, 3))] * 4 + [dma((3,))] * 2 + [dma((9,))] * 2,
        compiler_params=pltpu.CompilerParams(collective_id=1, has_side_effects=True, vmem_limit_bytes=61 << 20),
        name="layer",
    )(*ws, *vectors, tok, lat, cot, flags, seg)


def finish_kernel(fin, gsm, out_h, gin_h, gwq_o, gwo_o, gwf_o, gwp_o, v0, v1, v2, v3, v4, v5, v6, v7, out_o, gin_o,
                  ob, gb, gwq, gwo, gwf, gwp, isem, osem, wsem):
    f = lax.axis_index("fsdp")
    n = ob.shape[0]
    parts = []
    for i in range(4):
        rows = slice(i * (n // 4), (i + 1) * (n // 4))
        for src, buf, dst in ((gin_h, gb, gin_o), (out_h, ob, out_o)):
            k = len(parts)
            parts.append((pltpu.make_async_copy(src.at[rows], buf.at[rows], isem.at[k]),
                          pltpu.make_async_copy(buf.at[rows], dst.at[rows], osem.at[k])))
    for a, _ in parts:
        a.start()
    for v, at in zip((v0, v1, v2, v3, v4, v5, v6, v7), (G1, S1, BQ, BO, G2, S2, BF, BP)):
        m = v.shape[-1]
        turned = pltpu.roll(jnp.broadcast_to(gsm[:, at:at + 8 * m], (8, 8 * m)), (8 - f) * m, 1)
        v[...] = turned[0, 0:m]
    sends = []

    def send(buf, dst):
        cp = pltpu.make_async_copy(buf, dst, wsem.at[len(sends)])
        cp.start()
        sends.append(cp)

    for first_of, buf, dst in ((0, gwp, gwp_o), (1, gwf, gwf_o)):
        for yy in range(2):
            rows = slice(yy * 48, (yy + 1) * 48)
            for xx in range(2):
                for j in range(4):
                    buf[rows, j * D + xx * 384:j * D + (xx + 1) * 384] = fin[2 * j + first_of, yy, xx].astype(F32)
        send(buf, dst)
    for a, b in parts[:4]:
        a.wait()
        b.start()
    for yy in range(2):
        rows = slice(yy * 48, (yy + 1) * 48)
        for m in range(3):
            v = jnp.concatenate([fin[9 + m, yy, 0], fin[9 + m, yy, 1]], axis=1).astype(F32)
            for b in range(3):
                gwq[rows, b * D + m * 256:b * D + (m + 1) * 256] = v[:, b * 256:(b + 1) * 256]
        for xx in range(2):
            gwo[rows, xx * 384:(xx + 1) * 384] = fin[8, yy, xx].astype(F32)
    send(gwq, gwq_o)
    send(gwo, gwo_o)
    for a, b in parts[4:]:
        a.wait()
        b.start()
    for _, b in parts:
        b.wait()
    for cp in sends:
        cp.wait()


def finish(fin, gsm, out, gin, sizes):
    anyspec = pl.BlockSpec(memory_space=pl.ANY)
    vspec = pl.BlockSpec(memory_space=pltpu.VMEM)
    dma = pltpu.SemaphoreType.DMA
    shape = jax.ShapeDtypeStruct
    grads = [(96, 3 * D), (96, D), (96, FF), (96, FF)]
    return pl.pallas_call(
        finish_kernel,
        in_specs=[vspec, vspec, anyspec, anyspec],
        out_specs=[anyspec] * 4 + [vspec] * 8 + [anyspec] * 2,
        out_shape=[shape(u, F32) for u in grads] + [shape((m,), F32) for m in sizes]
        + [shape(out.shape, BF16), shape(gin.shape, F32)],
        scratch_shapes=[pltpu.VMEM(out.shape, BF16), pltpu.VMEM(gin.shape, F32)] + [pltpu.VMEM(u, F32) for u in grads]
        + [dma((8,)), dma((8,)), dma((4,))],
        compiler_params=pltpu.CompilerParams(vmem_limit_bytes=VLIM),
        name="finish",
    )(fin, gsm, out, gin)


def own_slots(v, nf, f):
    m = v.shape[0]
    wide = jnp.broadcast_to(v[None, :], (nf, m))
    mine = lax.broadcasted_iota(jnp.int32, (nf, m), 0) == f
    return jnp.where(mine, wide, jnp.zeros_like(wide)).reshape(-1)


def shards(fast, tokens, latent, segment_ids, latent_flags, norm1_gain, norm1_shift, w_qkv, b_qv, w_out, b_out,
           norm2_gain, norm2_shift, w_fc, b_fc, w_proj, b_proj, cotangent):
    nf = lax.axis_size("fsdp")
    f = lax.axis_index("fsdp")
    vectors = (norm1_gain, norm1_shift, b_qv, b_out, norm2_gain, norm2_shift, b_fc, b_proj)
    ws = (w_qkv, w_out.T, w_fc, w_proj.T)

    def mine(total, at, v):
        m = v.shape[0]
        return lax.dynamic_slice(total[0], (at + f * m,), (m,))

    if fast:
        _, _, out, gin, fin, gsm = layer(ws, vectors, tokens, latent, cotangent, latent_flags, segment_ids)
        tq, to, tf, tp, *v, out, gin = finish(fin, gsm, out, gin, [v.shape[0] for v in vectors])
        to, tp, v = to.T, tp.T, [u.reshape(-1) for u in v]
    else:
        row = jnp.concatenate([own_slots(v, nf, f) for v in vectors]).reshape(1, NSMALL)
        wq, wo, wf, wp = [lax.all_gather(w, "fsdp", axis=0, tiled=True) for w in ws]
        small8 = lax.all_gather(row, "fsdp", axis=0, tiled=True)
        qkv, a_t, small = ln_qkv(tokens, latent, latent_flags, small8, wq)
        o, lse = attn_fwd(segment_ids, qkv)
        out, dr, do, gffn, gsm = ffn(tokens, latent, latent_flags, small, o, cotangent, wo, wf, wp)
        dqkv = attn_bwd(segment_ids, qkv, do, lse)
        gin, gq, gsm = last(tokens, latent, latent_flags, small, gsm, dr, dqkv, a_t, wq)

        def scatter(v):
            part = lax.psum_scatter(v, "fsdp", scatter_dimension=0, tiled=True)
            return lax.psum(part, "rep")

        tq, tp, tf, to = [scatter(v) for v in (gq, gffn[:, :FF], gffn[:, FF:2 * FF], gffn[:, 2 * FF:])]
        tq, to, tf, tp = tq.astype(F32), to.astype(F32).T, tf.astype(F32), tp.astype(F32).T
        gsm = lax.psum(gsm, ("rep", "fsdp"))
        v = [mine(gsm, at, v) for at, v in zip((G1, S1, BQ, BO, G2, S2, BF, BP), vectors)]
    return (out, gin, v[0], v[1], tq, v[2], to, v[3], v[4], v[5], tf, v[6], tp, v[7])


def solution(mesh):
    fast = mesh.shape["rep"] == 4 and mesh.shape["fsdp"] == 8
    both = P(("rep", "fsdp"), None)
    one, row, col = P("fsdp"), P("fsdp", None), P(None, "fsdp")
    return jax.shard_map(
        partial(shards, fast),
        mesh=mesh,
        in_specs=(both, both, both, both, one, one, row, one, col, one, one, one, row, one, col, one, both),
        out_specs=(both, both, one, one, row, one, col, one, one, one, row, one, col, one),
        check_vma=False,
    )
```
